32 devices in a mesh: dp: 16 (over z, y, core), narrow: 2 (over x).
Axes of the slice: x: 2, y: 2, z: 4, core: 2. Of those that a mesh axis runs over, the one named last changes fastest.
Arguments:
- tokens: bfloat16 [6144, 6144], P('dp'), may hold values from -12 to 12
- group_slot: int32 [16, 384], P('dp'), may hold values from 0 to 383, each once within a row
- controller: bfloat16 [6144, 16], replicated, may hold values from -40 to 40
- expert_in: bfloat16 [16, 6144, 1024], P('dp', None, 'narrow'), may hold values from -0.078125 to 0.078125
- expert_out: bfloat16 [16, 6144, 1024], P('dp', None, 'narrow'), may hold values from -0.1875 to 0.1875
- cotangent: bfloat16 [6144, 6144], P('dp', 'narrow'), may hold values from -6 to 6
Outputs:
- token_grad: bfloat16 [6144, 6144], P('dp', 'narrow')
- ctrl_grad: float32 [6144, 16], P('narrow')
- in_grad: bfloat16 [16, 6144, 1024], P('dp', None, 'narrow')
- out_grad: bfloat16 [16, 6144, 1024], P('dp', None, 'narrow')
The draws below stay inside these ranges and needn't reach their ends.
Inputs may be any that keep to these rules, and one draw needn't show every extreme that they name: Each row is a permutation; a token belongs to group group_slot // 32 of its row.
All inputs are finite; a program needn't handle non-finite values.
Results may differ from the reference program's by a relative error of at most 0.029.
Values may be sent and summed in bfloat16 or wider, within the bound.
No kernel may reach another device: no remote copies, remote signals or barrier semaphores. Data moves between devices by JAX's collectives and lax.ppermute only.
A program may use at most 128 MiB of HBM per device.

```python
import math
import jax
import jax.numpy as jnp
from jax import lax

D = 6144
FFH = 1024
GSIZE = 32
TOK_DP = 384
EXPERTS = 16
TOKENS = 6144
N_DP = 16
N_NARROW = 2


def draw_tokens(key, part):
    values = jax.random.normal(jax.random.fold_in(key, 11), (TOKENS, D), jnp.float32)
    return jnp.clip(values, -12.0, 12.0).astype(jnp.bfloat16)


def draw_controller(key, part):
    values = 1.5 * jax.random.normal(jax.random.fold_in(key, 19), (D, EXPERTS), jnp.float32)
    return jnp.clip(values, -40.0, 40.0).astype(jnp.bfloat16)


def steps_of(rng, extent, pieces, smallest, top_value):
    loudness = 1.0
    for axis_at, shards_of in pieces:
        draws = jax.random.uniform(jax.random.fold_in(jax.random.fold_in(rng, 6), axis_at), (shards_of,), jnp.float32, smallest / len(pieces), top_value / len(pieces))
        loudness = loudness * jnp.repeat(jnp.exp(draws), extent[axis_at] // shards_of).reshape((-1,) + (1,) * (len(extent) - 1 - axis_at))
    return loudness


def noise(rng, dims, spread, bound, pieces=(), kind=jnp.bfloat16):
    array = spread * jax.random.normal(rng, dims, jnp.float32)
    if pieces:
        array = array * steps_of(rng, dims, pieces, -0.22, 0.18)
    return jnp.clip(array, -bound, bound).astype(kind)


def setup_inputs(seed: int = 0) -> dict:
    seeds = jax.random.split(jax.random.key(seed), 7)
    return {
        "tokens": draw_tokens(jax.random.fold_in(seeds[6], 71), 0),
        "group_slot": jax.vmap(lambda own: jax.random.permutation(own, TOK_DP))(jax.random.split(seeds[1], N_DP)).reshape((N_DP, TOK_DP)).astype(jnp.int32),
        "controller": draw_controller(jax.random.fold_in(seeds[6], 71), 0),
        "expert_in": noise(seeds[3], (EXPERTS, D, FFH), D ** -0.5, 0.078125, ((0, 16), (2, 2))),
        "expert_out": noise(seeds[4], (EXPERTS, D, FFH), FFH ** -0.5, 0.1875, ((0, 16), (2, 2))),
        "cotangent": noise(seeds[5], (TOKENS, D), 1.0, 6.0, ((0, 16), (1, 2))),
    }


def silu_slope(values):
    gate_sig = jax.nn.sigmoid(values)
    return gate_sig * (1.0 + values * (1.0 - gate_sig))

def to_low(values):
    return lax.optimization_barrier(values.astype(jnp.bfloat16)).astype(jnp.float32)

def group_blocks(matrix, group_slot):
    per_block = matrix.reshape(group_slot.shape[0], group_slot.shape[1], matrix.shape[1])
    positions = jnp.broadcast_to(jnp.arange(group_slot.shape[1], dtype=jnp.int32), group_slot.shape)
    inverse = jax.vmap(lambda slot_row, place_row: jnp.zeros_like(slot_row).at[slot_row].set(place_row))(group_slot, positions)
    taken_rows = jnp.take_along_axis(per_block, inverse[:, :, None].astype(jnp.int32), axis=1)
    return taken_rows.reshape(group_slot.shape[0], -1, GSIZE, matrix.shape[1])

def split_sum(partials):
    rounded = lax.optimization_barrier(partials.astype(jnp.bfloat16))
    return lax.optimization_barrier(jnp.sum(rounded.astype(jnp.float32), axis=0)).astype(jnp.bfloat16)

def reference(tokens, group_slot, controller, expert_in, expert_out, cotangent):
    scale_logit = 1.0 / math.sqrt(D)
    grouped = group_blocks(tokens, group_slot).astype(jnp.float32)
    grouped_cot = group_blocks(cotangent, group_slot).astype(jnp.float32)
    ctrl_wide = controller.astype(jnp.float32)
    logits = jnp.einsum('pgsd,de->pgse', grouped, ctrl_wide) * scale_logit
    weights = jax.nn.softmax(logits, axis=2)
    weights_low = to_low(weights)
    mixed_rows = to_low(jnp.einsum('pgse,pgsd->pged', weights_low, grouped))
    mixed_cot = to_low(jnp.einsum('pgse,pgsd->pged', weights_low, grouped_cot))
    expert_rows = mixed_rows.transpose(2, 0, 1, 3).reshape(EXPERTS, -1, D)
    expert_cot = mixed_cot.transpose(2, 0, 1, 3).reshape(EXPERTS, -1, D)

    def per_expert(packed):
        rows_in, cot_in, first_weight, second_weight = packed
        first_wide = first_weight.astype(jnp.float32)
        second_wide = second_weight.astype(jnp.float32)
        pre_act = jnp.dot(rows_in, first_wide, preferred_element_type=jnp.float32)
        hidden_act = to_low(jax.nn.silu(pre_act))
        hid_grad = jnp.dot(cot_in, second_wide, preferred_element_type=jnp.float32)
        act_grad = to_low(hid_grad * silu_slope(pre_act))
        in_part = jnp.dot(rows_in.T, act_grad, preferred_element_type=jnp.float32).astype(jnp.bfloat16)
        out_part = jnp.dot(cot_in.T, hidden_act, preferred_element_type=jnp.float32).astype(jnp.bfloat16)
        row_count = hidden_act.shape[0]
        hidden_blocks = hidden_act.reshape(row_count, N_NARROW, -1)
        act_blocks = act_grad.reshape(row_count, N_NARROW, -1)
        result = split_sum(jnp.einsum('rqh,dqh->qrd', hidden_blocks, second_wide.reshape(D, N_NARROW, -1)))
        back_rows = split_sum(jnp.einsum('rqh,dqh->qrd', act_blocks, first_wide.reshape(D, N_NARROW, -1)))
        return (result, back_rows, in_part, out_part)
    results, backs, in_grad, out_grad = lax.map(per_expert, (expert_rows, expert_cot, expert_in, expert_out))
    result_wide = results.astype(jnp.float32).reshape(EXPERTS, N_DP, -1, D).transpose(1, 2, 0, 3)
    back_wide = backs.astype(jnp.float32).reshape(EXPERTS, N_DP, -1, D).transpose(1, 2, 0, 3)
    mix_grad = jnp.einsum('pgsd,pged->pgse', grouped_cot, result_wide) + jnp.einsum('pgsd,pged->pgse', grouped, back_wide)
    logit_grad = weights * (mix_grad - lax.optimization_barrier(jnp.sum(weights * mix_grad, axis=2, keepdims=True)))
    logit_low = to_low(logit_grad)
    token_part = jnp.einsum('pgse,pged->pgsd', weights_low, back_wide) + scale_logit * jnp.einsum('pgse,de->pgsd', logit_low, ctrl_wide)
    token_low = token_part.astype(jnp.bfloat16).reshape(N_DP, TOK_DP, D)
    token_grad = jnp.take_along_axis(token_low, group_slot[:, :, None].astype(jnp.int32), axis=1).reshape(TOKENS, D)
    ctrl_grad = scale_logit * jnp.einsum('pgsd,pgse->de', grouped, logit_low)
    return (token_grad, ctrl_grad, in_grad, out_grad)
```

```python
import functools
import math

import jax
import jax.numpy as jnp
from jax import lax
from jax.experimental import pallas as pl
from jax.experimental.pallas import tpu as pltpu
from jax.sharding import PartitionSpec as P

GSIZE = 32
SUB = 8
HALF = 4
NEAR = 4
F32 = jnp.float32
BF16 = jnp.bfloat16
VMEM_LIMIT = 60 * 1024 * 1024


def dot_nn(a, b):
    return lax.dot_general(a, b, (((1,), (0,)), ((), ())), preferred_element_type=F32)


def dot_nt(a, b):
    return lax.dot_general(a, b, (((1,), (1,)), ((), ())), preferred_element_type=F32)


def dot_tn(a, b):
    return lax.dot_general(a, b, (((0,), (0,)), ((), ())), preferred_element_type=F32)


def iota(shape, dim):
    return lax.broadcasted_iota(jnp.int32, shape, dim)


def first_half(shape):
    return (iota(shape, 0) & HALF) == 0


def pick(width, most):
    size = most
    while width % size:
        size //= 2
    return size


def call(kernel, name, grid, in_specs, out_specs, out_shape, scratch=(), scalars=1, flops=0, nbytes=0):
    return pl.pallas_call(
        kernel,
        name=name,
        grid_spec=pltpu.PrefetchScalarGridSpec(
            num_scalar_prefetch=scalars,
            grid=grid,
            in_specs=in_specs,
            out_specs=out_specs,
            scratch_shapes=list(scratch),
        ),
        out_shape=out_shape,
        compiler_params=pltpu.CompilerParams(
            dimension_semantics=("arbitrary",) * len(grid),
        ),
        cost_estimate=pl.CostEstimate(flops=int(flops), bytes_accessed=int(nbytes), transcendentals=0),
    )


def whole(array):
    rank = len(array.shape)
    return pl.BlockSpec(array.shape, lambda *_: (0,) * rank)


def shape_of(dims, dtype):
    return jax.ShapeDtypeStruct(dims, dtype)


def rel_of(c8, far):
    return (c8 % far) * NEAR + c8 // far if isinstance(c8, int) else (
        (c8 & (far - 1)) * NEAR + lax.shift_right_logical(c8, far.bit_length() - 1)
    )


def group_masks(gid, cols):
    row = iota((cols, gid.shape[1]), 0)
    in_a = gid == (row & (SUB - 1))
    in_b = gid == (SUB + (row & (HALF - 1)))
    return in_a, in_b


def logits_kernel(far, scale, idx_ref, tok_ref, ctrl_ref, gid_ref, low_ref, w_ref, acc_ref):
    step = pl.program_id(0)
    experts = ctrl_ref.shape[0]
    cols = SUB * experts
    me = idx_ref[0]

    @pl.when(step == 0)
    def _():
        acc_ref[...] = jnp.zeros_like(acc_ref)

    c8 = lax.shift_right_logical(iota((cols, experts), 0), 3)
    owner = rel_of(c8, far) ^ me
    onehot = jnp.where(iota((cols, experts), 1) == owner, 1.0, 0.0).astype(BF16)
    ctrl = dot_nn(onehot, ctrl_ref[...]).astype(BF16)
    acc_ref[...] += dot_nt(ctrl, tok_ref[...])

    @pl.when(step == pl.num_programs(0) - 1)
    def _():
        logits = acc_ref[...] * scale
        masks = group_masks(gid_ref[...], cols)
        shared = jnp.zeros_like(logits)
        for part, mask in enumerate(masks):
            top = jnp.max(jnp.where(mask, logits, -jnp.inf), axis=1, keepdims=True)
            raised = jnp.where(mask, jnp.exp(jnp.where(mask, logits - top, 0.0)), 0.0)
            weights = raised / jnp.sum(raised, axis=1, keepdims=True)
            low_ref[part] = weights.astype(BF16)
            if part:
                weights = jnp.where(first_half(weights.shape), weights, 0.0)
            shared += weights
        w_ref[...] = jnp.sum(shared.reshape(experts, SUB, -1), axis=1)


def expand_kernel(rhs_t, idx_ref, left_ref, one_ref, two_ref, *out_refs):
    step = pl.program_id(0)
    left = left_ref[...]
    rows = left.shape[0] // 2
    one, two = one_ref[...], two_ref[...]
    one, two = one.reshape(one.shape[-2:]), two.reshape(two.shape[-2:])
    dot = dot_nt if rhs_t else dot_nn
    size = one.shape[0] if rhs_t else one.shape[1]
    top, low = dot(left, one), dot(left, two)
    mixed = jnp.where(first_half((rows, size)), top[rows:], low[rows:])
    width = out_refs[0].shape[1]
    full = width // 3 * 2
    each = rows // len(out_refs)
    for at, out_ref in enumerate(out_refs):
        span = slice(at * each, (at + 1) * each)
        base = pl.multiple_of(step * size, size)
        out_ref[:, pl.ds(base, size)] = top[:rows][span].astype(BF16)
        out_ref[:, pl.ds(full // 2 + base, size)] = low[:rows][span].astype(BF16)
        out_ref[:, pl.ds(full + base, size)] = mixed[span].astype(BF16)


def expand_tokens(name, left, source, at, slice_width, pieces):
    size = pick(slice_width // 2, 512)
    steps = slice_width // 2 // size
    count, rows = source.shape[0], left.shape[0] // 2
    outs = [shape_of((rows // pieces, slice_width // 2 * 3), BF16)] * pieces
    return call(
        functools.partial(expand_kernel, False),
        name,
        (steps,),
        [
            whole(left),
            pl.BlockSpec((count, size), lambda i, idx: (0, idx[0] * 2 * steps + i)),
            pl.BlockSpec((count, size), lambda i, idx: (0, idx[0] * 2 * steps + steps + i)),
        ],
        [whole(out) for out in outs],
        outs,
        flops=4 * rows * count * slice_width,
        nbytes=2 * count * slice_width + 3 * rows * slice_width,
    )(at, left, source, source)


def expand_weights(name, left, weights, at, pieces):
    _, _, half, hidden = weights.shape
    size = pick(half, 512)
    rows = left.shape[0] // 2
    outs = [shape_of((rows // pieces, half * 3), BF16)] * pieces
    return call(
        functools.partial(expand_kernel, True),
        name,
        (half // size,),
        [
            whole(left),
            pl.BlockSpec((1, 1, size, hidden), lambda i, idx: (idx[0], 0, i, 0)),
            pl.BlockSpec((1, 1, size, hidden), lambda i, idx: (idx[0], 1, i, 0)),
        ],
        [whole(out) for out in outs],
        outs,
        flops=8 * rows * half * hidden,
        nbytes=4 * half * hidden + 6 * rows * half,
    )(at, left, weights, weights)


def contract_kernel(rhs_t, pieces, idx_ref, one_ref, two_ref, *refs):
    step = pl.program_id(0)
    in_refs, out_ref = refs[:pieces], refs[pieces]
    rows = out_ref.shape[1]
    one, two = one_ref[...], two_ref[...]
    one, two = one.reshape(one.shape[-2:]), two.reshape(two.shape[-2:])
    dot = dot_nt if rhs_t else dot_nn
    size = one.shape[1] if rhs_t else one.shape[0]
    width = in_refs[0].shape[1]
    full = width // 3 * 2
    base = pl.multiple_of(step * size, size)

    def part(start):
        return [ref[:, pl.ds(start + base, size)] for ref in in_refs]

    packed = part(full)
    top = dot(jnp.concatenate(part(0) + packed, axis=0), one)
    low = dot(jnp.concatenate(part(full // 2) + packed, axis=0), two)
    straight = top[:rows] + low[:rows]
    halves = jnp.where(first_half(straight.shape), top[rows:], low[rows:])

    @pl.when(step == 0)
    def _():
        out_ref[0] = straight
        out_ref[1] = halves

    @pl.when(step > 0)
    def _():
        out_ref[0] += straight
        out_ref[1] += halves


def contract_weights(name, parts, weights, at):
    _, _, half, hidden = weights.shape
    size = pick(half, 512)
    rows = sum(part.shape[0] for part in parts)
    out = shape_of((2, rows, hidden), F32)
    return call(
        functools.partial(contract_kernel, False, len(parts)),
        name,
        (half // size,),
        [
            pl.BlockSpec((1, 1, size, hidden), lambda i, idx: (idx[0], 0, i, 0)),
            pl.BlockSpec((1, 1, size, hidden), lambda i, idx: (idx[0], 1, i, 0)),
        ]
        + [whole(part) for part in parts],
        whole(out),
        out,
        flops=8 * rows * half * hidden,
        nbytes=4 * half * hidden + 6 * rows * half,
    )(at, weights, weights, *parts)


def contract_tokens(name, parts, source, at):
    half = parts[0].shape[1] // 3
    size = pick(half, 512)
    steps = half // size
    rows = sum(part.shape[0] for part in parts)
    count = source.shape[0]
    out = shape_of((2, rows, count), F32)
    return call(
        functools.partial(contract_kernel, True, len(parts)),
        name,
        (steps,),
        [
            pl.BlockSpec((count, size), lambda i, idx: (0, idx[0] * 2 * steps + i)),
            pl.BlockSpec((count, size), lambda i, idx: (0, idx[0] * 2 * steps + steps + i)),
        ]
        + [whole(part) for part in parts],
        whole(out),
        out,
        flops=8 * rows * half * count,
        nbytes=4 * half * count + 6 * rows * half,
    )(at, source, source, *parts)


def joined(refs):
    total = refs[0][...]
    for ref in refs[1:]:
        total = total + ref[...]
    rows = total.shape[1]
    halves = total[1]
    other = jnp.where(
        first_half(halves.shape), pltpu.roll(halves, rows - HALF, 0), pltpu.roll(halves, HALF, 0)
    )
    return jnp.concatenate([total[0], halves + other], axis=0)


def hidden_kernel(idx_ref, *refs):
    pre_ref, hidden_ref = refs[-2:]
    pre = joined(refs[:-2])
    pre_ref[...] = pre
    hidden_ref[...] = (pre * jax.nn.sigmoid(pre)).astype(BF16)


def slope_kernel(idx_ref, pre_ref, *refs):
    act_ref = refs[-1]
    pre = pre_ref[...]
    sig = jax.nn.sigmoid(pre)
    act_ref[...] = (joined(refs[:-1]) * (sig * (1.0 + pre * (1.0 - sig)))).astype(BF16)


def grad_kernel(pieces, steps, idx_ref, act_ref, *refs):
    in_refs, out_ref, held = refs[:-2], refs[-2], refs[-1]
    step = pl.program_id(0)
    size = out_ref.shape[2]
    rows = act_ref.shape[0] // 2

    @pl.when(step == 0)
    def _():
        act = act_ref[...]
        mask = first_half((rows, act.shape[1]))
        zero = jnp.zeros((rows, act.shape[1]), F32)
        low = act[rows:].astype(F32)
        for side in range(2):
            held[side, :rows] = act[:rows]
            held[side, rows:] = (jnp.where(mask, low, zero) if side == 0 else jnp.where(mask, zero, low)).astype(BF16)

    for turn in range(len(in_refs) // pieces):

        @pl.when(step // steps == turn)
        def _():
            own = in_refs[turn * pieces : (turn + 1) * pieces]
            full = own[0].shape[1] // 3 * 2
            base = pl.multiple_of(lax.rem(step, steps) * size, size)
            packed = [ref[:, pl.ds(full + base, size)] for ref in own]
            for side in range(2):
                straight = [ref[:, pl.ds(side * (full // 2) + base, size)] for ref in own]
                out_ref[0, side] = dot_tn(jnp.concatenate(straight + packed, axis=0), held[side]).astype(BF16)


def weight_grad(name, act, slices, like, at):
    parts_n, _, half, hidden = like
    size = pick(half, 512)
    steps = half // size
    pieces = len(slices[0])
    flat = [part for one in slices for part in one]
    rows = act.shape[0] // 2
    out = shape_of(like, BF16)
    return call(
        functools.partial(grad_kernel, pieces, steps),
        name,
        (parts_n * steps,),
        [whole(act)] + [whole(part) for part in flat],
        pl.BlockSpec((1, 2, size, hidden), lambda i, idx: (idx[i // steps], 0, lax.rem(i, steps), 0)),
        out,
        scratch=[pltpu.VMEM((2, 2 * rows, hidden), BF16)],
        flops=8 * rows * half * parts_n * hidden,
        nbytes=parts_n * (4 * half * hidden + 6 * rows * half),
    )(at, act, *flat)


def mix_kernel(idx_ref, gid_ref, one_ref, two_ref, out_ref):
    cols, count = one_ref.shape[1:]
    in_a, in_b = group_masks(gid_ref[...], cols)
    picked = jnp.where(in_a, one_ref[0] + two_ref[0], 0.0) + jnp.where(in_b, one_ref[1] + two_ref[1], 0.0)
    out_ref[...] = jnp.sum(picked.reshape(cols // SUB, SUB, count), axis=1)


def ctrl_kernel(far, scale, turns, idx_ref, gid_ref, w_ref, *refs):
    mix_refs, tok_ref, low_ref, out_ref = refs[:turns], refs[turns], refs[turns + 1], refs[turns + 2]
    experts, count = w_ref.shape
    cols = SUB * experts

    @pl.when(pl.program_id(0) == 0)
    def _():
        mix = mix_refs[0][...]
        for ref in mix_refs[1:]:
            mix = mix + ref[...]
        weights = w_ref[...]
        in_a, in_b = group_masks(gid_ref[...], cols)
        spread = jnp.broadcast_to((weights * mix)[:, None, :], (experts, SUB, count)).reshape(cols, count)
        sum_a = jnp.sum(jnp.where(in_a, spread, 0.0), axis=1, keepdims=True)
        sum_b = jnp.sum(jnp.where(in_b, spread, 0.0), axis=1, keepdims=True)
        in_b = jnp.logical_and(in_b, first_half((cols, count)))
        back = jnp.where(in_a, sum_a, 0.0) + jnp.where(in_b, sum_b, 0.0)
        total = jnp.sum(back.reshape(experts, SUB, count), axis=1)
        low = (weights * (mix - total)).astype(BF16)
        place = rel_of(iota((experts, experts), 1), far) ^ idx_ref[1]
        onehot = jnp.where(iota((experts, experts), 0) == place, 1.0, 0.0).astype(BF16)
        low_ref[...] = dot_nn(onehot, low).astype(BF16)

    out_ref[...] = (scale * dot_nn(low_ref[...], tok_ref[...])).astype(BF16)


def token_kernel(scale, steps, pieces, idx_ref, left_ref, low_ref, ctrl_ref, *refs):
    in_refs, out_ref = refs[:pieces], refs[pieces]
    step = pl.program_id(0)
    size = out_ref.shape[1]
    full = in_refs[0].shape[1] // 3 * 2
    base = pl.multiple_of(step * size, size)
    lower = pl.multiple_of(lax.rem(step, steps) * size, size)
    straight = [ref[:, pl.ds(base, size)] for ref in in_refs]
    packed = [ref[:, pl.ds(full + lower, size)] for ref in in_refs]
    back = dot_tn(left_ref[0], jnp.concatenate(straight + packed, axis=0))
    out_ref[...] = (back + scale * dot_tn(low_ref[...], ctrl_ref[...])).astype(BF16)


def on_device(sizes, tokens, group_slot, controller, expert_in, expert_out, cotangent):
    n_dp, n_narrow = sizes
    count, model_width = tokens.shape
    slice_width = cotangent.shape[1]
    half = slice_width // 2
    experts = controller.shape[1]
    hidden = expert_in.shape[2]
    far = n_dp // NEAR
    cols = SUB * experts
    assert experts == n_dp and count // GSIZE == SUB + HALF and far & (far - 1) == 0
    scale = 1.0 / math.sqrt(model_width)
    me = lax.axis_index("dp").astype(jnp.int32)
    member = lax.axis_index("narrow").astype(jnp.int32)
    turns = [lax.rem(member - shift + n_narrow, n_narrow) for shift in range(n_narrow)]
    at = [jnp.stack([turn, me]) for turn in turns]
    zero = jnp.stack([jnp.zeros_like(me), me])
    order = jnp.stack(turns)
    gid = lax.shift_right_logical(group_slot, int(math.log2(GSIZE)))
    ctrl_t = controller.T
    first = expert_in.reshape(n_narrow, 2, half, hidden)
    second = expert_out.reshape(n_narrow, 2, half, hidden)

    def swap(array, bits):
        return lax.ppermute(array, "dp", [(i, i ^ bits) for i in range(n_dp)]) if bits else array

    def shifted(array, shift):
        return lax.ppermute(array, "narrow", [(i, (i + shift) % n_narrow) for i in range(n_narrow)])

    def regroup(parts):
        return [
            jnp.concatenate([part[SUB * at_row : SUB * (at_row + 1)] for part in parts], axis=0)
            for at_row in range(parts[0].shape[0] // SUB)
        ]

    def outward(parts):
        parts = [swap(part, bits) for bits, part in enumerate(parts)]
        parts = [swap(part, NEAR * bits) for bits, part in enumerate(regroup(parts))]
        return [parts] + [[shifted(part, shift) for part in parts] for shift in range(1, n_narrow)]

    def homeward(own, others):
        parts = []
        for bits in range(far):
            total = own[bits].astype(F32)
            for shift, other in enumerate(others, 1):
                total = total + shifted(other[bits], shift).astype(F32)
            parts.append(total.astype(BF16))
        parts = [swap(part, NEAR * bits) for bits, part in enumerate(parts)]
        return [swap(part, bits) for bits, part in enumerate(regroup(parts))]

    size = pick(model_width, 1024)
    low, weights = call(
        functools.partial(logits_kernel, far, scale),
        "logits",
        (model_width // size,),
        [
            pl.BlockSpec((count, size), lambda i, idx: (0, i)),
            pl.BlockSpec((experts, size), lambda i, idx: (0, i)),
            whole(gid),
        ],
        [whole(shape_of((2, cols, count), BF16)), whole(shape_of((experts, count), F32))],
        [shape_of((2, cols, count), BF16), shape_of((experts, count), F32)],
        scratch=[pltpu.VMEM((cols, count), F32)],
        flops=2 * cols * count * model_width,
        nbytes=2 * count * model_width,
    )(jnp.stack([me, me]), tokens, ctrl_t, gid)
    left = low.reshape(2 * cols, count)
    mixed = outward(expand_tokens("mix_rows", left, tokens, at[0], slice_width, NEAR))
    mixed_cot = outward(expand_tokens("mix_cot", left, cotangent, zero, slice_width, NEAR))

    pre_parts = [contract_weights("pre_%d" % s, mixed[s], first, at[s]) for s in range(n_narrow)]
    rows = 2 * cols
    pre, hidden_act = call(
        hidden_kernel,
        "hidden",
        (1,),
        [whole(part) for part in pre_parts],
        [whole(shape_of((rows, hidden), F32)), whole(shape_of((rows, hidden), BF16))],
        [shape_of((rows, hidden), F32), shape_of((rows, hidden), BF16)],
    )(zero, *pre_parts)
    ahead = [jnp.stack([lax.rem(member + shift, n_narrow), me]) for shift in range(n_narrow)]
    result_parts = [expand_weights("result_%d" % s, hidden_act, second, ahead[s], far) for s in reversed(range(n_narrow))][::-1]
    result = homeward(result_parts[0], result_parts[1:])

    grad_parts = [contract_weights("slope_%d" % s, mixed_cot[s], second, at[s]) for s in range(n_narrow)]
    act_grad = call(
        slope_kernel,
        "slope",
        (1,),
        [whole(pre)] + [whole(part) for part in grad_parts],
        whole(shape_of((rows, hidden), BF16)),
        shape_of((rows, hidden), BF16),
    )(zero, pre, *grad_parts)
    back_parts = [expand_weights("back_%d" % s, act_grad, first, ahead[s], far) for s in reversed(range(n_narrow))][::-1]
    back = homeward(back_parts[0], back_parts[1:])
    in_grad = weight_grad("in_grad", act_grad, mixed, first.shape, order).reshape(expert_in.shape)
    out_grad = weight_grad("out_grad", hidden_act, mixed_cot, second.shape, order).reshape(expert_out.shape)

    mix_one = contract_tokens("mix_result", result, cotangent, zero)
    mix_two = contract_tokens("mix_back", back, tokens, at[0])
    mix = call(
        mix_kernel,
        "mix",
        (1,),
        [whole(gid), whole(mix_one), whole(mix_two)],
        whole(shape_of((experts, count), F32)),
        shape_of((experts, count), F32),
    )(zero, gid, mix_one, mix_two)
    mixes = [mix] + [shifted(mix, shift) for shift in range(1, n_narrow)]
    size = pick(slice_width, 1024)
    per = slice_width // size
    low_grad, ctrl_part = call(
        functools.partial(ctrl_kernel, far, scale, n_narrow),
        "ctrl",
        (per,),
        [whole(gid), whole(weights)]
        + [whole(mix)] * n_narrow
        + [pl.BlockSpec((count, size), lambda i, idx: (0, idx[0] * per + i))],
        [whole(shape_of((experts, count), BF16)), pl.BlockSpec((experts, size), lambda i, idx: (0, i))],
        [shape_of((experts, count), BF16), shape_of((experts, slice_width), BF16)],
        flops=2 * experts * count * slice_width,
        nbytes=2 * count * slice_width,
    )(at[0], gid, weights, *mixes, tokens)
    bits = 1
    total = ctrl_part.astype(F32)
    while bits < n_dp:
        total = total.astype(BF16)
        total = total.astype(F32) + swap(total, bits).astype(F32)
        bits *= 2
    ctrl_grad = total.T

    size = pick(half, 512)
    steps = half // size
    side = jnp.where((jnp.arange(cols) & HALF)[:, None] == 0, low[1], jnp.zeros_like(low[1]))
    sides = jnp.stack([jnp.concatenate([low[0], side]), jnp.concatenate([low[0], low[1] - side])])
    token_grad = call(
        functools.partial(token_kernel, scale, steps, len(back)),
        "token_grad",
        (2 * steps,),
        [
            pl.BlockSpec((1, 2 * cols, count), lambda i, idx: (i // steps, 0, 0)),
            whole(low_grad),
            pl.BlockSpec((experts, size), lambda i, idx: (0, idx[0] * 2 * steps + i)),
        ]
        + [whole(part) for part in back],
        pl.BlockSpec((count, size), lambda i, idx: (0, i)),
        shape_of((count, slice_width), BF16),
        flops=4 * cols * count * slice_width,
        nbytes=2 * count * slice_width,
    )(at[0], sides, low_grad, ctrl_t, *back)
    return (token_grad, ctrl_grad, in_grad, out_grad)


def solution(mesh):
    sizes = (mesh.shape["dp"], mesh.shape["narrow"])
    placed = (
        P("dp", None),
        P("dp", None),
        P(),
        P("dp", None, "narrow"),
        P("dp", None, "narrow"),
        P("dp", "narrow"),
    )
    return jax.shard_map(
        functools.partial(on_device, sizes),
        mesh=mesh,
        in_specs=placed,
        out_specs=(
            P("dp", "narrow"),
            P("narrow", None),
            P("dp", None, "narrow"),
            P("dp", None, "narrow"),
        ),
        check_vma=False,
    )
```

```python
import functools
import math

import jax
import jax.numpy as jnp
from jax import lax
from jax.experimental import pallas as pl
from jax.experimental.pallas import tpu as pltpu
from jax.sharding import PartitionSpec as P

GSIZE = 32
SUB = 8
HALF = 4
NEAR = 4
F32 = jnp.float32
BF16 = jnp.bfloat16
VMEM_LIMIT = 60 * 1024 * 1024


def dot_nn(a, b):
    return lax.dot_general(a, b, (((1,), (0,)), ((), ())), preferred_element_type=F32)


def dot_nt(a, b):
    return lax.dot_general(a, b, (((1,), (1,)), ((), ())), preferred_element_type=F32)


def dot_tn(a, b):
    return lax.dot_general(a, b, (((0,), (0,)), ((), ())), preferred_element_type=F32)


def iota(shape, dim):
    return lax.broadcasted_iota(jnp.int32, shape, dim)


def first_half(shape):
    return (iota(shape, 0) & HALF) == 0


def pick(width, most):
    size = most
    while width % size:
        size //= 2
    return size


ANY = pl.BlockSpec(memory_space=pl.ANY)


def call(kernel, name, grid, in_specs, out_specs, out_shape, scratch=(), scalars=1, flops=0, nbytes=0, after=()):
    skip = len(after)

    def body(*refs):
        kernel(*refs[:scalars], *refs[scalars + skip :])

    run = pl.pallas_call(
        body,
        name=name,
        grid_spec=pltpu.PrefetchScalarGridSpec(
            num_scalar_prefetch=scalars,
            grid=grid,
            in_specs=[ANY] * skip + list(in_specs),
            out_specs=out_specs,
            scratch_shapes=list(scratch),
        ),
        out_shape=out_shape,
        compiler_params=pltpu.CompilerParams(
            dimension_semantics=("arbitrary",) * len(grid),
        ),
        cost_estimate=pl.CostEstimate(flops=int(flops), bytes_accessed=int(nbytes), transcendentals=0),
    )
    return lambda *args: run(*args[:scalars], *after, *args[scalars:])


def placed_here():
    return lax.axis_index("dp").astype(jnp.int32), lax.axis_index("narrow").astype(jnp.int32)


def start_all(copies):
    for copy in copies:
        copy.start()
    return copies


def whole(array):
    rank = len(array.shape)
    return pl.BlockSpec(array.shape, lambda *_: (0,) * rank)


def shape_of(dims, dtype):
    return jax.ShapeDtypeStruct(dims, dtype)


def rel_of(c8, far):
    return (c8 % far) * NEAR + c8 // far if isinstance(c8, int) else (
        (c8 & (far - 1)) * NEAR + lax.shift_right_logical(c8, far.bit_length() - 1)
    )


def group_masks(gid, cols):
    row = iota((cols, gid.shape[1]), 0)
    in_a = gid == (row & (SUB - 1))
    in_b = gid == (SUB + (row & (HALF - 1)))
    return in_a, in_b


def soften(logits, gid, low_ref, w_ref):
    experts = w_ref.shape[0]
    masks = group_masks(gid, logits.shape[0])
    shared = jnp.zeros_like(logits)
    for part, mask in enumerate(masks):
        top = jnp.max(jnp.where(mask, logits, -jnp.inf), axis=1, keepdims=True)
        raised = jnp.where(mask, jnp.exp(jnp.where(mask, logits - top, 0.0)), 0.0)
        weights = raised / jnp.sum(raised, axis=1, keepdims=True)
        low_ref[part] = weights.astype(BF16)
        if part:
            weights = jnp.where(first_half(weights.shape), weights, 0.0)
        shared += weights
    w_ref[...] = jnp.sum(shared.reshape(experts, SUB, -1), axis=1)


def expand_into(out_refs, left, one, two, base, rhs_t):
    rows = left.shape[0] // 2
    dot = dot_nt if rhs_t else dot_nn
    size = one.shape[0] if rhs_t else one.shape[1]
    top, low = dot(left, one), dot(left, two)
    mixed = jnp.where(first_half((rows, size)), top[rows:], low[rows:])
    full = out_refs[0].shape[1] // 3 * 2
    each = rows // len(out_refs)
    for at, out_ref in enumerate(out_refs):
        span = slice(at * each, (at + 1) * each)
        out_ref[:, pl.ds(base, size)] = top[:rows][span].astype(BF16)
        out_ref[:, pl.ds(full // 2 + base, size)] = low[:rows][span].astype(BF16)
        out_ref[:, pl.ds(full + base, size)] = mixed[span].astype(BF16)


def head_kernel(far, scale, slice_width, tok_hbm, ctrl_ref, gid_ref, *refs):
    out_refs, (low_ref, w_ref, tok_ref, acc_ref, sems) = refs[:NEAR], refs[NEAR:]
    count, width = tok_ref.shape
    chunks = sems.shape[0]
    size = width // chunks
    spans = [slice(c * size, (c + 1) * size) for c in range(chunks)]
    copies = start_all(
        [pltpu.make_async_copy(tok_hbm.at[:, span], tok_ref.at[:, span], sems.at[c]) for c, span in enumerate(spans)]
    )
    me, member = placed_here()
    experts = ctrl_ref.shape[0]
    cols = SUB * experts
    c8 = lax.shift_right_logical(iota((cols, experts), 0), 3)
    onehot = jnp.where(iota((cols, experts), 1) == (rel_of(c8, far) ^ me), 1.0, 0.0).astype(BF16)
    for c, span in enumerate(spans):
        ctrl = dot_nn(onehot, ctrl_ref[:, span]).astype(BF16)
        copies[c].wait()
        part = dot_nt(ctrl, tok_ref[:, span])
        if c:
            acc_ref[...] += part
        else:
            acc_ref[...] = part
    soften(acc_ref[...] * scale, gid_ref[...], low_ref, w_ref)
    left = jnp.concatenate([low_ref[0], low_ref[1]], axis=0)
    half = slice_width // 2
    size = pick(half, 512)
    for step in range(half // size):
        base = pl.multiple_of(member * slice_width + step * size, size)
        other = pl.multiple_of(member * slice_width + half + step * size, size)
        expand_into(
            out_refs, left, tok_ref[:, pl.ds(base, size)], tok_ref[:, pl.ds(other, size)], step * size, False
        )


def cot_kernel(src_hbm, low_ref, *refs):
    out_refs, (src_ref, sems) = refs[:NEAR], refs[NEAR:]
    half = src_ref.shape[1] // 2
    steps = sems.shape[0] // 2
    size = half // steps
    spans = [slice(at, at + size) for step in range(steps) for at in (step * size, half + step * size)]
    copies = start_all(
        [pltpu.make_async_copy(src_hbm.at[:, span], src_ref.at[:, span], sems.at[c]) for c, span in enumerate(spans)]
    )
    left = jnp.concatenate([low_ref[0], low_ref[1]], axis=0)
    for step in range(steps):
        copies[2 * step].wait()
        copies[2 * step + 1].wait()
        expand_into(
            out_refs, left, src_ref[:, spans[2 * step]], src_ref[:, spans[2 * step + 1]], step * size, False
        )


def expand_kernel(rhs_t, idx_ref, left_ref, one_ref, two_ref, *out_refs):
    one, two = one_ref[...], two_ref[...]
    one, two = one.reshape(one.shape[-2:]), two.reshape(two.shape[-2:])
    size = one.shape[0] if rhs_t else one.shape[1]
    expand_into(out_refs, left_ref[...], one, two, pl.multiple_of(pl.program_id(0) * size, size), rhs_t)


def expand_weights(name, left, weights, at, pieces, after=()):
    _, _, half, hidden = weights.shape
    size = pick(half, 512)
    rows = left.shape[0] // 2
    outs = [shape_of((rows // pieces, half * 3), BF16)] * pieces
    return call(
        functools.partial(expand_kernel, True),
        name,
        (half // size,),
        [
            whole(left),
            pl.BlockSpec((1, 1, size, hidden), lambda i, idx: (idx[0], 0, i, 0)),
            pl.BlockSpec((1, 1, size, hidden), lambda i, idx: (idx[0], 1, i, 0)),
        ],
        [whole(out) for out in outs],
        outs,
        flops=8 * rows * half * hidden,
        nbytes=4 * half * hidden + 6 * rows * half,
        after=after,
    )(at, left, weights, weights)


def contract_kernel(rhs_t, pieces, idx_ref, one_ref, two_ref, *refs):
    step = pl.program_id(0)
    in_refs, out_ref = refs[:pieces], refs[pieces]
    rows = out_ref.shape[1]
    one, two = one_ref[...], two_ref[...]
    one, two = one.reshape(one.shape[-2:]), two.reshape(two.shape[-2:])
    dot = dot_nt if rhs_t else dot_nn
    size = one.shape[1] if rhs_t else one.shape[0]
    width = in_refs[0].shape[1]
    full = width // 3 * 2
    base = pl.multiple_of(step * size, size)

    def part(start):
        return [ref[:, pl.ds(start + base, size)] for ref in in_refs]

    packed = part(full)
    top = dot(jnp.concatenate(part(0) + packed, axis=0), one)
    low = dot(jnp.concatenate(part(full // 2) + packed, axis=0), two)
    straight = top[:rows] + low[:rows]
    halves = jnp.where(first_half(straight.shape), top[rows:], low[rows:])

    @pl.when(step == 0)
    def _():
        out_ref[0] = straight
        out_ref[1] = halves

    @pl.when(step > 0)
    def _():
        out_ref[0] += straight
        out_ref[1] += halves


def contract_weights(name, parts, weights, at, after=()):
    _, _, half, hidden = weights.shape
    size = pick(half, 512)
    rows = sum(part.shape[0] for part in parts)
    out = shape_of((2, rows, hidden), F32)
    return call(
        functools.partial(contract_kernel, False, len(parts)),
        name,
        (half // size,),
        [
            pl.BlockSpec((1, 1, size, hidden), lambda i, idx: (idx[0], 0, i, 0)),
            pl.BlockSpec((1, 1, size, hidden), lambda i, idx: (idx[0], 1, i, 0)),
        ]
        + [whole(part) for part in parts],
        whole(out),
        out,
        flops=8 * rows * half * hidden,
        nbytes=4 * half * hidden + 6 * rows * half,
        after=after,
    )(at, weights, weights, *parts)


def contract_tokens(name, parts, source, at, after=()):
    half = parts[0].shape[1] // 3
    size = pick(half, 512)
    steps = half // size
    rows = sum(part.shape[0] for part in parts)
    count = source.shape[0]
    out = shape_of((2, rows, count), F32)
    return call(
        functools.partial(contract_kernel, True, len(parts)),
        name,
        (steps,),
        [
            pl.BlockSpec((count, size), lambda i, idx: (0, idx[0] * 2 * steps + i)),
            pl.BlockSpec((count, size), lambda i, idx: (0, idx[0] * 2 * steps + steps + i)),
        ]
        + [whole(part) for part in parts],
        whole(out),
        out,
        flops=8 * rows * half * count,
        nbytes=4 * half * count + 6 * rows * half,
        after=after,
    )(at, source, source, *parts)


def turn_kernel(far, n_narrow, forward, w_in, w_out, *refs):
    others = n_narrow - 1
    count = others * far
    n_in = 1 if forward else 2
    ins, parts = refs[:n_in], refs[n_in : n_in + count]
    refs = refs[n_in + count :]
    out_refs, refs = refs[:count], refs[count:]
    act_ref, refs = refs[0], refs[1:]
    if forward:
        pre_out, refs = refs[0], refs[1:]
    in_bufs, refs = refs[:n_in], refs[n_in:]
    part_ref, wa, wb, sem_in, sem_part, sem_a, sem_b = refs
    member = lax.axis_index("narrow").astype(jnp.int32)
    steps = sem_a.shape[1]
    half = wa.shape[2]
    size = half // steps
    load_a, load_b = [], []
    small = [pltpu.make_async_copy(src, dst, sem_in.at[i]) for i, (src, dst) in enumerate(zip(ins, in_bufs))]
    small += [pltpu.make_async_copy(src, part_ref.at[i], sem_part.at[i]) for i, src in enumerate(parts)]
    for shift in range(1, n_narrow):
        turn = lax.rem(member + n_narrow - shift, n_narrow)
        for step in range(steps):
            span = slice(step * size, (step + 1) * size)
            load_a.append(
                pltpu.make_async_copy(w_in.at[turn, :, span], wa.at[shift - 1, :, span], sem_a.at[shift - 1, step])
            )
    for shift in range(1, n_narrow):
        turn = lax.rem(member + shift, n_narrow)
        for step in range(steps):
            span = slice(step * size, (step + 1) * size)
            load_b.append(
                pltpu.make_async_copy(w_out.at[turn, :, span], wb.at[shift - 1, :, span], sem_b.at[shift - 1, step])
            )
    start_all(small)
    start_all(load_a)
    start_all(load_b)
    for copy in small:
        copy.wait()
    own = in_bufs[0]
    rows = own.shape[1]
    full = 2 * half
    for at in range(others):
        held = [part_ref.at[at * far + k] for k in range(far)]
        for step in range(steps):
            load_a[at * steps + step].wait()
            base = step * size
            packed = [ref[:, full + base : full + base + size] for ref in held]
            one = [ref[:, base : base + size] for ref in held]
            two = [ref[:, half + base : half + base + size] for ref in held]
            top = dot_nn(jnp.concatenate(one + packed, axis=0), wa[at, 0, base : base + size])
            low = dot_nn(jnp.concatenate(two + packed, axis=0), wa[at, 1, base : base + size])
            own[0] += top[:rows] + low[:rows]
            own[1] += jnp.where(first_half(top[rows:].shape), top[rows:], low[rows:])
    halves = own[1]
    other = jnp.where(
        first_half(halves.shape), pltpu.roll(halves, rows - HALF, 0), pltpu.roll(halves, HALF, 0)
    )
    total = jnp.concatenate([own[0], halves + other], axis=0)
    if forward:
        pre_out[...] = total
        act_ref[...] = (total * jax.nn.sigmoid(total)).astype(BF16)
    else:
        pre = in_bufs[1][...]
        sig = jax.nn.sigmoid(pre)
        act_ref[...] = (total * (sig * (1.0 + pre * (1.0 - sig)))).astype(BF16)
    for at in range(others):
        for step in range(steps):
            load_b[at * steps + step].wait()
            base = step * size
            expand_into(
                out_refs[at * far : (at + 1) * far],
                act_ref[...],
                wb[at, 0, base : base + size],
                wb[at, 1, base : base + size],
                base,
                True,
            )


def run_turn(name, far, own, pre, others, w_in, w_out, after=()):
    n_narrow, _, half, hidden = w_in.shape
    flat = [part for one in others for part in one]
    rows = own.shape[1]
    size = pick(half, 512)
    steps = half // size
    forward = pre is None
    ins = [own] if forward else [own, pre]
    piece = flat[0]
    outs = [shape_of(piece.shape, BF16) for _ in flat] + [shape_of((2 * rows, hidden), BF16)]
    if forward:
        outs.append(shape_of((2 * rows, hidden), F32))
    weight = pltpu.VMEM((n_narrow - 1, 2, half, hidden), BF16)
    got = call(
        functools.partial(turn_kernel, far, n_narrow, forward),
        name,
        (1,),
        [ANY] * (2 + len(ins) + len(flat)),
        [whole(out) for out in outs],
        outs,
        scratch=[pltpu.VMEM(array.shape, F32) for array in ins]
        + [
            pltpu.VMEM((len(flat),) + piece.shape, BF16),
            weight,
            weight,
            pltpu.SemaphoreType.DMA((len(ins),)),
            pltpu.SemaphoreType.DMA((len(flat),)),
            pltpu.SemaphoreType.DMA((n_narrow - 1, steps)),
            pltpu.SemaphoreType.DMA((n_narrow - 1, steps)),
        ],
        scalars=0,
        flops=16 * rows * half * hidden * (n_narrow - 1),
        nbytes=(n_narrow - 1) * (8 * half * hidden + 12 * rows * half),
        after=after,
    )(w_in, w_out, *ins, *flat)
    sends = [list(got[at * far : (at + 1) * far]) for at in range(n_narrow - 1)]
    return sends, got[len(flat)], got[-1] if forward else None


def grad_kernel(pieces, steps, idx_ref, act_ref, *refs):
    in_refs, out_ref, held = refs[:-2], refs[-2], refs[-1]
    step = pl.program_id(0)
    size = out_ref.shape[2]
    rows = act_ref.shape[0] // 2

    @pl.when(step == 0)
    def _():
        act = act_ref[...]
        mask = first_half((rows, act.shape[1]))
        zero = jnp.zeros((rows, act.shape[1]), F32)
        low = act[rows:].astype(F32)
        for side in range(2):
            held[side, :rows] = act[:rows]
            held[side, rows:] = (jnp.where(mask, low, zero) if side == 0 else jnp.where(mask, zero, low)).astype(BF16)

    for turn in range(len(in_refs) // pieces):

        @pl.when(step // steps == turn)
        def _():
            own = in_refs[turn * pieces : (turn + 1) * pieces]
            full = own[0].shape[1] // 3 * 2
            base = pl.multiple_of(lax.rem(step, steps) * size, size)
            packed = [ref[:, pl.ds(full + base, size)] for ref in own]
            for side in range(2):
                straight = [ref[:, pl.ds(side * (full // 2) + base, size)] for ref in own]
                out_ref[0, side] = dot_tn(jnp.concatenate(straight + packed, axis=0), held[side]).astype(BF16)


def weight_grad(name, act, slices, like, at, after=()):
    parts_n, _, half, hidden = like
    size = pick(half, 512)
    steps = half // size
    pieces = len(slices[0])
    flat = [part for one in slices for part in one]
    rows = act.shape[0] // 2
    out = shape_of(like, BF16)
    return call(
        functools.partial(grad_kernel, pieces, steps),
        name,
        (parts_n * steps,),
        [whole(act)] + [whole(part) for part in flat],
        pl.BlockSpec((1, 2, size, hidden), lambda i, idx: (idx[i // steps], 0, lax.rem(i, steps), 0)),
        out,
        scratch=[pltpu.VMEM((2, 2 * rows, hidden), BF16)],
        flops=8 * rows * half * parts_n * hidden,
        nbytes=parts_n * (4 * half * hidden + 6 * rows * half),
        after=after,
    )(at, act, *flat)


def mix_kernel(pieces, slice_width, src_hbm, gid_ref, prev_hbm, *refs):
    parts, (out_ref, prev_ref, src_ref, part_ref, sems, sem_prev, sem_part) = refs[:pieces], refs[pieces:]
    member = lax.axis_index("narrow").astype(jnp.int32)
    half = slice_width // 2
    steps = sems.shape[0] // 2
    size = half // steps
    small = [pltpu.make_async_copy(src, part_ref.at[i], sem_part.at[i]) for i, src in enumerate(parts)]
    spans = [slice(at, at + size) for step in range(steps) for at in (step * size, half + step * size)]
    copies = [
        pltpu.make_async_copy(
            src_hbm.at[:, pl.ds(pl.multiple_of(member * slice_width + span.start, size), size)],
            src_ref.at[:, span],
            sems.at[c],
        )
        for c, span in enumerate(spans)
    ]
    prev = pltpu.make_async_copy(prev_hbm, prev_ref, sem_prev.at[0])
    start_all(small)
    start_all(copies)
    prev.start()
    for copy in small:
        copy.wait()
    prev.wait()
    rows = prev_ref.shape[1]
    full = 2 * half
    held = [part_ref.at[k] for k in range(pieces)]
    for step in range(steps):
        copies[2 * step].wait()
        copies[2 * step + 1].wait()
        base = step * size
        packed = [ref[:, full + base : full + base + size] for ref in held]
        one = [ref[:, base : base + size] for ref in held]
        two = [ref[:, half + base : half + base + size] for ref in held]
        top = dot_nt(jnp.concatenate(one + packed, axis=0), src_ref[:, spans[2 * step]])
        low = dot_nt(jnp.concatenate(two + packed, axis=0), src_ref[:, spans[2 * step + 1]])
        prev_ref[0] += top[:rows] + low[:rows]
        prev_ref[1] += jnp.where(first_half(top[rows:].shape), top[rows:], low[rows:])
    in_a, in_b = group_masks(gid_ref[...], rows)
    picked = jnp.where(in_a, prev_ref[0], 0.0) + jnp.where(in_b, prev_ref[1], 0.0)
    out_ref[...] = jnp.sum(picked.reshape(rows // SUB, SUB, -1), axis=1)


def ctrl_kernel(far, scale, turns, slice_width, tok_hbm, gid_ref, w_ref, *refs):
    mix_refs, (low_ref, out_ref, tok_ref, sems) = refs[:turns], refs[turns:]
    me, member = placed_here()
    experts, count = w_ref.shape
    cols = SUB * experts
    steps = sems.shape[0]
    size = slice_width // steps
    spans = [slice(step * size, (step + 1) * size) for step in range(steps)]
    copies = start_all(
        [
            pltpu.make_async_copy(
                tok_hbm.at[:, pl.ds(pl.multiple_of(member * slice_width + span.start, size), size)],
                tok_ref.at[:, span],
                sems.at[c],
            )
            for c, span in enumerate(spans)
        ]
    )
    mix = mix_refs[0][...]
    for ref in mix_refs[1:]:
        mix = mix + ref[...]
    weights = w_ref[...]
    in_a, in_b = group_masks(gid_ref[...], cols)
    spread = jnp.broadcast_to((weights * mix)[:, None, :], (experts, SUB, count)).reshape(cols, count)
    sum_a = jnp.sum(jnp.where(in_a, spread, 0.0), axis=1, keepdims=True)
    sum_b = jnp.sum(jnp.where(in_b, spread, 0.0), axis=1, keepdims=True)
    in_b = jnp.logical_and(in_b, first_half((cols, count)))
    back = jnp.where(in_a, sum_a, 0.0) + jnp.where(in_b, sum_b, 0.0)
    total = jnp.sum(back.reshape(experts, SUB, count), axis=1)
    low = (weights * (mix - total)).astype(BF16)
    place = rel_of(iota((experts, experts), 1), far) ^ me
    onehot = jnp.where(iota((experts, experts), 0) == place, 1.0, 0.0).astype(BF16)
    low_ref[...] = dot_nn(onehot, low).astype(BF16)
    for step in range(steps):
        copies[step].wait()
        out_ref[:, spans[step]] = (scale * dot_nn(low_ref[...], tok_ref[:, spans[step]])).astype(BF16)


def token_kernel(scale, steps, pieces, idx_ref, left_ref, low_ref, ctrl_ref, *refs):
    in_refs, out_ref = refs[:pieces], refs[pieces]
    step = pl.program_id(0)
    size = out_ref.shape[1]
    full = in_refs[0].shape[1] // 3 * 2
    base = pl.multiple_of(step * size, size)
    lower = pl.multiple_of(lax.rem(step, steps) * size, size)
    straight = [ref[:, pl.ds(base, size)] for ref in in_refs]
    packed = [ref[:, pl.ds(full + lower, size)] for ref in in_refs]
    back = dot_tn(left_ref[0], jnp.concatenate(straight + packed, axis=0))
    out_ref[...] = (back + scale * dot_tn(low_ref[...], ctrl_ref[...])).astype(BF16)


def on_device(sizes, tokens, group_slot, controller, expert_in, expert_out, cotangent):
    n_dp, n_narrow = sizes
    count, model_width = tokens.shape
    slice_width = cotangent.shape[1]
    half = slice_width // 2
    experts = controller.shape[1]
    hidden = expert_in.shape[2]
    far = n_dp // NEAR
    cols = SUB * experts
    assert experts == n_dp and count // GSIZE == SUB + HALF and far & (far - 1) == 0
    scale = 1.0 / math.sqrt(model_width)
    me = lax.axis_index("dp").astype(jnp.int32)
    member = lax.axis_index("narrow").astype(jnp.int32)
    turns = [lax.rem(member - shift + n_narrow, n_narrow) for shift in range(n_narrow)]
    at = [jnp.stack([turn, me]) for turn in turns]
    zero = jnp.stack([jnp.zeros_like(me), me])
    order = jnp.stack(turns)
    gid = lax.shift_right_logical(group_slot, int(math.log2(GSIZE)))
    ctrl_t = controller.T
    first = expert_in.reshape(n_narrow, 2, half, hidden)
    second = expert_out.reshape(n_narrow, 2, half, hidden)

    def swap(array, bits):
        return lax.ppermute(array, "dp", [(i, i ^ bits) for i in range(n_dp)]) if bits else array

    def shifted(array, shift):
        return lax.ppermute(array, "narrow", [(i, (i + shift) % n_narrow) for i in range(n_narrow)])

    def regroup(parts):
        return [
            jnp.concatenate([part[SUB * at_row : SUB * (at_row + 1)] for part in parts], axis=0)
            for at_row in range(parts[0].shape[0] // SUB)
        ]

    def outward(parts):
        parts = [swap(part, bits) for bits, part in enumerate(parts)]
        parts = [swap(part, NEAR * bits) for bits, part in enumerate(regroup(parts))]
        return [parts] + [[shifted(part, shift) for part in parts] for shift in range(1, n_narrow)]

    def homeward(own, others):
        parts = []
        for bits in range(far):
            total = own[bits].astype(F32)
            for shift, other in enumerate(others, 1):
                total = total + shifted(other[bits], shift).astype(F32)
            parts.append(total.astype(BF16))
        parts = [swap(part, NEAR * bits) for bits, part in enumerate(parts)]
        return [swap(part, bits) for bits, part in enumerate(regroup(parts))]

    packed = shape_of((SUB * far, 3 * half), BF16)
    low_shape, w_shape = shape_of((2, cols, count), BF16), shape_of((experts, count), F32)
    outs = [packed] * NEAR + [low_shape, w_shape]
    chunks = 8
    *rows_out, low, weights = call(
        functools.partial(head_kernel, far, scale, slice_width),
        "head",
        (1,),
        [ANY, whole(ctrl_t), whole(gid)],
        [whole(out) for out in outs],
        outs,
        scratch=[
            pltpu.VMEM((count, model_width), BF16),
            pltpu.VMEM((cols, count), F32),
            pltpu.SemaphoreType.DMA((chunks,)),
        ],
        scalars=0,
        flops=2 * cols * count * model_width,
        nbytes=2 * count * model_width,
    )(tokens, ctrl_t, gid)
    mixed = outward(rows_out)
    size = pick(half, 512)
    cot_out = call(
        cot_kernel,
        "cot",
        (1,),
        [ANY, whole(low_shape)],
        [whole(packed)] * NEAR,
        [packed] * NEAR,
        scratch=[pltpu.VMEM((count, slice_width), BF16), pltpu.SemaphoreType.DMA((2 * (half // size),))],
        scalars=0,
        flops=4 * cols * count * slice_width,
        nbytes=2 * count * slice_width,
    )(cotangent, low)
    mixed_cot = outward(cot_out)

    pre_own = contract_weights("pre_own", mixed[0], first, at[0])
    sends, hidden_act, pre = run_turn("turn_result", far, pre_own, None, mixed[1:], first, second)
    slope_own = contract_weights("slope_own", mixed_cot[0], second, at[0], after=(sends[0][0],))
    result_own = expand_weights("result_own", hidden_act, second, at[0], far, after=(slope_own,))
    result = homeward(result_own, sends)
    sends, act_grad, _ = run_turn("turn_back", far, slope_own, pre, mixed_cot[1:], second, first)
    back_own = expand_weights("back_own", act_grad, first, at[0], far)
    back = homeward(back_own, sends)
    out_grad = weight_grad("out_grad", hidden_act, mixed_cot, second.shape, order, after=(back_own[0],))
    in_grad = weight_grad("in_grad", act_grad, mixed, first.shape, order, after=(out_grad,))

    mix_one = contract_tokens("mix_result", result, cotangent, zero, after=(in_grad,))
    out_grad, in_grad = out_grad.reshape(expert_out.shape), in_grad.reshape(expert_in.shape)
    size = pick(half, 512)
    mix = call(
        functools.partial(mix_kernel, NEAR, slice_width),
        "mix_back",
        (1,),
        [ANY, whole(gid), ANY] + [ANY] * NEAR,
        whole(w_shape),
        w_shape,
        scratch=[
            pltpu.VMEM((2, cols, count), F32),
            pltpu.VMEM((count, slice_width), BF16),
            pltpu.VMEM((NEAR,) + back[0].shape, BF16),
            pltpu.SemaphoreType.DMA((2 * (half // size),)),
            pltpu.SemaphoreType.DMA((1,)),
            pltpu.SemaphoreType.DMA((NEAR,)),
        ],
        scalars=0,
        flops=4 * cols * count * slice_width,
        nbytes=2 * count * slice_width + 6 * cols * half,
    )(tokens, gid, mix_one, *back)
    mixes = [mix] + [shifted(mix, shift) for shift in range(1, n_narrow)]
    steps = slice_width // pick(slice_width, 1024)
    low_grad, ctrl_part = call(
        functools.partial(ctrl_kernel, far, scale, n_narrow, slice_width),
        "ctrl",
        (1,),
        [ANY, whole(gid), whole(weights)] + [whole(mix)] * n_narrow,
        [whole(shape_of((experts, count), BF16)), whole(shape_of((experts, slice_width), BF16))],
        [shape_of((experts, count), BF16), shape_of((experts, slice_width), BF16)],
        scratch=[pltpu.VMEM((count, slice_width), BF16), pltpu.SemaphoreType.DMA((steps,))],
        scalars=0,
        flops=2 * experts * count * slice_width,
        nbytes=2 * count * slice_width,
    )(tokens, gid, weights, *mixes)
    bits = 1
    total = ctrl_part.astype(F32)
    while bits < n_dp:
        total = total.astype(BF16)
        total = total.astype(F32) + swap(total, bits).astype(F32)
        bits *= 2
    ctrl_grad = total.T

    size = pick(half, 512)
    steps = half // size
    side = jnp.where((jnp.arange(cols) & HALF)[:, None] == 0, low[1], jnp.zeros_like(low[1]))
    sides = jnp.stack([jnp.concatenate([low[0], side]), jnp.concatenate([low[0], low[1] - side])])
    token_grad = call(
        functools.partial(token_kernel, scale, steps, len(back)),
        "token_grad",
        (2 * steps,),
        [
            pl.BlockSpec((1, 2 * cols, count), lambda i, idx: (i // steps, 0, 0)),
            whole(low_grad),
            pl.BlockSpec((experts, size), lambda i, idx: (0, idx[0] * 2 * steps + i)),
        ]
        + [whole(part) for part in back],
        pl.BlockSpec((count, size), lambda i, idx: (0, i)),
        shape_of((count, slice_width), BF16),
        flops=4 * cols * count * slice_width,
        nbytes=2 * count * slice_width,
    )(at[0], sides, low_grad, ctrl_t, *back)
    return (token_grad, ctrl_grad, in_grad, out_grad)


def solution(mesh):
    sizes = (mesh.shape["dp"], mesh.shape["narrow"])
    placed = (
        P("dp", None),
        P("dp", None),
        P(),
        P("dp", None, "narrow"),
        P("dp", None, "narrow"),
        P("dp", "narrow"),
    )
    return jax.shard_map(
        functools.partial(on_device, sizes),
        mesh=mesh,
        in_specs=placed,
        out_specs=(
            P("dp", "narrow"),
            P("narrow", None),
            P("dp", None, "narrow"),
            P("dp", None, "narrow"),
        ),
        check_vma=False,
    )
```

```python
import functools
import math

import jax
import jax.numpy as jnp
from jax import lax
from jax.experimental import pallas as pl
from jax.experimental.pallas import tpu as pltpu
from jax.sharding import PartitionSpec as P


GSIZE = 32
SUB = 8
HALF = 4
NEAR = 4
F32 = jnp.float32
BF16 = jnp.bfloat16
VMEM_LIMIT = 32 * 1024 * 1024


def dot_nn(a, b):
    return lax.dot_general(a, b, (((1,), (0,)), ((), ())), preferred_element_type=F32)


def dot_nt(a, b):
    return lax.dot_general(a, b, (((1,), (1,)), ((), ())), preferred_element_type=F32)


def dot_tn(a, b):
    return lax.dot_general(a, b, (((0,), (0,)), ((), ())), preferred_element_type=F32)


def iota(shape, dim):
    return lax.broadcasted_iota(jnp.int32, shape, dim)


def first_half(shape):
    return (iota(shape, 0) & HALF) == 0


def pick(width, most):
    size = most
    while width % size:
        size //= 2
    return size


ANY = pl.BlockSpec(memory_space=pl.ANY)


def call(kernel, grid, in_specs, out_specs, out_shape, scratch=(), scalars=1, flops=0, nbytes=0, after=()):
    skip = len(after)

    def body(*refs):
        kernel(*refs[:scalars], *refs[scalars + skip :])

    run = pl.pallas_call(
        body,
        grid_spec=pltpu.PrefetchScalarGridSpec(
            num_scalar_prefetch=scalars,
            grid=grid,
            in_specs=[ANY] * skip + list(in_specs),
            out_specs=out_specs,
            scratch_shapes=list(scratch),
        ),
        out_shape=out_shape,
        compiler_params=pltpu.CompilerParams(
            dimension_semantics=("arbitrary",) * len(grid),
            vmem_limit_bytes=VMEM_LIMIT,
        ),
        cost_estimate=pl.CostEstimate(flops=int(flops), bytes_accessed=int(nbytes), transcendentals=0),
    )
    return lambda *args: run(*args[:scalars], *after, *args[scalars:])


def placed_here():
    return lax.axis_index("dp").astype(jnp.int32), lax.axis_index("narrow").astype(jnp.int32)


def start_all(copies):
    for copy in copies:
        copy.start()
    return copies


def whole(array):
    rank = len(array.shape)
    return pl.BlockSpec(array.shape, lambda *_: (0,) * rank)


def shape_of(dims, dtype):
    return jax.ShapeDtypeStruct(dims, dtype)


def rel_of(c8, far):
    return (c8 % far) * NEAR + c8 // far if isinstance(c8, int) else (
        (c8 & (far - 1)) * NEAR + lax.shift_right_logical(c8, far.bit_length() - 1)
    )


def group_masks(gid, cols):
    row = iota((cols, gid.shape[1]), 0)
    in_a = gid == (row & (SUB - 1))
    in_b = gid == (SUB + (row & (HALF - 1)))
    return in_a, in_b


def soften(logits, gid, low_ref, w_ref):
    experts = w_ref.shape[0]
    masks = group_masks(gid, logits.shape[0])
    shared = jnp.zeros_like(logits)
    for part, mask in enumerate(masks):
        top = jnp.max(jnp.where(mask, logits, -jnp.inf), axis=1, keepdims=True)
        raised = jnp.where(mask, jnp.exp(jnp.where(mask, logits - top, 0.0)), 0.0)
        weights = raised / jnp.sum(raised, axis=1, keepdims=True)
        low_ref[part] = weights.astype(BF16)
        if part:
            weights = jnp.where(first_half(weights.shape), weights, 0.0)
        shared += weights
    w_ref[...] = jnp.sum(shared.reshape(experts, SUB, -1), axis=1)


def plan(refs, by_far, far):
    if not by_far:
        each = refs[0].shape[0]
        return [(ref, 0, at * each, each) for at, ref in enumerate(refs)]
    return [(ref, SUB * y, SUB * (y * far + k), SUB) for k, ref in enumerate(refs) for y in range(NEAR)]


def expand_into(targets, left, one, two, base, rhs_t):
    rows = left.shape[0] // 2
    dot = dot_nt if rhs_t else dot_nn
    size = one.shape[0] if rhs_t else one.shape[1]
    top, low = dot(left, one), dot(left, two)
    mixed = jnp.where(first_half((rows, size)), top[rows:], low[rows:])
    for ref, to, at, many in targets:
        wide = ref.shape[1] // 3
        for place, value in enumerate((top, low, mixed)):
            ref[to : to + many, pl.ds(place * wide + base, size)] = value[at : at + many].astype(BF16)


def head_kernel(far, scale, slice_width, tok_hbm, ctrl_ref, slot_ref, *refs):
    out_refs, (gid_ref, low_ref, w_ref, tok_ref, acc_ref, sems) = refs[:-6], refs[-6:]
    targets_of = [plan(out_refs[:NEAR], False, far)]
    if out_refs[NEAR:]:
        targets_of.append(plan(out_refs[NEAR:], True, far))
    _, width = tok_ref.shape
    chunks = sems.shape[0]
    size = width // chunks
    spans = [slice(c * size, (c + 1) * size) for c in range(chunks)]
    copies = start_all(
        [pltpu.make_async_copy(tok_hbm.at[:, span], tok_ref.at[:, span], sems.at[c]) for c, span in enumerate(spans)]
    )
    me, member = placed_here()
    experts = ctrl_ref.shape[0]
    cols = SUB * experts
    c8 = lax.shift_right_logical(iota((experts, cols), 1), 3)
    onehot = jnp.where(iota((experts, cols), 0) == (rel_of(c8, far) ^ me), 1.0, 0.0).astype(BF16)
    gid_ref[...] = lax.shift_right_logical(slot_ref[...], GSIZE.bit_length() - 1)
    for c, span in enumerate(spans):
        ctrl = dot_tn(ctrl_ref[:, span], onehot).astype(BF16)
        copies[c].wait()
        part = dot_nn(tok_ref[:, span], ctrl)
        if c:
            acc_ref[...] += part
        else:
            acc_ref[...] = part
    soften(acc_ref[...].T * scale, gid_ref[...], low_ref, w_ref)
    left = jnp.concatenate([low_ref[0], low_ref[1]], axis=0)
    half = slice_width // 2
    part = half // len(targets_of)
    size = pick(part, 768)
    for which, targets in enumerate(targets_of):
        for step in range(part // size):
            start = member * slice_width + which * part + step * size
            one = pl.multiple_of(start, 128)
            two = pl.multiple_of(start + half, 128)
            expand_into(
                targets, left, tok_ref[:, pl.ds(one, size)], tok_ref[:, pl.ds(two, size)], step * size, False
            )


def cot_kernel(src_hbm, low_ref, *refs):
    out_refs, (src_ref, sems) = refs[:NEAR], refs[NEAR:]
    half = src_ref.shape[1] // 2
    steps = sems.shape[0] // 2
    size = half // steps
    spans = [slice(at, at + size) for step in range(steps) for at in (step * size, half + step * size)]
    copies = start_all(
        [pltpu.make_async_copy(src_hbm.at[:, span], src_ref.at[:, span], sems.at[c]) for c, span in enumerate(spans)]
    )
    left = jnp.concatenate([low_ref[0], low_ref[1]], axis=0)
    for step in range(steps):
        copies[2 * step].wait()
        copies[2 * step + 1].wait()
        expand_into(
            plan(out_refs, False, 0),
            left,
            src_ref[:, spans[2 * step]],
            src_ref[:, spans[2 * step + 1]],
            step * size,
            False,
        )


def expand_kernel(per, idx_ref, left_ref, one_ref, two_ref, *out_refs):
    one, two = one_ref[0, 0], two_ref[0, 0]
    size = one.shape[0]
    step = pl.program_id(0)
    for chunk, out_ref in enumerate(out_refs):

        @pl.when(step // per == chunk)
        def _():
            base = pl.multiple_of(lax.rem(step, per) * size, size)
            expand_into(plan([out_ref], False, 0), left_ref[...], one, two, base, True)


def expand_weights(left, weights, at, chunks, after=()):
    _, _, half, hidden = weights.shape
    part = half // chunks
    size = pick(part, 768)
    rows = left.shape[0] // 2
    outs = [shape_of((rows, part * 3), BF16)] * chunks
    return call(
        functools.partial(expand_kernel, part // size),
        (half // size,),
        [
            whole(left),
            pl.BlockSpec((1, 1, size, hidden), lambda i, idx: (idx[0], 0, i, 0)),
            pl.BlockSpec((1, 1, size, hidden), lambda i, idx: (idx[0], 1, i, 0)),
        ],
        [whole(out) for out in outs],
        outs,
        flops=8 * rows * half * hidden,
        nbytes=4 * half * hidden + 6 * rows * half,
        after=after,
    )(at, left, weights, weights)


def contract_kernel(rhs_t, pieces, idx_ref, one_ref, two_ref, *refs):
    step = pl.program_id(0)
    in_refs, out_ref = refs[:pieces], refs[pieces]
    rows = out_ref.shape[1]
    one, two = one_ref[...], two_ref[...]
    one, two = one.reshape(one.shape[-2:]), two.reshape(two.shape[-2:])
    dot = dot_nt if rhs_t else dot_nn
    size = one.shape[1] if rhs_t else one.shape[0]
    width = in_refs[0].shape[1]
    full = width // 3 * 2
    base = pl.multiple_of(step * size, size)

    def part(start):
        return [ref[:, pl.ds(start + base, size)] for ref in in_refs]

    packed = part(full)
    top = dot(jnp.concatenate(part(0) + packed, axis=0), one)
    low = dot(jnp.concatenate(part(full // 2) + packed, axis=0), two)
    straight = top[:rows] + low[:rows]
    halves = jnp.where(first_half(straight.shape), top[rows:], low[rows:])

    @pl.when(step == 0)
    def _():
        out_ref[0] = straight
        out_ref[1] = halves

    @pl.when(step > 0)
    def _():
        out_ref[0] += straight
        out_ref[1] += halves


def contract_tokens(parts, source, at, after=()):
    half = parts[0].shape[1] // 3
    size = pick(half, 512)
    steps = half // size
    rows = sum(part.shape[0] for part in parts)
    count = source.shape[0]
    out = shape_of((2, rows, count), F32)
    return call(
        functools.partial(contract_kernel, True, len(parts)),
        (steps,),
        [
            pl.BlockSpec((count, size), lambda i, idx: (0, idx[0] * 2 * steps + i)),
            pl.BlockSpec((count, size), lambda i, idx: (0, idx[0] * 2 * steps + steps + i)),
        ]
        + [whole(part) for part in parts],
        whole(out),
        out,
        flops=8 * rows * half * count,
        nbytes=4 * half * count + 6 * rows * half,
        after=after,
    )(at, source, source, *parts)


def rows_of(by_far, far, piece):
    if by_far:
        return [(0, SUB * NEAR * piece, SUB * NEAR)]
    return [(SUB * k, SUB * (NEAR * k + piece), SUB) for k in range(far)]


def turn_kernel(far, n_narrow, orders, sends, forward, w_in, w_out, *refs):
    chunks, others = len(orders), n_narrow - 1
    n_in = 0 if forward else 1
    count = n_narrow * sum(far if by_far else NEAR for by_far in orders)
    ins, parts, refs = refs[:n_in], refs[n_in : n_in + count], refs[n_in + count :]
    out_refs, refs = refs[: others * sends], refs[others * sends :]
    act_ref, all_ref, refs = refs[0], refs[1], refs[2:]
    if forward:
        pre_out, refs = refs[0], refs[1:]
    in_bufs, refs = refs[:n_in], refs[n_in:]
    acc, wa, wb, sem_in, sem_part, sem_a, sem_b = refs
    member = lax.axis_index("narrow").astype(jnp.int32)
    steps = sem_a.shape[1]
    half = wa.shape[2]
    size = half // steps
    small = [pltpu.make_async_copy(src, dst, sem_in.at[i]) for i, (src, dst) in enumerate(zip(ins, in_bufs))]
    at = 0
    moves = 0
    for shift in range(n_narrow):
        for chunk, by_far in enumerate(orders):
            for piece in range(far if by_far else NEAR):
                for src, dst, many in rows_of(by_far, far, piece):
                    small.append(
                        pltpu.make_async_copy(
                            parts[at].at[src : src + many],
                            all_ref.at[shift, chunk, dst : dst + many],
                            sem_part.at[moves],
                        )
                    )
                    moves += 1
                at += 1
    load_a, load_b = [], []
    for shift in range(n_narrow):
        turn = lax.rem(member + n_narrow - shift, n_narrow)
        for step in range(steps):
            span = slice(step * size, (step + 1) * size)
            load_a.append(pltpu.make_async_copy(w_in.at[turn, :, span], wa.at[shift, :, span], sem_a.at[shift, step]))
    for shift in range(1, n_narrow):
        turn = lax.rem(member + shift, n_narrow)
        for step in range(steps):
            span = slice(step * size, (step + 1) * size)
            load_b.append(
                pltpu.make_async_copy(w_out.at[turn, :, span], wb.at[shift - 1, :, span], sem_b.at[shift - 1, step])
            )
    start_all(small)
    start_all(load_a)
    start_all(load_b)
    for copy in small:
        copy.wait()
    rows = acc.shape[1]
    part = half // chunks
    for shift in range(n_narrow):
        for step in range(steps):
            load_a[shift * steps + step].wait()
            base = step * size
            chunk, within = base // part, base % part
            packed = all_ref[shift, chunk, :, 2 * part + within : 2 * part + within + size]
            one = all_ref[shift, chunk, :, within : within + size]
            two = all_ref[shift, chunk, :, part + within : part + within + size]
            top = dot_nn(jnp.concatenate([one, packed], axis=0), wa[shift, 0, base : base + size])
            low = dot_nn(jnp.concatenate([two, packed], axis=0), wa[shift, 1, base : base + size])
            straight = top[:rows] + low[:rows]
            halves = jnp.where(first_half(straight.shape), top[rows:], low[rows:])
            if shift or step:
                acc[0] += straight
                acc[1] += halves
            else:
                acc[0] = straight
                acc[1] = halves
    halves = acc[1]
    other = jnp.where(
        first_half(halves.shape), pltpu.roll(halves, rows - HALF, 0), pltpu.roll(halves, HALF, 0)
    )
    total = jnp.concatenate([acc[0], halves + other], axis=0)
    if forward:
        pre_out[...] = total
        act_ref[...] = (total * jax.nn.sigmoid(total)).astype(BF16)
    else:
        pre = in_bufs[0][...]
        sig = jax.nn.sigmoid(pre)
        act_ref[...] = (total * (sig * (1.0 + pre * (1.0 - sig)))).astype(BF16)
    part = half // sends
    for at in range(others):
        for step in range(steps):
            load_b[at * steps + step].wait()
            base = step * size
            expand_into(
                plan([out_refs[at * sends + base // part]], False, 0),
                act_ref[...],
                wb[at, 0, base : base + size],
                wb[at, 1, base : base + size],
                base % part,
                True,
            )


def run_turn(far, pre, slices, orders, sends, w_in, w_out, after=()):
    n_narrow, _, half, hidden = w_in.shape
    flat = [piece for one in slices for chunk in one for piece in chunk]
    cols = sum(piece.shape[0] for piece in slices[0][0])
    chunks = len(orders)
    size = pick(half // max(chunks, sends), 768)
    steps = half // size
    forward = pre is None
    ins = [] if forward else [pre]
    outs = [shape_of((cols, half // sends * 3), BF16)] * ((n_narrow - 1) * sends)
    outs += [shape_of((2 * cols, hidden), BF16), shape_of((n_narrow, chunks, cols, half // chunks * 3), BF16)]
    if forward:
        outs.append(shape_of((2 * cols, hidden), F32))
    moves = n_narrow * sum(len(rows_of(f, far, p)) for f in orders for p in range(far if f else NEAR))
    got = call(
        functools.partial(turn_kernel, far, n_narrow, orders, sends, forward),
        (1,),
        [ANY] * (2 + len(ins) + len(flat)),
        [whole(out) for out in outs],
        outs,
        scratch=[pltpu.VMEM(array.shape, F32) for array in ins]
        + [
            pltpu.VMEM((2, cols, hidden), F32),
            pltpu.VMEM((n_narrow, 2, half, hidden), BF16),
            pltpu.VMEM((n_narrow - 1, 2, half, hidden), BF16),
            pltpu.SemaphoreType.DMA((max(len(ins), 1),)),
            pltpu.SemaphoreType.DMA((moves,)),
            pltpu.SemaphoreType.DMA((n_narrow, steps)),
            pltpu.SemaphoreType.DMA((n_narrow - 1, steps)),
        ],
        scalars=0,
        flops=8 * cols * half * hidden * (2 * n_narrow - 1),
        nbytes=(2 * n_narrow - 1) * (4 * half * hidden + 6 * cols * half),
        after=after,
    )(w_in, w_out, *ins, *flat)
    count = (n_narrow - 1) * sends
    out = [list(got[at * sends : (at + 1) * sends]) for at in range(n_narrow - 1)]
    return out, got[count], got[count + 1], got[-1] if forward else None


def grad_kernel(idx_ref, act_ref, one_ref, two_ref, packed_ref, out_ref, held):
    rows = act_ref.shape[0] // 2

    @pl.when(pl.program_id(0) == 0)
    def _():
        act = act_ref[...]
        mask = first_half((rows, act.shape[1]))
        low = act[rows:].astype(F32)
        zero = jnp.zeros_like(low)
        for side in range(2):
            held[side, :rows] = act[:rows]
            held[side, rows:] = (jnp.where(mask, low, zero) if side == 0 else jnp.where(mask, zero, low)).astype(BF16)

    packed = packed_ref[0, 0]
    out_ref[0, 0] = dot_tn(jnp.concatenate([one_ref[0, 0], packed], axis=0), held[0]).astype(BF16)
    out_ref[0, 1] = dot_tn(jnp.concatenate([two_ref[0, 0], packed], axis=0), held[1]).astype(BF16)


def weight_grad(act, gathered, like, at, after=()):
    parts_n, _, half, hidden = like
    _, chunks, rows, _ = gathered.shape
    part = half // chunks
    size = pick(part, 768)
    per, steps = part // size, half // size
    out = shape_of(like, BF16)

    def rows_at(place):
        return pl.BlockSpec(
            (1, 1, rows, size),
            lambda i, idx: (i // steps, lax.rem(i, steps) // per, 0, place * per + lax.rem(i, per)),
        )

    return call(
        grad_kernel,
        (parts_n * steps,),
        [whole(act), rows_at(0), rows_at(1), rows_at(2)],
        pl.BlockSpec(
            (1, 2, size, hidden),
            lambda i, idx: (lax.rem(idx[0] + parts_n - i // steps, parts_n), 0, lax.rem(i, steps), 0),
        ),
        out,
        scratch=[pltpu.VMEM((2, 2 * rows, hidden), BF16)],
        flops=8 * rows * half * parts_n * hidden,
        nbytes=parts_n * (4 * half * hidden + 6 * rows * half),
        after=after,
    )(at, act, gathered, gathered, gathered)


def regroup_kernel(count, *refs):
    ins, outs, sems = refs[:count], refs[count:-1], refs[-1]
    copies = start_all(
        [
            pltpu.make_async_copy(
                src.at[SUB * j : SUB * (j + 1)], dst.at[SUB * i : SUB * (i + 1)], sems.at[i * len(outs) + j]
            )
            for i, src in enumerate(ins)
            for j, dst in enumerate(outs)
        ]
    )
    for copy in copies:
        copy.wait()


def regroup(parts):
    many = parts[0].shape[0] // SUB
    out = shape_of((SUB * len(parts), parts[0].shape[1]), BF16)
    return call(
        functools.partial(regroup_kernel, len(parts)),
        (1,),
        [ANY] * len(parts),
        [whole(out)] * many,
        [out] * many,
        scratch=[pltpu.SemaphoreType.DMA((many * len(parts),))],
        scalars=0,
        nbytes=4 * many * out.shape[0] * out.shape[1],
    )(*parts)


def sum_kernel(count, *refs):
    ins, outs, (buf, sems) = refs[:count], refs[count:-2], refs[-2:]
    each = outs[0].shape[0]
    copies = [
        [
            pltpu.make_async_copy(
                src.at[k * each : (k + 1) * each], buf.at[i, k * each : (k + 1) * each], sems.at[k * count + i]
            )
            for i, src in enumerate(ins)
        ]
        for k in range(len(outs))
    ]
    for some in copies:
        start_all(some)
    for k, out_ref in enumerate(outs):
        for copy in copies[k]:
            copy.wait()
        total = buf[0, k * each : (k + 1) * each].astype(F32)
        for i in range(1, count):
            total = total + buf[i, k * each : (k + 1) * each].astype(F32)
        out_ref[...] = total.astype(BF16)


def sum_parts(arrays, pieces):
    rows, width = arrays[0].shape
    out = shape_of((rows // pieces, width), BF16)
    return call(
        functools.partial(sum_kernel, len(arrays)),
        (1,),
        [ANY] * len(arrays),
        [whole(out)] * pieces,
        [out] * pieces,
        scratch=[
            pltpu.VMEM((len(arrays), rows, width), BF16),
            pltpu.SemaphoreType.DMA((len(arrays) * pieces,)),
        ],
        scalars=0,
        nbytes=2 * (len(arrays) + 1) * rows * width,
    )(*arrays)


def mix_kernel(chunks, slice_width, src_hbm, gid_ref, prev_hbm, *refs):
    count = chunks * NEAR
    parts, (out_ref, prev_ref, src_ref, part_ref, sems, sem_prev, sem_part) = refs[:count], refs[count:]
    member = lax.axis_index("narrow").astype(jnp.int32)
    half = slice_width // 2
    part = half // chunks
    steps = sems.shape[0] // 2
    size = half // steps
    each = parts[0].shape[0]
    small = [
        pltpu.make_async_copy(
            src, part_ref.at[i // NEAR, (i % NEAR) * each : (i % NEAR + 1) * each], sem_part.at[i]
        )
        for i, src in enumerate(parts)
    ]
    spans = [slice(at, at + size) for step in range(steps) for at in (step * size, half + step * size)]
    copies = [
        pltpu.make_async_copy(
            src_hbm.at[:, pl.ds(pl.multiple_of(member * slice_width + span.start, 128), size)],
            src_ref.at[:, span],
            sems.at[c],
        )
        for c, span in enumerate(spans)
    ]
    prev = pltpu.make_async_copy(prev_hbm, prev_ref, sem_prev.at[0])
    start_all(small)
    start_all(copies)
    prev.start()
    for copy in small:
        copy.wait()
    prev.wait()
    rows = prev_ref.shape[1]
    for step in range(steps):
        copies[2 * step].wait()
        copies[2 * step + 1].wait()
        chunk, base = step * size // part, step * size % part
        packed = part_ref[chunk, :, 2 * part + base : 2 * part + base + size]
        one = part_ref[chunk, :, base : base + size]
        two = part_ref[chunk, :, part + base : part + base + size]
        top = dot_nt(jnp.concatenate([one, packed], axis=0), src_ref[:, spans[2 * step]])
        low = dot_nt(jnp.concatenate([two, packed], axis=0), src_ref[:, spans[2 * step + 1]])
        prev_ref[0] += top[:rows] + low[:rows]
        prev_ref[1] += jnp.where(first_half(top[rows:].shape), top[rows:], low[rows:])
    in_a, in_b = group_masks(gid_ref[...], rows)
    picked = jnp.where(in_a, prev_ref[0], 0.0) + jnp.where(in_b, prev_ref[1], 0.0)
    out_ref[...] = jnp.sum(picked.reshape(rows // SUB, SUB, -1), axis=1)


def ctrl_kernel(far, scale, turns, slice_width, tok_hbm, gid_ref, w_ref, *refs):
    mix_refs, (low_ref, out_ref, tok_ref, sems) = refs[:turns], refs[turns:]
    me, member = placed_here()
    experts, count = w_ref.shape
    cols = SUB * experts
    steps = sems.shape[0]
    size = slice_width // steps
    spans = [slice(step * size, (step + 1) * size) for step in range(steps)]
    copies = start_all(
        [
            pltpu.make_async_copy(
                tok_hbm.at[:, pl.ds(pl.multiple_of(member * slice_width + span.start, size), size)],
                tok_ref.at[:, span],
                sems.at[c],
            )
            for c, span in enumerate(spans)
        ]
    )
    mix = mix_refs[0][...]
    for ref in mix_refs[1:]:
        mix = mix + ref[...]
    weights = w_ref[...]
    in_a, in_b = group_masks(gid_ref[...], cols)
    spread = jnp.broadcast_to((weights * mix)[:, None, :], (experts, SUB, count)).reshape(cols, count)
    sum_a = jnp.sum(jnp.where(in_a, spread, 0.0), axis=1, keepdims=True)
    sum_b = jnp.sum(jnp.where(in_b, spread, 0.0), axis=1, keepdims=True)
    in_b = jnp.logical_and(in_b, first_half((cols, count)))
    back = jnp.where(in_a, sum_a, 0.0) + jnp.where(in_b, sum_b, 0.0)
    total = jnp.sum(back.reshape(experts, SUB, count), axis=1)
    low = (weights * (mix - total)).astype(BF16)
    place = rel_of(iota((experts, experts), 1), far) ^ me
    onehot = jnp.where(iota((experts, experts), 0) == place, 1.0, 0.0).astype(BF16)
    low_ref[...] = dot_nn(onehot, low).astype(BF16)
    for step in range(steps):
        copies[step].wait()
        out_ref[:, spans[step]] = (scale * dot_nn(low_ref[...], tok_ref[:, spans[step]])).astype(BF16)


def token_kernel(scale, steps, chunks, idx_ref, left_ref, low_ref, ctrl_ref, *refs):
    in_refs, out_ref = refs[: chunks * NEAR], refs[chunks * NEAR]
    step = pl.program_id(0)
    size = out_ref.shape[1]
    part = in_refs[0].shape[1] // 3
    per = part // size
    side, within = step // steps, lax.rem(step, steps)
    for chunk in range(chunks):

        @pl.when(within // per == chunk)
        def _():
            own = in_refs[chunk * NEAR : (chunk + 1) * NEAR]
            lower = lax.rem(within, per) * size
            base = pl.multiple_of(side * part + lower, 128)
            third = pl.multiple_of(2 * part + lower, 128)
            straight = [ref[:, pl.ds(base, size)] for ref in own]
            packed = [ref[:, pl.ds(third, size)] for ref in own]
            back = dot_tn(left_ref[0], jnp.concatenate(straight + packed, axis=0))
            out_ref[...] = (back + scale * dot_tn(low_ref[...], ctrl_ref[...])).astype(BF16)


def on_device(sizes, tokens, group_slot, controller, expert_in, expert_out, cotangent):
    n_dp, n_narrow = sizes
    count, model_width = tokens.shape
    slice_width = cotangent.shape[1]
    half = slice_width // 2
    experts = controller.shape[1]
    hidden = expert_in.shape[2]
    far = n_dp // NEAR
    splits = 2 if half % 256 == 0 else 1
    cols = SUB * experts
    assert experts == n_dp and count // GSIZE == SUB + HALF and far & (far - 1) == 0
    scale = 1.0 / math.sqrt(model_width)
    me = lax.axis_index("dp").astype(jnp.int32)
    member = lax.axis_index("narrow").astype(jnp.int32)
    at = jnp.stack([member])
    zero = jnp.zeros((1,), jnp.int32)
    ctrl_t = controller.T
    first = expert_in.reshape(n_narrow, 2, half, hidden)
    second = expert_out.reshape(n_narrow, 2, half, hidden)

    def swap(array, bits):
        return lax.ppermute(array, "dp", [(i, i ^ bits) for i in range(n_dp)]) if bits else array

    def shifted(array, shift):
        return lax.ppermute(array, "narrow", [(i, (i + shift) % n_narrow) for i in range(n_narrow)])

    def near_swap(parts):
        return [swap(part, bits) for bits, part in enumerate(parts)]

    def far_swap(parts):
        return [swap(part, NEAR * bits) for bits, part in enumerate(parts)]

    def spread(parts):
        return [parts] + [[shifted(part, shift) for part in parts] for shift in range(1, n_narrow)]

    def homeward(own, others):
        arrived = [shifted(other, shift) for shift, other in enumerate(others, 1)]
        parts = far_swap(sum_parts([own] + arrived, far))
        return near_swap(regroup(parts))

    def pairwise(values):
        values = [value.astype(F32) for value in values]
        while len(values) > 1:
            values = [values[i] + values[i + 1] for i in range(0, len(values), 2)]
        return values[0]

    near_piece = shape_of((SUB * far, 3 * half // splits), BF16)
    far_piece = shape_of((SUB * NEAR, 3 * half // splits), BF16)
    low_shape, w_shape = shape_of((2, cols, count), BF16), shape_of((experts, count), F32)
    gid_shape = shape_of((1, count), jnp.int32)
    outs = [near_piece] * NEAR + [far_piece] * (far * (splits - 1)) + [gid_shape, low_shape, w_shape]
    loads = 8
    *rows_out, gid, low, weights = call(
        functools.partial(head_kernel, far, scale, slice_width),
        (1,),
        [ANY, whole(ctrl_t), whole(gid_shape)],
        [whole(out) for out in outs],
        outs,
        scratch=[
            pltpu.VMEM((count, model_width), BF16),
            pltpu.VMEM((count, cols), F32),
            pltpu.SemaphoreType.DMA((loads,)),
        ],
        scalars=0,
        flops=2 * cols * count * model_width,
        nbytes=2 * count * model_width,
    )(tokens, ctrl_t, group_slot)
    lanes = [spread(far_swap(regroup(near_swap(rows_out[:NEAR]))))]
    if splits > 1:
        lanes.append(spread(near_swap(regroup(far_swap(rows_out[NEAR:])))))
    mixed = [list(pair) for pair in zip(*lanes)]
    size = pick(half, 768)
    packed = shape_of((SUB * far, 3 * half), BF16)
    cot_out = call(
        cot_kernel,
        (1,),
        [ANY, whole(low_shape)],
        [whole(packed)] * NEAR,
        [packed] * NEAR,
        scratch=[pltpu.VMEM((count, slice_width), BF16), pltpu.SemaphoreType.DMA((2 * (half // size),))],
        scalars=0,
        flops=4 * cols * count * slice_width,
        nbytes=2 * count * slice_width,
    )(cotangent, low)
    mixed_cot = [[parts] for parts in spread(far_swap(regroup(near_swap(cot_out))))]

    sends, hidden_act, mixed_all, pre = run_turn(far, None, mixed, (True, False)[:splits], 1, first, second)
    result_own = expand_weights(hidden_act, second, at, 1)
    result = homeward(result_own[0], [one[0] for one in sends])
    sends, act_grad, cot_all, _ = run_turn(far, pre, mixed_cot, (True,), splits, second, first, after=(result_own[0],))
    back_own = expand_weights(act_grad, first, at, splits)
    back = [homeward(back_own[c], [one[c] for one in sends]) for c in range(splits)]
    out_grad = weight_grad(hidden_act, cot_all, second.shape, at, after=(back_own[0],))
    in_grad = weight_grad(act_grad, mixed_all, first.shape, at, after=(out_grad,))

    mix_one = contract_tokens(result, cotangent, zero, after=(in_grad,))
    out_grad, in_grad = out_grad.reshape(expert_out.shape), in_grad.reshape(expert_in.shape)
    size = pick(half // len(back), 768)
    mix = call(
        functools.partial(mix_kernel, len(back), slice_width),
        (1,),
        [ANY, whole(gid), ANY] + [ANY] * (NEAR * len(back)),
        whole(w_shape),
        w_shape,
        scratch=[
            pltpu.VMEM((2, cols, count), F32),
            pltpu.VMEM((count, slice_width), BF16),
            pltpu.VMEM((len(back), cols, back[0][0].shape[1]), BF16),
            pltpu.SemaphoreType.DMA((2 * (half // size),)),
            pltpu.SemaphoreType.DMA((1,)),
            pltpu.SemaphoreType.DMA((NEAR * len(back),)),
        ],
        scalars=0,
        flops=4 * cols * count * slice_width,
        nbytes=2 * count * slice_width + 6 * cols * half,
    )(tokens, gid, mix_one, *[part for chunk in back for part in chunk])
    mixes = [mix] + [shifted(mix, shift) for shift in range(1, n_narrow)]
    steps = slice_width // pick(slice_width, 1024)
    low_grad, ctrl_part = call(
        functools.partial(ctrl_kernel, far, scale, n_narrow, slice_width),
        (1,),
        [ANY, whole(gid), whole(weights)] + [whole(mix)] * n_narrow,
        [whole(shape_of((experts, count), BF16)), whole(shape_of((experts, slice_width), BF16))],
        [shape_of((experts, count), BF16), shape_of((experts, slice_width), BF16)],
        scratch=[pltpu.VMEM((count, slice_width), BF16), pltpu.SemaphoreType.DMA((steps,))],
        scalars=0,
        flops=2 * experts * count * slice_width,
        nbytes=2 * count * slice_width,
    )(tokens, gid, weights, *mixes)
    total = pairwise(near_swap([ctrl_part] * NEAR)).astype(BF16)
    total = pairwise(far_swap([total] * far))
    ctrl_grad = total.T

    size = pick(half // len(back), 768)
    steps = half // size
    side = jnp.where((jnp.arange(cols) & HALF)[:, None] == 0, low[1], jnp.zeros_like(low[1]))
    sides = jnp.stack([jnp.concatenate([low[0], side]), jnp.concatenate([low[0], low[1] - side])])
    token_grad = call(
        functools.partial(token_kernel, scale, steps, len(back)),
        (2 * steps,),
        [
            pl.BlockSpec((1, 2 * cols, count), lambda i, idx: (i // steps, 0, 0)),
            whole(low_grad),
            pl.BlockSpec((experts, size), lambda i, idx: (0, idx[0] * 2 * steps + i)),
        ]
        + [whole(part) for chunk in back for part in chunk],
        pl.BlockSpec((count, size), lambda i, idx: (0, i)),
        shape_of((count, slice_width), BF16),
        flops=4 * cols * count * slice_width,
        nbytes=2 * count * slice_width,
    )(at, sides, low_grad, ctrl_t, *[part for chunk in back for part in chunk])
    return (token_grad, ctrl_grad, in_grad, out_grad)


def solution(mesh):
    sizes = (mesh.shape["dp"], mesh.shape["narrow"])
    placed = (
        P("dp", None),
        P("dp", None),
        P(),
        P("dp", None, "narrow"),
        P("dp", None, "narrow"),
        P("dp", "narrow"),
    )

    def body(*args):
        return on_device(sizes, *args)

    return jax.shard_map(
        body,
        mesh=mesh,
        in_specs=placed,
        out_specs=(
            P("dp", "narrow"),
            P("narrow", None),
            P("dp", None, "narrow"),
            P("dp", None, "narrow"),
        ),
        check_vma=False,
    )
```

```python
import functools
import math

import jax
import jax.numpy as jnp
from jax import lax
from jax.experimental import pallas as pl
from jax.experimental.pallas import tpu as pltpu
from jax.sharding import PartitionSpec as P


GSIZE = 32
SUB = 8
HALF = 4
NEAR = 4
F32 = jnp.float32
BF16 = jnp.bfloat16
VMEM_LIMIT = 32 * 1024 * 1024


def dot_nn(a, b):
    return lax.dot_general(a, b, (((1,), (0,)), ((), ())), preferred_element_type=F32)


def dot_nt(a, b):
    return lax.dot_general(a, b, (((1,), (1,)), ((), ())), preferred_element_type=F32)


def dot_tn(a, b):
    return lax.dot_general(a, b, (((0,), (0,)), ((), ())), preferred_element_type=F32)


def iota(shape, dim):
    return lax.broadcasted_iota(jnp.int32, shape, dim)


def first_half(shape):
    return (iota(shape, 0) & HALF) == 0


def pick(width, most):
    size = most
    while width % size:
        size //= 2
    return size


ANY = pl.BlockSpec(memory_space=pl.ANY)
HBM = pl.BlockSpec(memory_space=pltpu.HBM)


def call(kernel, grid, in_specs, out_specs, out_shape, scratch=(), scalars=1, flops=0, nbytes=0, after=()):
    skip = len(after)

    def body(*refs):
        kernel(*refs[:scalars], *refs[scalars + skip :])

    run = pl.pallas_call(
        body,
        grid_spec=pltpu.PrefetchScalarGridSpec(
            num_scalar_prefetch=scalars,
            grid=grid,
            in_specs=[ANY] * skip + list(in_specs),
            out_specs=out_specs,
            scratch_shapes=list(scratch),
        ),
        out_shape=out_shape,
        compiler_params=pltpu.CompilerParams(
            dimension_semantics=("arbitrary",) * len(grid),
            vmem_limit_bytes=VMEM_LIMIT,
        ),
        cost_estimate=pl.CostEstimate(flops=int(flops), bytes_accessed=int(nbytes), transcendentals=0),
    )
    return lambda *args: run(*args[:scalars], *after, *args[scalars:])


def placed_here():
    return lax.axis_index("dp").astype(jnp.int32), lax.axis_index("narrow").astype(jnp.int32)


def keep(array):
    return pltpu.with_memory_space_constraint(array, pltpu.HBM)


def start_all(copies):
    for copy in copies:
        copy.start()
    return copies


def whole(array):
    rank = len(array.shape)
    return pl.BlockSpec(array.shape, lambda *_: (0,) * rank)


def shape_of(dims, dtype):
    return jax.ShapeDtypeStruct(dims, dtype)


def rel_of(c8, far):
    return (c8 % far) * NEAR + c8 // far if isinstance(c8, int) else (
        (c8 & (far - 1)) * NEAR + lax.shift_right_logical(c8, far.bit_length() - 1)
    )


def group_masks(gid, cols):
    row = iota((cols, gid.shape[1]), 0)
    in_a = gid == (row & (SUB - 1))
    in_b = gid == (SUB + (row & (HALF - 1)))
    return in_a, in_b


def soften(logits, gid, low_ref, w_ref):
    experts = w_ref.shape[0]
    masks = group_masks(gid, logits.shape[0])
    shared = jnp.zeros_like(logits)
    for part, mask in enumerate(masks):
        top = jnp.max(jnp.where(mask, logits, -jnp.inf), axis=1, keepdims=True)
        raised = jnp.where(mask, jnp.exp(jnp.where(mask, logits - top, 0.0)), 0.0)
        weights = raised / jnp.sum(raised, axis=1, keepdims=True)
        low_ref[part] = weights.astype(BF16)
        if part:
            weights = jnp.where(first_half(weights.shape), weights, 0.0)
        shared += weights
    w_ref[...] = jnp.sum(shared.reshape(experts, SUB, -1), axis=1)


def plan(refs, by_far, far):
    if not by_far:
        each = refs[0].shape[0]
        return [(ref, 0, at * each, each) for at, ref in enumerate(refs)]
    return [(ref, SUB * y, SUB * (y * far + k), SUB) for k, ref in enumerate(refs) for y in range(NEAR)]


def expand_into(targets, left, one, two, base, rhs_t):
    rows = left.shape[0] // 2
    dot = dot_nt if rhs_t else dot_nn
    size = one.shape[0] if rhs_t else one.shape[1]
    top, low = dot(left, one), dot(left, two)
    mixed = jnp.where(first_half((rows, size)), top[rows:], low[rows:])
    for ref, to, at, many in targets:
        wide = ref.shape[1] // 3
        for place, value in enumerate((top, low, mixed)):
            ref[to : to + many, pl.ds(place * wide + base, size)] = value[at : at + many].astype(BF16)


def head_kernel(far, scale, slice_width, tok_hbm, ctrl_hbm, slot_hbm, *refs):
    out_refs, (gid_ref, low_ref, w_ref, tok_ref, ctrl_ref, slot_ref, acc_ref, sems, more) = refs[:-9], refs[-9:]
    targets_of = [plan(out_refs[:NEAR], False, far)]
    if out_refs[NEAR:]:
        targets_of.append(plan(out_refs[NEAR:], True, far))
    _, width = tok_ref.shape
    chunks = sems.shape[0]
    size = width // chunks
    spans = [slice(c * size, (c + 1) * size) for c in range(chunks)]
    extra = start_all(
        [
            pltpu.make_async_copy(ctrl_hbm, ctrl_ref, more.at[0]),
            pltpu.make_async_copy(slot_hbm, slot_ref, more.at[1]),
        ]
    )
    copies = start_all(
        [pltpu.make_async_copy(tok_hbm.at[:, span], tok_ref.at[:, span], sems.at[c]) for c, span in enumerate(spans)]
    )
    me, member = placed_here()
    experts = ctrl_ref.shape[0]
    cols = SUB * experts
    c8 = lax.shift_right_logical(iota((experts, cols), 1), 3)
    onehot = jnp.where(iota((experts, cols), 0) == (rel_of(c8, far) ^ me), 1.0, 0.0).astype(BF16)
    for copy in extra:
        copy.wait()
    gid_ref[...] = lax.shift_right_logical(slot_ref[...], GSIZE.bit_length() - 1)
    for c, span in enumerate(spans):
        ctrl = dot_tn(ctrl_ref[:, span], onehot).astype(BF16)
        copies[c].wait()
        part = dot_nn(tok_ref[:, span], ctrl)
        if c:
            acc_ref[...] += part
        else:
            acc_ref[...] = part
    soften(acc_ref[...].T * scale, gid_ref[...], low_ref, w_ref)
    left = jnp.concatenate([low_ref[0], low_ref[1]], axis=0)
    half = slice_width // 2
    part = half // len(targets_of)
    size = pick(part, 768)
    for which, targets in enumerate(targets_of):
        for step in range(part // size):
            start = member * slice_width + which * part + step * size
            one = pl.multiple_of(start, 128)
            two = pl.multiple_of(start + half, 128)
            expand_into(
                targets, left, tok_ref[:, pl.ds(one, size)], tok_ref[:, pl.ds(two, size)], step * size, False
            )


def cot_kernel(src_hbm, low_ref, *refs):
    out_refs, (src_ref, sems) = refs[:NEAR], refs[NEAR:]
    half = src_ref.shape[1] // 2
    steps = sems.shape[0] // 2
    size = half // steps
    spans = [slice(at, at + size) for step in range(steps) for at in (step * size, half + step * size)]
    copies = start_all(
        [pltpu.make_async_copy(src_hbm.at[:, span], src_ref.at[:, span], sems.at[c]) for c, span in enumerate(spans)]
    )
    left = jnp.concatenate([low_ref[0], low_ref[1]], axis=0)
    for step in range(steps):
        copies[2 * step].wait()
        copies[2 * step + 1].wait()
        expand_into(
            plan(out_refs, False, 0),
            left,
            src_ref[:, spans[2 * step]],
            src_ref[:, spans[2 * step + 1]],
            step * size,
            False,
        )


def expand_kernel(per, idx_ref, left_ref, one_ref, two_ref, *out_refs):
    one, two = one_ref[0, 0], two_ref[0, 0]
    size = one.shape[0]
    step = pl.program_id(0)
    for chunk, out_ref in enumerate(out_refs):

        @pl.when(step // per == chunk)
        def _():
            base = pl.multiple_of(lax.rem(step, per) * size, size)
            expand_into(plan([out_ref], False, 0), left_ref[...], one, two, base, True)


def expand_weights(left, weights, at, chunks, after=()):
    _, _, half, hidden = weights.shape
    part = half // chunks
    size = pick(part, 768)
    rows = left.shape[0] // 2
    outs = [shape_of((rows, part * 3), BF16)] * chunks
    return call(
        functools.partial(expand_kernel, part // size),
        (half // size,),
        [
            whole(left),
            pl.BlockSpec((1, 1, size, hidden), lambda i, idx: (idx[0], 0, i, 0)),
            pl.BlockSpec((1, 1, size, hidden), lambda i, idx: (idx[0], 1, i, 0)),
        ],
        [whole(out) for out in outs],
        outs,
        flops=8 * rows * half * hidden,
        nbytes=4 * half * hidden + 6 * rows * half,
        after=after,
    )(at, left, weights, weights)


def rows_of(by_far, far, piece):
    if by_far:
        return [(0, SUB * NEAR * piece, SUB * NEAR)]
    return [(SUB * k, SUB * (NEAR * k + piece), SUB) for k in range(far)]


def turn_kernel(far, n_narrow, orders, sends, forward, w_in, w_out, *refs):
    chunks, others = len(orders), n_narrow - 1
    n_in = 0 if forward else 1
    count = n_narrow * sum(far if by_far else NEAR for by_far in orders)
    ins, parts, refs = refs[:n_in], refs[n_in : n_in + count], refs[n_in + count :]
    out_refs, refs = refs[: others * sends], refs[others * sends :]
    act_ref, all_ref, refs = refs[0], refs[1], refs[2:]
    if forward:
        pre_out, refs = refs[0], refs[1:]
    in_bufs, refs = refs[:n_in], refs[n_in:]
    acc, wa, wb, sem_in, sem_part, sem_a, sem_b = refs
    member = lax.axis_index("narrow").astype(jnp.int32)
    steps = sem_a.shape[1]
    half = wa.shape[2]
    size = half // steps
    small = [pltpu.make_async_copy(src, dst, sem_in.at[i]) for i, (src, dst) in enumerate(zip(ins, in_bufs))]
    at = 0
    moves = 0
    for shift in range(n_narrow):
        for chunk, by_far in enumerate(orders):
            for piece in range(far if by_far else NEAR):
                for src, dst, many in rows_of(by_far, far, piece):
                    small.append(
                        pltpu.make_async_copy(
                            parts[at].at[src : src + many],
                            all_ref.at[shift, chunk, dst : dst + many],
                            sem_part.at[moves],
                        )
                    )
                    moves += 1
                at += 1
    load_a, load_b = [], []
    for shift in range(n_narrow):
        turn = lax.rem(member + n_narrow - shift, n_narrow)
        for step in range(steps):
            span = slice(step * size, (step + 1) * size)
            load_a.append(pltpu.make_async_copy(w_in.at[turn, :, span], wa.at[shift, :, span], sem_a.at[shift, step]))
    for shift in range(1, n_narrow):
        turn = lax.rem(member + shift, n_narrow)
        for step in range(steps):
            span = slice(step * size, (step + 1) * size)
            load_b.append(
                pltpu.make_async_copy(w_out.at[turn, :, span], wb.at[shift - 1, :, span], sem_b.at[shift - 1, step])
            )
    start_all(small)
    start_all(load_a)
    start_all(load_b)
    for copy in small:
        copy.wait()
    rows = acc.shape[1]
    part = half // chunks
    for shift in range(n_narrow):
        for step in range(steps):
            load_a[shift * steps + step].wait()
            base = step * size
            chunk, within = base // part, base % part
            packed = all_ref[shift, chunk, :, 2 * part + within : 2 * part + within + size]
            one = all_ref[shift, chunk, :, within : within + size]
            two = all_ref[shift, chunk, :, part + within : part + within + size]
            top = dot_nn(jnp.concatenate([one, packed], axis=0), wa[shift, 0, base : base + size])
            low = dot_nn(jnp.concatenate([two, packed], axis=0), wa[shift, 1, base : base + size])
            straight = top[:rows] + low[:rows]
            halves = jnp.where(first_half(straight.shape), top[rows:], low[rows:])
            if shift or step:
                acc[0] += straight
                acc[1] += halves
            else:
                acc[0] = straight
                acc[1] = halves
    halves = acc[1]
    other = jnp.where(
        first_half(halves.shape), pltpu.roll(halves, rows - HALF, 0), pltpu.roll(halves, HALF, 0)
    )
    total = jnp.concatenate([acc[0], halves + other], axis=0)
    if forward:
        pre_out[...] = total
        act_ref[...] = (total * jax.nn.sigmoid(total)).astype(BF16)
    else:
        pre = in_bufs[0][...]
        sig = jax.nn.sigmoid(pre)
        act_ref[...] = (total * (sig * (1.0 + pre * (1.0 - sig)))).astype(BF16)
    part = half // sends
    for at in range(others):
        for step in range(steps):
            load_b[at * steps + step].wait()
            base = step * size
            expand_into(
                plan([out_refs[at * sends + base // part]], False, 0),
                act_ref[...],
                wb[at, 0, base : base + size],
                wb[at, 1, base : base + size],
                base % part,
                True,
            )


def run_turn(far, pre, slices, orders, sends, w_in, w_out, after=()):
    n_narrow, _, half, hidden = w_in.shape
    flat = [piece for one in slices for chunk in one for piece in chunk]
    cols = sum(piece.shape[0] for piece in slices[0][0])
    chunks = len(orders)
    size = pick(half // max(chunks, sends), 768)
    steps = half // size
    forward = pre is None
    ins = [] if forward else [pre]
    outs = [shape_of((cols, half // sends * 3), BF16)] * ((n_narrow - 1) * sends)
    outs += [shape_of((2 * cols, hidden), BF16), shape_of((n_narrow, chunks, cols, half // chunks * 3), BF16)]
    if forward:
        outs.append(shape_of((2 * cols, hidden), F32))
    moves = n_narrow * sum(len(rows_of(f, far, p)) for f in orders for p in range(far if f else NEAR))
    got = call(
        functools.partial(turn_kernel, far, n_narrow, orders, sends, forward),
        (1,),
        [HBM] * 2 + [ANY] * (len(ins) + len(flat)),
        [whole(out) for out in outs],
        outs,
        scratch=[pltpu.VMEM(array.shape, F32) for array in ins]
        + [
            pltpu.VMEM((2, cols, hidden), F32),
            pltpu.VMEM((n_narrow, 2, half, hidden), BF16),
            pltpu.VMEM((n_narrow - 1, 2, half, hidden), BF16),
            pltpu.SemaphoreType.DMA((max(len(ins), 1),)),
            pltpu.SemaphoreType.DMA((moves,)),
            pltpu.SemaphoreType.DMA((n_narrow, steps)),
            pltpu.SemaphoreType.DMA((n_narrow - 1, steps)),
        ],
        scalars=0,
        flops=8 * cols * half * hidden * (2 * n_narrow - 1),
        nbytes=(2 * n_narrow - 1) * (4 * half * hidden + 6 * cols * half),
        after=after,
    )(keep(w_in), keep(w_out), *ins, *flat)
    count = (n_narrow - 1) * sends
    out = [list(got[at * sends : (at + 1) * sends]) for at in range(n_narrow - 1)]
    return out, got[count], got[count + 1], got[-1] if forward else None


def grad_kernel(idx_ref, act_ref, one_ref, two_ref, packed_ref, out_ref, held):
    rows = act_ref.shape[0] // 2

    @pl.when(pl.program_id(0) == 0)
    def _():
        act = act_ref[...]
        mask = first_half((rows, act.shape[1]))
        low = act[rows:].astype(F32)
        zero = jnp.zeros_like(low)
        for side in range(2):
            held[side, :rows] = act[:rows]
            held[side, rows:] = (jnp.where(mask, low, zero) if side == 0 else jnp.where(mask, zero, low)).astype(BF16)

    packed = packed_ref[0, 0]
    out_ref[0, 0] = dot_tn(jnp.concatenate([one_ref[0, 0], packed], axis=0), held[0]).astype(BF16)
    out_ref[0, 1] = dot_tn(jnp.concatenate([two_ref[0, 0], packed], axis=0), held[1]).astype(BF16)


def weight_grad(act, gathered, like, at, after=()):
    parts_n, _, half, hidden = like
    _, chunks, rows, _ = gathered.shape
    part = half // chunks
    size = pick(part, 768)
    per, steps = part // size, half // size
    out = shape_of(like, BF16)

    def rows_at(place):
        return pl.BlockSpec(
            (1, 1, rows, size),
            lambda i, idx: (i // steps, lax.rem(i, steps) // per, 0, place * per + lax.rem(i, per)),
        )

    return call(
        grad_kernel,
        (parts_n * steps,),
        [whole(act), rows_at(0), rows_at(1), rows_at(2)],
        pl.BlockSpec(
            (1, 2, size, hidden),
            lambda i, idx: (lax.rem(idx[0] + parts_n - i // steps, parts_n), 0, lax.rem(i, steps), 0),
        ),
        out,
        scratch=[pltpu.VMEM((2, 2 * rows, hidden), BF16)],
        flops=8 * rows * half * parts_n * hidden,
        nbytes=parts_n * (4 * half * hidden + 6 * rows * half),
        after=after,
    )(at, act, gathered, gathered, gathered)


def regroup_kernel(count, *refs):
    ins, outs, sems = refs[:count], refs[count:-1], refs[-1]
    copies = start_all(
        [
            pltpu.make_async_copy(
                src.at[SUB * j : SUB * (j + 1)], dst.at[SUB * i : SUB * (i + 1)], sems.at[i * len(outs) + j]
            )
            for i, src in enumerate(ins)
            for j, dst in enumerate(outs)
        ]
    )
    for copy in copies:
        copy.wait()


def regroup(parts):
    many = parts[0].shape[0] // SUB
    out = shape_of((SUB * len(parts), parts[0].shape[1]), BF16)
    return call(
        functools.partial(regroup_kernel, len(parts)),
        (1,),
        [ANY] * len(parts),
        [whole(out)] * many,
        [out] * many,
        scratch=[pltpu.SemaphoreType.DMA((many * len(parts),))],
        scalars=0,
        nbytes=4 * many * out.shape[0] * out.shape[1],
    )(*parts)


def sum_kernel(count, *refs):
    ins, outs, (buf, sems) = refs[:count], refs[count:-2], refs[-2:]
    each = outs[0].shape[0]
    copies = [
        [
            pltpu.make_async_copy(
                src.at[k * each : (k + 1) * each], buf.at[i, k * each : (k + 1) * each], sems.at[k * count + i]
            )
            for i, src in enumerate(ins)
        ]
        for k in range(len(outs))
    ]
    for some in copies:
        start_all(some)
    for k, out_ref in enumerate(outs):
        for copy in copies[k]:
            copy.wait()
        total = buf[0, k * each : (k + 1) * each].astype(F32)
        for i in range(1, count):
            total = total + buf[i, k * each : (k + 1) * each].astype(F32)
        out_ref[...] = total.astype(BF16)


def sum_parts(arrays, pieces):
    rows, width = arrays[0].shape
    out = shape_of((rows // pieces, width), BF16)
    return call(
        functools.partial(sum_kernel, len(arrays)),
        (1,),
        [ANY] * len(arrays),
        [whole(out)] * pieces,
        [out] * pieces,
        scratch=[
            pltpu.VMEM((len(arrays), rows, width), BF16),
            pltpu.SemaphoreType.DMA((len(arrays) * pieces,)),
        ],
        scalars=0,
        nbytes=2 * (len(arrays) + 1) * rows * width,
    )(*arrays)


def mix_kernel(chunks, sliced, src_hbm, *refs):
    count = chunks * NEAR
    if sliced:
        (gid_ref, prev_hbm), refs = refs[:2], refs[2:]
    parts, (out_ref, acc_ref, src_ref, part_ref, sems, sem_prev, sem_part) = refs[:count], refs[count:]
    half = src_ref.shape[1] // 2
    part = half // chunks
    steps = sems.shape[0] // 2
    size = half // steps
    each = parts[0].shape[0]
    small = [
        pltpu.make_async_copy(
            src, part_ref.at[i // NEAR, (i % NEAR) * each : (i % NEAR + 1) * each], sem_part.at[i]
        )
        for i, src in enumerate(parts)
    ]
    if sliced:
        small.append(pltpu.make_async_copy(prev_hbm, acc_ref, sem_prev.at[0]))
    spans = [slice(at, at + size) for step in range(steps) for at in (step * size, half + step * size)]
    offset = lax.axis_index("narrow").astype(jnp.int32) * (2 * half) if sliced else 0
    copies = [
        pltpu.make_async_copy(
            src_hbm.at[:, pl.ds(pl.multiple_of(offset + span.start, 128), size)] if sliced else src_hbm.at[:, span],
            src_ref.at[:, span],
            sems.at[c],
        )
        for c, span in enumerate(spans)
    ]
    start_all(small)
    start_all(copies)
    for copy in small:
        copy.wait()
    rows = acc_ref.shape[1]
    for step in range(steps):
        copies[2 * step].wait()
        copies[2 * step + 1].wait()
        chunk, base = step * size // part, step * size % part
        packed = part_ref[chunk, :, 2 * part + base : 2 * part + base + size]
        one = part_ref[chunk, :, base : base + size]
        two = part_ref[chunk, :, part + base : part + base + size]
        top = dot_nt(jnp.concatenate([one, packed], axis=0), src_ref[:, spans[2 * step]])
        low = dot_nt(jnp.concatenate([two, packed], axis=0), src_ref[:, spans[2 * step + 1]])
        straight = top[:rows] + low[:rows]
        halves = jnp.where(first_half(straight.shape), top[rows:], low[rows:])
        if sliced or step:
            acc_ref[0] += straight
            acc_ref[1] += halves
        else:
            acc_ref[0] = straight
            acc_ref[1] = halves
    if sliced:
        in_a, in_b = group_masks(gid_ref[...], rows)
        picked = jnp.where(in_a, acc_ref[0], 0.0) + jnp.where(in_b, acc_ref[1], 0.0)
        out_ref[...] = jnp.sum(picked.reshape(rows // SUB, SUB, -1), axis=1)
    else:
        out_ref[...] = acc_ref[...]


def run_mix(source, slice_width, parts, gid=None, prev=None):
    flat = [part for chunk in parts for part in chunk]
    chunks, count = len(parts), source.shape[0]
    cols = sum(part.shape[0] for part in parts[0])
    sliced = prev is not None
    size = pick(slice_width // 2 // chunks, 768)
    out = shape_of((cols // SUB, count) if sliced else (2, cols, count), F32)
    return call(
        functools.partial(mix_kernel, chunks, sliced),
        (1,),
        [HBM] + ([whole(gid), ANY] if sliced else []) + [ANY] * len(flat),
        whole(out),
        out,
        scratch=[
            pltpu.VMEM((2, cols, count), F32),
            pltpu.VMEM((count, slice_width), BF16),
            pltpu.VMEM((chunks, cols, flat[0].shape[1]), BF16),
            pltpu.SemaphoreType.DMA((slice_width // size,)),
            pltpu.SemaphoreType.DMA((1,)),
            pltpu.SemaphoreType.DMA((len(flat),)),
        ],
        scalars=0,
        flops=4 * cols * count * slice_width,
        nbytes=2 * count * slice_width + 3 * cols * slice_width,
    )(keep(source), *([gid, prev] if sliced else []), *flat)


def ctrl_kernel(far, scale, turns, slice_width, tok_hbm, gid_ref, w_ref, *refs):
    mix_refs, (low_ref, out_ref, tok_ref, sems) = refs[:turns], refs[turns:]
    me, member = placed_here()
    experts, count = w_ref.shape
    cols = SUB * experts
    steps = sems.shape[0]
    size = slice_width // steps
    spans = [slice(step * size, (step + 1) * size) for step in range(steps)]
    copies = start_all(
        [
            pltpu.make_async_copy(
                tok_hbm.at[:, pl.ds(pl.multiple_of(member * slice_width + span.start, size), size)],
                tok_ref.at[:, span],
                sems.at[c],
            )
            for c, span in enumerate(spans)
        ]
    )
    mix = mix_refs[0][...]
    for ref in mix_refs[1:]:
        mix = mix + ref[...]
    weights = w_ref[...]
    in_a, in_b = group_masks(gid_ref[...], cols)
    spread = jnp.broadcast_to((weights * mix)[:, None, :], (experts, SUB, count)).reshape(cols, count)
    sum_a = jnp.sum(jnp.where(in_a, spread, 0.0), axis=1, keepdims=True)
    sum_b = jnp.sum(jnp.where(in_b, spread, 0.0), axis=1, keepdims=True)
    in_b = jnp.logical_and(in_b, first_half((cols, count)))
    back = jnp.where(in_a, sum_a, 0.0) + jnp.where(in_b, sum_b, 0.0)
    total = jnp.sum(back.reshape(experts, SUB, count), axis=1)
    low = (weights * (mix - total)).astype(BF16)
    place = rel_of(iota((experts, experts), 1), far) ^ me
    onehot = jnp.where(iota((experts, experts), 0) == place, 1.0, 0.0).astype(BF16)
    low_ref[...] = dot_nn(onehot, low).astype(BF16)
    for step in range(steps):
        copies[step].wait()
        out_ref[:, spans[step]] = (scale * dot_nn(low_ref[...], tok_ref[:, spans[step]])).astype(BF16)


def token_kernel(scale, steps, chunks, idx_ref, left_ref, low_ref, ctrl_ref, *refs):
    in_refs, out_ref = refs[: chunks * NEAR], refs[chunks * NEAR]
    step = pl.program_id(0)
    size = out_ref.shape[1]
    part = in_refs[0].shape[1] // 3
    per = part // size
    side, within = step // steps, lax.rem(step, steps)
    for chunk in range(chunks):

        @pl.when(within // per == chunk)
        def _():
            own = in_refs[chunk * NEAR : (chunk + 1) * NEAR]
            lower = lax.rem(within, per) * size
            base = pl.multiple_of(side * part + lower, 128)
            third = pl.multiple_of(2 * part + lower, 128)
            straight = [ref[:, pl.ds(base, size)] for ref in own]
            packed = [ref[:, pl.ds(third, size)] for ref in own]
            back = dot_tn(left_ref[0], jnp.concatenate(straight + packed, axis=0))
            out_ref[...] = (back + scale * dot_tn(low_ref[...], ctrl_ref[...])).astype(BF16)


def on_device(sizes, tokens, group_slot, controller, expert_in, expert_out, cotangent):
    n_dp, n_narrow = sizes
    count, model_width = tokens.shape
    slice_width = cotangent.shape[1]
    half = slice_width // 2
    experts = controller.shape[1]
    hidden = expert_in.shape[2]
    far = n_dp // NEAR
    splits = 2 if half % 256 == 0 else 1
    cols = SUB * experts
    assert experts == n_dp and count // GSIZE == SUB + HALF and far & (far - 1) == 0
    scale = 1.0 / math.sqrt(model_width)
    me = lax.axis_index("dp").astype(jnp.int32)
    member = lax.axis_index("narrow").astype(jnp.int32)
    at = jnp.stack([member])
    ctrl_t = controller.T
    first = expert_in.reshape(n_narrow, 2, half, hidden)
    second = expert_out.reshape(n_narrow, 2, half, hidden)

    def swap(array, bits):
        return lax.ppermute(array, "dp", [(i, i ^ bits) for i in range(n_dp)]) if bits else array

    def shifted(array, shift):
        return lax.ppermute(array, "narrow", [(i, (i + shift) % n_narrow) for i in range(n_narrow)])

    def near_swap(parts):
        return [swap(part, bits) for bits, part in enumerate(parts)]

    def far_swap(parts):
        return [swap(part, NEAR * bits) for bits, part in enumerate(parts)]

    def spread(parts):
        slices = [parts]
        for shift in range(1, n_narrow):
            moved = []
            for part in parts:
                moved.append(shifted(part, shift))
            slices.append(moved)
        return slices

    def homeward(own, others):
        arrived = [shifted(other, shift) for shift, other in enumerate(others, 1)]
        parts = far_swap(sum_parts([own] + arrived, far))
        return near_swap(regroup(parts))

    def pairwise(values):
        values = [value.astype(F32) for value in values]
        while len(values) > 1:
            values = [values[i] + values[i + 1] for i in range(0, len(values), 2)]
        return values[0]

    near_piece = shape_of((SUB * far, 3 * half // splits), BF16)
    far_piece = shape_of((SUB * NEAR, 3 * half // splits), BF16)
    low_shape, w_shape = shape_of((2, cols, count), BF16), shape_of((experts, count), F32)
    gid_shape = shape_of((1, count), jnp.int32)
    outs = [near_piece] * NEAR + [far_piece] * (far * (splits - 1)) + [gid_shape, low_shape, w_shape]
    loads = 8
    *rows_out, gid, low, weights = call(
        functools.partial(head_kernel, far, scale, slice_width),
        (1,),
        [HBM] * 3,
        [whole(out) for out in outs],
        outs,
        scratch=[
            pltpu.VMEM((count, model_width), BF16),
            pltpu.VMEM((experts, model_width), BF16),
            pltpu.VMEM((1, count), jnp.int32),
            pltpu.VMEM((count, cols), F32),
            pltpu.SemaphoreType.DMA((loads,)),
            pltpu.SemaphoreType.DMA((2,)),
        ],
        scalars=0,
        flops=2 * cols * count * model_width,
        nbytes=2 * count * model_width,
    )(keep(tokens), keep(ctrl_t), keep(group_slot))
    lanes = [spread(far_swap(regroup(near_swap(rows_out[:NEAR]))))]
    if splits > 1:
        lanes.append(spread(near_swap(regroup(far_swap(rows_out[NEAR:])))))
    mixed = [list(pair) for pair in zip(*lanes)]
    size = pick(half, 768)
    packed = shape_of((SUB * far, 3 * half), BF16)
    cot_out = call(
        cot_kernel,
        (1,),
        [HBM, whole(low_shape)],
        [whole(packed)] * NEAR,
        [packed] * NEAR,
        scratch=[pltpu.VMEM((count, slice_width), BF16), pltpu.SemaphoreType.DMA((2 * (half // size),))],
        scalars=0,
        flops=4 * cols * count * slice_width,
        nbytes=2 * count * slice_width,
    )(keep(cotangent), low)
    mixed_cot = [[parts] for parts in spread(far_swap(regroup(near_swap(cot_out))))]

    sends, hidden_act, mixed_all, pre = run_turn(far, None, mixed, (True, False)[:splits], splits, first, second)
    result_own = expand_weights(hidden_act, second, at, splits)
    result = [homeward(result_own[c], [one[c] for one in sends]) for c in range(splits)]
    sends, act_grad, cot_all, _ = run_turn(far, pre, mixed_cot, (True,), splits, second, first)
    back_own = expand_weights(act_grad, first, at, splits)
    back = [homeward(back_own[c], [one[c] for one in sends]) for c in range(splits)]
    out_grad = weight_grad(hidden_act, cot_all, second.shape, at)
    in_grad = weight_grad(act_grad, mixed_all, first.shape, at)

    mix_one = run_mix(cotangent, slice_width, result)
    out_grad, in_grad = out_grad.reshape(expert_out.shape), in_grad.reshape(expert_in.shape)
    mix = run_mix(tokens, slice_width, back, gid, mix_one)
    mixes = [mix] + [shifted(mix, shift) for shift in range(1, n_narrow)]
    steps = slice_width // pick(slice_width, 1024)
    low_grad, ctrl_part = call(
        functools.partial(ctrl_kernel, far, scale, n_narrow, slice_width),
        (1,),
        [HBM, whole(gid), whole(weights)] + [whole(mix)] * n_narrow,
        [whole(shape_of((experts, count), BF16)), whole(shape_of((experts, slice_width), BF16))],
        [shape_of((experts, count), BF16), shape_of((experts, slice_width), BF16)],
        scratch=[pltpu.VMEM((count, slice_width), BF16), pltpu.SemaphoreType.DMA((steps,))],
        scalars=0,
        flops=2 * experts * count * slice_width,
        nbytes=2 * count * slice_width,
    )(keep(tokens), gid, weights, *mixes)
    total = pairwise(near_swap([ctrl_part] * NEAR)).astype(BF16)
    total = pairwise(far_swap([total] * far))
    ctrl_grad = total.T

    size = pick(half // len(back), 768)
    steps = half // size
    side = jnp.where((jnp.arange(cols) & HALF)[:, None] == 0, low[1], jnp.zeros_like(low[1]))
    sides = jnp.stack([jnp.concatenate([low[0], side]), jnp.concatenate([low[0], low[1] - side])])
    token_grad = call(
        functools.partial(token_kernel, scale, steps, len(back)),
        (2 * steps,),
        [
            pl.BlockSpec((1, 2 * cols, count), lambda i, idx: (i // steps, 0, 0)),
            whole(low_grad),
            pl.BlockSpec((experts, size), lambda i, idx: (0, idx[0] * 2 * steps + i)),
        ]
        + [whole(part) for chunk in back for part in chunk],
        pl.BlockSpec((count, size), lambda i, idx: (0, i)),
        shape_of((count, slice_width), BF16),
        flops=4 * cols * count * slice_width,
        nbytes=2 * count * slice_width,
    )(at, sides, low_grad, ctrl_t, *[part for chunk in back for part in chunk])
    return (token_grad, ctrl_grad, in_grad, out_grad)


def solution(mesh):
    sizes = (mesh.shape["dp"], mesh.shape["narrow"])
    placed = (
        P("dp", None),
        P("dp", None),
        P(),
        P("dp", None, "narrow"),
        P("dp", None, "narrow"),
        P("dp", "narrow"),
    )

    def body(*args):
        return on_device(sizes, *args)

    return jax.shard_map(
        body,
        mesh=mesh,
        in_specs=placed,
        out_specs=(
            P("dp", "narrow"),
            P("narrow", None),
            P("dp", None, "narrow"),
            P("dp", None, "narrow"),
        ),
        check_vma=False,
    )
```

```python
import functools
import math

import jax
import jax.numpy as jnp
from jax import lax
from jax.experimental import pallas as pl
from jax.experimental.pallas import tpu as pltpu
from jax.sharding import PartitionSpec as P


GSIZE = 32
SUB = 8
HALF = 4
NEAR = 4
F32 = jnp.float32
BF16 = jnp.bfloat16
VMEM_LIMIT = 20 * 1024 * 1024


def dot_nn(a, b):
    return lax.dot_general(a, b, (((1,), (0,)), ((), ())), preferred_element_type=F32)


def dot_nt(a, b):
    return lax.dot_general(a, b, (((1,), (1,)), ((), ())), preferred_element_type=F32)


def dot_tn(a, b):
    return lax.dot_general(a, b, (((0,), (0,)), ((), ())), preferred_element_type=F32)


def iota(shape, dim):
    return lax.broadcasted_iota(jnp.int32, shape, dim)


def first_half(shape):
    return (iota(shape, 0) & HALF) == 0


def pick(width, most):
    size = most
    while width % size:
        size //= 2
    return size


ANY = pl.BlockSpec(memory_space=pl.ANY)
HBM = pl.BlockSpec(memory_space=pltpu.HBM)


def call(kernel, grid, in_specs, out_specs, out_shape, scratch=(), scalars=1, flops=0, nbytes=0, after=()):
    skip = len(after)

    def body(*refs):
        kernel(*refs[:scalars], *refs[scalars + skip :])

    run = pl.pallas_call(
        body,
        grid_spec=pltpu.PrefetchScalarGridSpec(
            num_scalar_prefetch=scalars,
            grid=grid,
            in_specs=[ANY] * skip + list(in_specs),
            out_specs=out_specs,
            scratch_shapes=list(scratch),
        ),
        out_shape=out_shape,
        compiler_params=pltpu.CompilerParams(
            dimension_semantics=("arbitrary",) * len(grid),
            vmem_limit_bytes=VMEM_LIMIT,
        ),
        cost_estimate=pl.CostEstimate(flops=int(flops), bytes_accessed=int(nbytes), transcendentals=0),
    )
    return lambda *args: run(*args[:scalars], *after, *args[scalars:])


def placed_here():
    return lax.axis_index("dp").astype(jnp.int32), lax.axis_index("narrow").astype(jnp.int32)


def keep(array):
    return pltpu.with_memory_space_constraint(array, pltpu.HBM)


def start_all(copies):
    for copy in copies:
        copy.start()
    return copies


def whole(array):
    rank = len(array.shape)
    return pl.BlockSpec(array.shape, lambda *_: (0,) * rank)


def shape_of(dims, dtype):
    return jax.ShapeDtypeStruct(dims, dtype)


def rel_of(c8, far):
    return (c8 % far) * NEAR + c8 // far if isinstance(c8, int) else (
        (c8 & (far - 1)) * NEAR + lax.shift_right_logical(c8, far.bit_length() - 1)
    )


def group_masks(gid, cols):
    row = iota((cols, gid.shape[1]), 0)
    in_a = gid == (row & (SUB - 1))
    in_b = gid == (SUB + (row & (HALF - 1)))
    return in_a, in_b


def soften(logits, gid, low_ref, w_ref):
    experts = w_ref.shape[0]
    masks = group_masks(gid, logits.shape[0])
    shared = jnp.zeros_like(logits)
    for part, mask in enumerate(masks):
        top = jnp.max(jnp.where(mask, logits, -jnp.inf), axis=1, keepdims=True)
        raised = jnp.where(mask, jnp.exp(jnp.where(mask, logits - top, 0.0)), 0.0)
        weights = raised / jnp.sum(raised, axis=1, keepdims=True)
        low_ref[part] = weights.astype(BF16)
        if part:
            weights = jnp.where(first_half(weights.shape), weights, 0.0)
        shared += weights
    w_ref[...] = jnp.sum(shared.reshape(experts, SUB, -1), axis=1)


def plan(refs, by_far, far):
    if not by_far:
        each = refs[0].shape[0]
        return [(ref, 0, at * each, each) for at, ref in enumerate(refs)]
    return [(ref, SUB * y, SUB * (y * far + k), SUB) for k, ref in enumerate(refs) for y in range(NEAR)]


def expand_into(targets, left, one, two, base, rhs_t):
    rows = left.shape[0] // 2
    dot = dot_nt if rhs_t else dot_nn
    size = one.shape[0] if rhs_t else one.shape[1]
    top, low = dot(left, one), dot(left, two)
    mixed = jnp.where(first_half((rows, size)), top[rows:], low[rows:])
    for ref, to, at, many in targets:
        wide = ref.shape[1] // 3
        for place, value in enumerate((top, low, mixed)):
            ref[to : to + many, pl.ds(place * wide + base, size)] = value[at : at + many].astype(BF16)


def head_kernel(far, scale, slice_width, tok_hbm, ctrl_hbm, slot_hbm, *refs):
    out_refs, (gid_ref, low_ref, w_ref, tok_ref, ctrl_ref, slot_ref, acc_ref, sems, more) = refs[:-9], refs[-9:]
    targets_of = [plan(out_refs[:NEAR], False, far)]
    if out_refs[NEAR:]:
        targets_of.append(plan(out_refs[NEAR:], True, far))
    _, width = tok_ref.shape
    chunks = sems.shape[0]
    size = width // chunks
    spans = [slice(c * size, (c + 1) * size) for c in range(chunks)]
    extra = start_all(
        [
            pltpu.make_async_copy(ctrl_hbm, ctrl_ref, more.at[0]),
            pltpu.make_async_copy(slot_hbm, slot_ref, more.at[1]),
        ]
    )
    copies = start_all(
        [pltpu.make_async_copy(tok_hbm.at[:, span], tok_ref.at[:, span], sems.at[c]) for c, span in enumerate(spans)]
    )
    me, member = placed_here()
    experts = ctrl_ref.shape[0]
    cols = SUB * experts
    c8 = lax.shift_right_logical(iota((experts, cols), 1), 3)
    onehot = jnp.where(iota((experts, cols), 0) == (rel_of(c8, far) ^ me), 1.0, 0.0).astype(BF16)
    for copy in extra:
        copy.wait()
    gid_ref[...] = lax.shift_right_logical(slot_ref[...], GSIZE.bit_length() - 1)
    for c, span in enumerate(spans):
        ctrl = dot_tn(ctrl_ref[:, span], onehot).astype(BF16)
        copies[c].wait()
        part = dot_nn(tok_ref[:, span], ctrl)
        if c:
            acc_ref[...] += part
        else:
            acc_ref[...] = part
    soften(acc_ref[...].T * scale, gid_ref[...], low_ref, w_ref)
    left = jnp.concatenate([low_ref[0], low_ref[1]], axis=0)
    half = slice_width // 2
    part = half // len(targets_of)
    size = pick(part, 768)
    for which, targets in enumerate(targets_of):
        for step in range(part // size):
            start = member * slice_width + which * part + step * size
            one = pl.multiple_of(start, 128)
            two = pl.multiple_of(start + half, 128)
            expand_into(
                targets, left, tok_ref[:, pl.ds(one, size)], tok_ref[:, pl.ds(two, size)], step * size, False
            )


def cot_kernel(src_hbm, low_ref, *refs):
    out_refs, (src_ref, sems) = refs[:NEAR], refs[NEAR:]
    half = src_ref.shape[1] // 2
    steps = sems.shape[0] // 2
    size = half // steps
    spans = [slice(at, at + size) for step in range(steps) for at in (step * size, half + step * size)]
    copies = start_all(
        [pltpu.make_async_copy(src_hbm.at[:, span], src_ref.at[:, span], sems.at[c]) for c, span in enumerate(spans)]
    )
    left = jnp.concatenate([low_ref[0], low_ref[1]], axis=0)
    for step in range(steps):
        copies[2 * step].wait()
        copies[2 * step + 1].wait()
        expand_into(
            plan(out_refs, False, 0),
            left,
            src_ref[:, spans[2 * step]],
            src_ref[:, spans[2 * step + 1]],
            step * size,
            False,
        )


def expand_kernel(per, idx_ref, left_ref, one_ref, two_ref, *out_refs):
    one, two = one_ref[0, 0], two_ref[0, 0]
    size = one.shape[0]
    step = pl.program_id(0)
    for chunk, out_ref in enumerate(out_refs):

        @pl.when(step // per == chunk)
        def _():
            base = pl.multiple_of(lax.rem(step, per) * size, size)
            expand_into(plan([out_ref], False, 0), left_ref[...], one, two, base, True)


def expand_weights(left, weights, at, chunks, after=()):
    _, _, half, hidden = weights.shape
    part = half // chunks
    size = pick(part, 768)
    rows = left.shape[0] // 2
    outs = [shape_of((rows, part * 3), BF16)] * chunks
    return call(
        functools.partial(expand_kernel, part // size),
        (half // size,),
        [
            whole(left),
            pl.BlockSpec((1, 1, size, hidden), lambda i, idx: (idx[0], 0, i, 0)),
            pl.BlockSpec((1, 1, size, hidden), lambda i, idx: (idx[0], 1, i, 0)),
        ],
        [whole(out) for out in outs],
        outs,
        flops=8 * rows * half * hidden,
        nbytes=4 * half * hidden + 6 * rows * half,
        after=after,
    )(at, left, weights, weights)


def rows_of(by_far, far, piece):
    if by_far:
        return [(0, SUB * NEAR * piece, SUB * NEAR)]
    return [(SUB * k, SUB * (NEAR * k + piece), SUB) for k in range(far)]


def turn_kernel(far, n_narrow, orders, sends, forward, w_in, w_out, *refs):
    chunks, others = len(orders), n_narrow - 1
    n_in = 0 if forward else 1
    count = n_narrow * sum(far if by_far else NEAR for by_far in orders)
    ins, parts, refs = refs[:n_in], refs[n_in : n_in + count], refs[n_in + count :]
    out_refs, refs = refs[: others * sends], refs[others * sends :]
    act_ref, all_ref, refs = refs[0], refs[1], refs[2:]
    if forward:
        pre_out, refs = refs[0], refs[1:]
    in_bufs, refs = refs[:n_in], refs[n_in:]
    acc, wa, wb, sem_in, sem_part, sem_a, sem_b = refs
    member = lax.axis_index("narrow").astype(jnp.int32)
    steps = sem_a.shape[1]
    half = wa.shape[2]
    size = half // steps
    small = [pltpu.make_async_copy(src, dst, sem_in.at[i]) for i, (src, dst) in enumerate(zip(ins, in_bufs))]
    at = 0
    moves = 0
    for shift in range(n_narrow):
        for chunk, by_far in enumerate(orders):
            for piece in range(far if by_far else NEAR):
                for src, dst, many in rows_of(by_far, far, piece):
                    small.append(
                        pltpu.make_async_copy(
                            parts[at].at[src : src + many],
                            all_ref.at[shift, chunk, dst : dst + many],
                            sem_part.at[moves],
                        )
                    )
                    moves += 1
                at += 1
    load_a, load_b = [], []
    for shift in range(n_narrow):
        turn = lax.rem(member + n_narrow - shift, n_narrow)
        for step in range(steps):
            span = slice(step * size, (step + 1) * size)
            load_a.append(pltpu.make_async_copy(w_in.at[turn, :, span], wa.at[shift, :, span], sem_a.at[shift, step]))
    for shift in range(1, n_narrow):
        turn = lax.rem(member + shift, n_narrow)
        for step in range(steps):
            span = slice(step * size, (step + 1) * size)
            load_b.append(
                pltpu.make_async_copy(w_out.at[turn, :, span], wb.at[shift - 1, :, span], sem_b.at[shift - 1, step])
            )
    start_all(small)
    start_all(load_a)
    start_all(load_b)
    for copy in small:
        copy.wait()
    rows = acc.shape[1]
    part = half // chunks
    for shift in range(n_narrow):
        for step in range(steps):
            load_a[shift * steps + step].wait()
            base = step * size
            chunk, within = base // part, base % part
            packed = all_ref[shift, chunk, :, 2 * part + within : 2 * part + within + size]
            one = all_ref[shift, chunk, :, within : within + size]
            two = all_ref[shift, chunk, :, part + within : part + within + size]
            top = dot_nn(jnp.concatenate([one, packed], axis=0), wa[shift, 0, base : base + size])
            low = dot_nn(jnp.concatenate([two, packed], axis=0), wa[shift, 1, base : base + size])
            straight = top[:rows] + low[:rows]
            halves = jnp.where(first_half(straight.shape), top[rows:], low[rows:])
            if shift or step:
                acc[0] += straight
                acc[1] += halves
            else:
                acc[0] = straight
                acc[1] = halves
    halves = acc[1]
    other = jnp.where(
        first_half(halves.shape), pltpu.roll(halves, rows - HALF, 0), pltpu.roll(halves, HALF, 0)
    )
    total = jnp.concatenate([acc[0], halves + other], axis=0)
    if forward:
        pre_out[...] = total
        act_ref[...] = (total * jax.nn.sigmoid(total)).astype(BF16)
    else:
        pre = in_bufs[0][...]
        sig = jax.nn.sigmoid(pre)
        act_ref[...] = (total * (sig * (1.0 + pre * (1.0 - sig)))).astype(BF16)
    part = half // sends
    for at in range(others):
        for step in range(steps):
            load_b[at * steps + step].wait()
            base = step * size
            expand_into(
                plan([out_refs[at * sends + base // part]], False, 0),
                act_ref[...],
                wb[at, 0, base : base + size],
                wb[at, 1, base : base + size],
                base % part,
                True,
            )


def run_turn(far, pre, slices, orders, sends, w_in, w_out, after=()):
    n_narrow, _, half, hidden = w_in.shape
    flat = [piece for one in slices for chunk in one for piece in chunk]
    cols = sum(piece.shape[0] for piece in slices[0][0])
    chunks = len(orders)
    size = pick(half // max(chunks, sends), 768)
    steps = half // size
    forward = pre is None
    ins = [] if forward else [pre]
    outs = [shape_of((cols, half // sends * 3), BF16)] * ((n_narrow - 1) * sends)
    outs += [shape_of((2 * cols, hidden), BF16), shape_of((n_narrow, chunks, cols, half // chunks * 3), BF16)]
    if forward:
        outs.append(shape_of((2 * cols, hidden), F32))
    moves = n_narrow * sum(len(rows_of(f, far, p)) for f in orders for p in range(far if f else NEAR))
    got = call(
        functools.partial(turn_kernel, far, n_narrow, orders, sends, forward),
        (1,),
        [HBM] * 2 + [ANY] * (len(ins) + len(flat)),
        [whole(out) for out in outs],
        outs,
        scratch=[pltpu.VMEM(array.shape, F32) for array in ins]
        + [
            pltpu.VMEM((2, cols, hidden), F32),
            pltpu.VMEM((n_narrow, 2, half, hidden), BF16),
            pltpu.VMEM((n_narrow - 1, 2, half, hidden), BF16),
            pltpu.SemaphoreType.DMA((max(len(ins), 1),)),
            pltpu.SemaphoreType.DMA((moves,)),
            pltpu.SemaphoreType.DMA((n_narrow, steps)),
            pltpu.SemaphoreType.DMA((n_narrow - 1, steps)),
        ],
        scalars=0,
        flops=8 * cols * half * hidden * (2 * n_narrow - 1),
        nbytes=(2 * n_narrow - 1) * (4 * half * hidden + 6 * cols * half),
        after=after,
    )(keep(w_in), keep(w_out), *[keep(array) for array in ins], *flat)
    count = (n_narrow - 1) * sends
    out = [list(got[at * sends : (at + 1) * sends]) for at in range(n_narrow - 1)]
    return out, got[count], got[count + 1], got[-1] if forward else None


def grad_kernel(idx_ref, act_ref, one_ref, two_ref, packed_ref, out_ref, held):
    rows = act_ref.shape[0] // 2

    @pl.when(pl.program_id(0) == 0)
    def _():
        act = act_ref[...]
        mask = first_half((rows, act.shape[1]))
        low = act[rows:].astype(F32)
        zero = jnp.zeros_like(low)
        for side in range(2):
            held[side, :rows] = act[:rows]
            held[side, rows:] = (jnp.where(mask, low, zero) if side == 0 else jnp.where(mask, zero, low)).astype(BF16)

    packed = packed_ref[0, 0]
    out_ref[0, 0] = dot_tn(jnp.concatenate([one_ref[0, 0], packed], axis=0), held[0]).astype(BF16)
    out_ref[0, 1] = dot_tn(jnp.concatenate([two_ref[0, 0], packed], axis=0), held[1]).astype(BF16)


def weight_grad(act, gathered, like, at, after=()):
    parts_n, _, half, hidden = like
    _, chunks, rows, _ = gathered.shape
    part = half // chunks
    size = pick(part, 768)
    per, steps = part // size, half // size
    out = shape_of(like, BF16)

    def rows_at(place):
        return pl.BlockSpec(
            (1, 1, rows, size),
            lambda i, idx: (i // steps, lax.rem(i, steps) // per, 0, place * per + lax.rem(i, per)),
        )

    return call(
        grad_kernel,
        (parts_n * steps,),
        [whole(act), rows_at(0), rows_at(1), rows_at(2)],
        pl.BlockSpec(
            (1, 2, size, hidden),
            lambda i, idx: (lax.rem(idx[0] + parts_n - i // steps, parts_n), 0, lax.rem(i, steps), 0),
        ),
        out,
        scratch=[pltpu.VMEM((2, 2 * rows, hidden), BF16)],
        flops=8 * rows * half * parts_n * hidden,
        nbytes=parts_n * (4 * half * hidden + 6 * rows * half),
        after=after,
    )(at, act, gathered, gathered, gathered)


def regroup_kernel(count, *refs):
    ins, outs, sems = refs[:count], refs[count:-1], refs[-1]
    copies = start_all(
        [
            pltpu.make_async_copy(
                src.at[SUB * j : SUB * (j + 1)], dst.at[SUB * i : SUB * (i + 1)], sems.at[i * len(outs) + j]
            )
            for i, src in enumerate(ins)
            for j, dst in enumerate(outs)
        ]
    )
    for copy in copies:
        copy.wait()


def regroup(parts):
    many = parts[0].shape[0] // SUB
    out = shape_of((SUB * len(parts), parts[0].shape[1]), BF16)
    return call(
        functools.partial(regroup_kernel, len(parts)),
        (1,),
        [ANY] * len(parts),
        [whole(out)] * many,
        [out] * many,
        scratch=[pltpu.SemaphoreType.DMA((many * len(parts),))],
        scalars=0,
        nbytes=4 * many * out.shape[0] * out.shape[1],
    )(*parts)


def sum_kernel(count, *refs):
    ins, outs, (buf, sems) = refs[:count], refs[count:-2], refs[-2:]
    each = outs[0].shape[0]
    copies = [
        [
            pltpu.make_async_copy(
                src.at[k * each : (k + 1) * each], buf.at[i, k * each : (k + 1) * each], sems.at[k * count + i]
            )
            for i, src in enumerate(ins)
        ]
        for k in range(len(outs))
    ]
    for some in copies:
        start_all(some)
    for k, out_ref in enumerate(outs):
        for copy in copies[k]:
            copy.wait()
        total = buf[0, k * each : (k + 1) * each].astype(F32)
        for i in range(1, count):
            total = total + buf[i, k * each : (k + 1) * each].astype(F32)
        out_ref[...] = total.astype(BF16)


def sum_parts(arrays, pieces):
    rows, width = arrays[0].shape
    out = shape_of((rows // pieces, width), BF16)
    return call(
        functools.partial(sum_kernel, len(arrays)),
        (1,),
        [ANY] * len(arrays),
        [whole(out)] * pieces,
        [out] * pieces,
        scratch=[
            pltpu.VMEM((len(arrays), rows, width), BF16),
            pltpu.SemaphoreType.DMA((len(arrays) * pieces,)),
        ],
        scalars=0,
        nbytes=2 * (len(arrays) + 1) * rows * width,
    )(*arrays)


def mix_kernel(chunks, total, start, sliced, more, last, src_hbm, *refs):
    count = chunks * NEAR
    if last:
        gid_ref, refs = refs[0], refs[1:]
    if more:
        prev_hbm, refs = refs[0], refs[1:]
    parts, (out_ref, acc_ref, src_ref, part_ref, sems, sem_prev, sem_part) = refs[:count], refs[count:]
    part = src_ref.shape[2] // chunks
    half = part * total
    steps = sems.shape[1]
    size = src_ref.shape[2] // steps
    each = parts[0].shape[0]
    small = [
        pltpu.make_async_copy(
            src, part_ref.at[i // NEAR, (i % NEAR) * each : (i % NEAR + 1) * each], sem_part.at[i]
        )
        for i, src in enumerate(parts)
    ]
    if more:
        small.append(pltpu.make_async_copy(prev_hbm, acc_ref, sem_prev.at[0]))
    offset = lax.axis_index("narrow").astype(jnp.int32) * (2 * half) if sliced else 0
    copies = [
        [
            pltpu.make_async_copy(
                src_hbm.at[:, pl.ds(pl.multiple_of(offset + side * half + start * part + step * size, 128), size)],
                src_ref.at[side, :, step * size : (step + 1) * size],
                sems.at[side, step],
            )
            for side in range(2)
        ]
        for step in range(steps)
    ]
    start_all(small)
    for pair in copies:
        start_all(pair)
    for copy in small:
        copy.wait()
    rows = acc_ref.shape[1]
    for step in range(steps):
        copies[step][0].wait()
        copies[step][1].wait()
        chunk, base = step * size // part, step * size % part
        packed = part_ref[chunk, :, 2 * part + base : 2 * part + base + size]
        one = part_ref[chunk, :, base : base + size]
        two = part_ref[chunk, :, part + base : part + base + size]
        span = slice(step * size, (step + 1) * size)
        top = dot_nt(jnp.concatenate([one, packed], axis=0), src_ref[0, :, span])
        low = dot_nt(jnp.concatenate([two, packed], axis=0), src_ref[1, :, span])
        straight = top[:rows] + low[:rows]
        halves = jnp.where(first_half(straight.shape), top[rows:], low[rows:])
        if more or step:
            acc_ref[0] += straight
            acc_ref[1] += halves
        else:
            acc_ref[0] = straight
            acc_ref[1] = halves
    if last:
        in_a, in_b = group_masks(gid_ref[...], rows)
        picked = jnp.where(in_a, acc_ref[0], 0.0) + jnp.where(in_b, acc_ref[1], 0.0)
        out_ref[...] = jnp.sum(picked.reshape(rows // SUB, SUB, -1), axis=1)
    else:
        out_ref[...] = acc_ref[...]


def run_mix(source, slice_width, parts, total, start, sliced, gid=None, prev=None):
    flat = [part for chunk in parts for part in chunk]
    chunks, count = len(parts), source.shape[0]
    cols = sum(part.shape[0] for part in parts[0])
    more, last = prev is not None, gid is not None
    part = slice_width // 2 // total
    size = pick(part, 768)
    out = shape_of((cols // SUB, count) if last else (2, cols, count), F32)
    return call(
        functools.partial(mix_kernel, chunks, total, start, sliced, more, last),
        (1,),
        [HBM] + ([whole(gid)] if last else []) + [ANY] * (more + len(flat)),
        whole(out),
        out,
        scratch=[
            pltpu.VMEM((2, cols, count), F32),
            pltpu.VMEM((2, count, part * chunks), BF16),
            pltpu.VMEM((chunks, cols, flat[0].shape[1]), BF16),
            pltpu.SemaphoreType.DMA((2, part * chunks // size)),
            pltpu.SemaphoreType.DMA((1,)),
            pltpu.SemaphoreType.DMA((len(flat),)),
        ],
        scalars=0,
        flops=8 * cols * count * part * chunks,
        nbytes=4 * count * part * chunks + 6 * cols * part * chunks,
    )(keep(source), *([gid] if last else []), *([prev] if more else []), *flat)


def ctrl_kernel(far, scale, turns, slice_width, tok_hbm, gid_ref, w_ref, *refs):
    mix_refs, (low_ref, keep_ref, send_ref, tok_ref, sems) = refs[:turns], refs[turns:]
    me, member = placed_here()
    experts, count = w_ref.shape
    cols = SUB * experts
    steps = sems.shape[0]
    size = slice_width // steps
    spans = [slice(step * size, (step + 1) * size) for step in range(steps)]
    copies = start_all(
        [
            pltpu.make_async_copy(
                tok_hbm.at[:, pl.ds(pl.multiple_of(member * slice_width + span.start, size), size)],
                tok_ref.at[:, span],
                sems.at[c],
            )
            for c, span in enumerate(spans)
        ]
    )
    mix = mix_refs[0][...]
    for ref in mix_refs[1:]:
        mix = mix + ref[...]
    weights = w_ref[...]
    in_a, in_b = group_masks(gid_ref[...], cols)
    spread = jnp.broadcast_to((weights * mix)[:, None, :], (experts, SUB, count)).reshape(cols, count)
    sum_a = jnp.sum(jnp.where(in_a, spread, 0.0), axis=1, keepdims=True)
    sum_b = jnp.sum(jnp.where(in_b, spread, 0.0), axis=1, keepdims=True)
    in_b = jnp.logical_and(in_b, first_half((cols, count)))
    back = jnp.where(in_a, sum_a, 0.0) + jnp.where(in_b, sum_b, 0.0)
    total = jnp.sum(back.reshape(experts, SUB, count), axis=1)
    low = (weights * (mix - total)).astype(BF16)
    place = rel_of(iota((experts, experts), 1), far) ^ me
    row = iota((experts, experts), 0)
    onehot = jnp.where(row == place, 1.0, 0.0).astype(BF16)
    low_ref[...] = dot_nn(onehot, low).astype(BF16)
    few = experts // 2
    turned = jnp.where(row == (place ^ ((me & 1) * few)), 1.0, 0.0).astype(BF16)
    ordered = dot_nn(turned, low).astype(BF16)
    for step in range(steps):
        copies[step].wait()
        part = scale * dot_nn(ordered, tok_ref[:, spans[step]])
        keep_ref[:, spans[step]] = part[:few].astype(BF16)
        send_ref[:, spans[step]] = part[few:].astype(BF16)


def token_kernel(scale, steps, chunks, idx_ref, left_ref, low_ref, ctrl_ref, *refs):
    in_refs, out_ref = refs[: chunks * NEAR], refs[chunks * NEAR]
    step = pl.program_id(0)
    size = out_ref.shape[1]
    part = in_refs[0].shape[1] // 3
    per = part // size
    side, within = step // steps, lax.rem(step, steps)
    for chunk in range(chunks):

        @pl.when(within // per == chunk)
        def _():
            own = in_refs[chunk * NEAR : (chunk + 1) * NEAR]
            lower = lax.rem(within, per) * size
            base = pl.multiple_of(side * part + lower, 128)
            third = pl.multiple_of(2 * part + lower, 128)
            straight = [ref[:, pl.ds(base, size)] for ref in own]
            packed = [ref[:, pl.ds(third, size)] for ref in own]
            back = dot_tn(left_ref[0], jnp.concatenate(straight + packed, axis=0))
            out_ref[...] = (back + scale * dot_tn(low_ref[...], ctrl_ref[...])).astype(BF16)


def on_device(sizes, tokens, group_slot, controller, expert_in, expert_out, cotangent):
    n_dp, n_narrow = sizes
    count, model_width = tokens.shape
    slice_width = cotangent.shape[1]
    half = slice_width // 2
    experts = controller.shape[1]
    hidden = expert_in.shape[2]
    far = n_dp // NEAR
    splits = 2 if half % 256 == 0 else 1
    cols = SUB * experts
    assert experts == n_dp and count // GSIZE == SUB + HALF and far & (far - 1) == 0
    scale = 1.0 / math.sqrt(model_width)
    me = lax.axis_index("dp").astype(jnp.int32)
    member = lax.axis_index("narrow").astype(jnp.int32)
    at = jnp.stack([member])
    ctrl_t = controller.T
    first = expert_in.reshape(n_narrow, 2, half, hidden)
    second = expert_out.reshape(n_narrow, 2, half, hidden)

    def swap(array, bits):
        return lax.ppermute(array, "dp", [(i, i ^ bits) for i in range(n_dp)]) if bits else array

    def shifted(array, shift):
        return lax.ppermute(array, "narrow", [(i, (i + shift) % n_narrow) for i in range(n_narrow)])

    def near_swap(parts):
        return [swap(part, bits) for bits, part in enumerate(parts)]

    def far_swap(parts):
        return [swap(part, NEAR * bits) for bits, part in enumerate(parts)]

    def spread(parts):
        slices = [parts]
        for shift in range(1, n_narrow):
            moved = []
            for part in parts:
                moved.append(shifted(part, shift))
            slices.append(moved)
        return slices

    def homeward(own, others):
        arrived = [shifted(other, shift) for shift, other in enumerate(others, 1)]
        parts = far_swap(sum_parts([own] + arrived, far))
        return near_swap(regroup(parts))

    def pairwise(values):
        values = [value.astype(F32) for value in values]
        while len(values) > 1:
            values = [values[i] + values[i + 1] for i in range(0, len(values), 2)]
        return values[0]

    near_piece = shape_of((SUB * far, 3 * half // splits), BF16)
    far_piece = shape_of((SUB * NEAR, 3 * half // splits), BF16)
    low_shape, w_shape = shape_of((2, cols, count), BF16), shape_of((experts, count), F32)
    gid_shape = shape_of((1, count), jnp.int32)
    outs = [near_piece] * NEAR + [far_piece] * (far * (splits - 1)) + [gid_shape, low_shape, w_shape]
    loads = 8
    *rows_out, gid, low, weights = call(
        functools.partial(head_kernel, far, scale, slice_width),
        (1,),
        [HBM] * 3,
        [whole(out) for out in outs],
        outs,
        scratch=[
            pltpu.VMEM((count, model_width), BF16),
            pltpu.VMEM((experts, model_width), BF16),
            pltpu.VMEM((1, count), jnp.int32),
            pltpu.VMEM((count, cols), F32),
            pltpu.SemaphoreType.DMA((loads,)),
            pltpu.SemaphoreType.DMA((2,)),
        ],
        scalars=0,
        flops=2 * cols * count * model_width,
        nbytes=2 * count * model_width,
    )(keep(tokens), keep(ctrl_t), keep(group_slot))
    lanes = [spread(far_swap(regroup(near_swap(rows_out[:NEAR]))))]
    if splits > 1:
        lanes.append(spread(near_swap(regroup(far_swap(rows_out[NEAR:])))))
    mixed = [list(pair) for pair in zip(*lanes)]
    size = pick(half, 768)
    packed = shape_of((SUB * far, 3 * half), BF16)
    cot_out = call(
        cot_kernel,
        (1,),
        [HBM, whole(low_shape)],
        [whole(packed)] * NEAR,
        [packed] * NEAR,
        scratch=[pltpu.VMEM((count, slice_width), BF16), pltpu.SemaphoreType.DMA((2 * (half // size),))],
        scalars=0,
        flops=4 * cols * count * slice_width,
        nbytes=2 * count * slice_width,
    )(keep(cotangent), low)
    mixed_cot = [[parts] for parts in spread(far_swap(regroup(near_swap(cot_out))))]

    sends, hidden_act, mixed_all, pre = run_turn(far, None, mixed, (True, False)[:splits], splits, first, second)
    result_own = expand_weights(hidden_act, second, at, splits)
    result = [homeward(result_own[c], [one[c] for one in sends]) for c in range(splits)]
    sends, act_grad, cot_all, _ = run_turn(far, pre, mixed_cot, (True,), splits, second, first)
    back_own = expand_weights(act_grad, first, at, splits)
    back = [homeward(back_own[c], [one[c] for one in sends]) for c in range(splits)]
    out_grad = weight_grad(hidden_act, cot_all, second.shape, at)
    in_grad = weight_grad(act_grad, mixed_all, first.shape, at)

    mix_part = run_mix(cotangent, slice_width, result, splits, 0, False)
    for c in range(splits - 1):
        mix_part = run_mix(tokens, slice_width, back[c : c + 1], splits, c, True, None, mix_part)
    out_grad, in_grad = out_grad.reshape(expert_out.shape), in_grad.reshape(expert_in.shape)
    mix = run_mix(tokens, slice_width, back[-1:], splits, splits - 1, True, gid, mix_part)
    mixes = [mix] + [shifted(mix, shift) for shift in range(1, n_narrow)]
    steps = slice_width // pick(slice_width, 1024)
    few = shape_of((experts // 2, slice_width), BF16)
    low_grad, ctrl_keep, ctrl_send = call(
        functools.partial(ctrl_kernel, far, scale, n_narrow, slice_width),
        (1,),
        [HBM, whole(gid), whole(weights)] + [whole(mix)] * n_narrow,
        [whole(shape_of((experts, count), BF16)), whole(few), whole(few)],
        [shape_of((experts, count), BF16), few, few],
        scratch=[pltpu.VMEM((count, slice_width), BF16), pltpu.SemaphoreType.DMA((steps,))],
        scalars=0,
        flops=2 * experts * count * slice_width,
        nbytes=2 * count * slice_width,
    )(keep(tokens), gid, weights, *mixes)
    total = pairwise([ctrl_keep, swap(ctrl_send, 1)]).astype(BF16)
    total = pairwise([total, swap(total, 2)]).astype(BF16)
    total = pairwise(far_swap([total] * far))
    other = swap(total, 1)
    lower = (me & 1) == 0
    total = jnp.concatenate([jnp.where(lower, total, other), jnp.where(lower, other, total)], axis=0)
    ctrl_grad = total.T

    size = pick(half // len(back), 768)
    steps = half // size
    side = jnp.where((jnp.arange(cols) & HALF)[:, None] == 0, low[1], jnp.zeros_like(low[1]))
    sides = jnp.stack([jnp.concatenate([low[0], side]), jnp.concatenate([low[0], low[1] - side])])
    token_grad = call(
        functools.partial(token_kernel, scale, steps, len(back)),
        (2 * steps,),
        [
            pl.BlockSpec((1, 2 * cols, count), lambda i, idx: (i // steps, 0, 0)),
            whole(low_grad),
            pl.BlockSpec((experts, size), lambda i, idx: (0, idx[0] * 2 * steps + i)),
        ]
        + [whole(part) for chunk in back for part in chunk],
        pl.BlockSpec((count, size), lambda i, idx: (0, i)),
        shape_of((count, slice_width), BF16),
        flops=4 * cols * count * slice_width,
        nbytes=2 * count * slice_width,
    )(at, sides, low_grad, ctrl_t, *[part for chunk in back for part in chunk])
    return (token_grad, ctrl_grad, in_grad, out_grad)


def solution(mesh):
    sizes = (mesh.shape["dp"], mesh.shape["narrow"])
    placed = (
        P("dp", None),
        P("dp", None),
        P(),
        P("dp", None, "narrow"),
        P("dp", None, "narrow"),
        P("dp", "narrow"),
    )

    def body(*args):
        return on_device(sizes, *args)

    return jax.shard_map(
        body,
        mesh=mesh,
        in_specs=placed,
        out_specs=(
            P("dp", "narrow"),
            P("narrow", None),
            P("dp", None, "narrow"),
            P("dp", None, "narrow"),
        ),
        check_vma=False,
    )
```

```python
import functools
import math

import jax
import jax.numpy as jnp
from jax import lax
from jax.experimental import pallas as pl
from jax.experimental.pallas import tpu as pltpu
from jax.sharding import PartitionSpec as P


GSIZE = 32
SUB = 8
HALF = 4
NEAR = 4
F32 = jnp.float32
BF16 = jnp.bfloat16
VMEM_LIMIT = 20 * 1024 * 1024


def dot_nn(a, b):
    return lax.dot_general(a, b, (((1,), (0,)), ((), ())), preferred_element_type=F32)


def dot_nt(a, b):
    return lax.dot_general(a, b, (((1,), (1,)), ((), ())), preferred_element_type=F32)


def dot_tn(a, b):
    return lax.dot_general(a, b, (((0,), (0,)), ((), ())), preferred_element_type=F32)


def iota(shape, dim):
    return lax.broadcasted_iota(jnp.int32, shape, dim)


def first_half(shape):
    return (iota(shape, 0) & HALF) == 0


def pick(width, most):
    size = most
    while width % size:
        size //= 2
    return size


ANY = pl.BlockSpec(memory_space=pl.ANY)
HBM = pl.BlockSpec(memory_space=pltpu.HBM)


def call(kernel, grid, in_specs, out_specs, out_shape, scratch=(), scalars=1, flops=0, nbytes=0, after=()):
    skip = len(after)

    def body(*refs):
        kernel(*refs[:scalars], *refs[scalars + skip :])

    run = pl.pallas_call(
        body,
        grid_spec=pltpu.PrefetchScalarGridSpec(
            num_scalar_prefetch=scalars,
            grid=grid,
            in_specs=[ANY] * skip + list(in_specs),
            out_specs=out_specs,
            scratch_shapes=list(scratch),
        ),
        out_shape=out_shape,
        compiler_params=pltpu.CompilerParams(
            dimension_semantics=("arbitrary",) * len(grid),
            vmem_limit_bytes=VMEM_LIMIT,
        ),
        cost_estimate=pl.CostEstimate(flops=int(flops), bytes_accessed=int(nbytes), transcendentals=0),
    )
    return lambda *args: run(*args[:scalars], *after, *args[scalars:])


def placed_here():
    return lax.axis_index("dp").astype(jnp.int32), lax.axis_index("narrow").astype(jnp.int32)


def keep(array):
    return pltpu.with_memory_space_constraint(array, pltpu.HBM)


def start_all(copies):
    for copy in copies:
        copy.start()
    return copies


def whole(array):
    rank = len(array.shape)
    return pl.BlockSpec(array.shape, lambda *_: (0,) * rank)


def shape_of(dims, dtype):
    return jax.ShapeDtypeStruct(dims, dtype)


def rel_of(c8, far):
    return (c8 % far) * NEAR + c8 // far if isinstance(c8, int) else (
        (c8 & (far - 1)) * NEAR + lax.shift_right_logical(c8, far.bit_length() - 1)
    )


def group_masks(gid, cols):
    row = iota((cols, gid.shape[1]), 0)
    in_a = gid == (row & (SUB - 1))
    in_b = gid == (SUB + (row & (HALF - 1)))
    return in_a, in_b


def soften(logits, gid, low_ref, w_ref):
    experts = w_ref.shape[0]
    masks = group_masks(gid, logits.shape[0])
    shared = jnp.zeros_like(logits)
    for part, mask in enumerate(masks):
        top = jnp.max(jnp.where(mask, logits, -jnp.inf), axis=1, keepdims=True)
        raised = jnp.where(mask, jnp.exp(jnp.where(mask, logits - top, 0.0)), 0.0)
        weights = raised / jnp.sum(raised, axis=1, keepdims=True)
        low_ref[part] = weights.astype(BF16)
        if part:
            weights = jnp.where(first_half(weights.shape), weights, 0.0)
        shared += weights
    w_ref[...] = jnp.sum(shared.reshape(experts, SUB, -1), axis=1)


def plan(refs, by_far, far):
    if not by_far:
        each = refs[0].shape[0]
        return [(ref, 0, at * each, each) for at, ref in enumerate(refs)]
    return [(ref, SUB * y, SUB * (y * far + k), SUB) for k, ref in enumerate(refs) for y in range(NEAR)]


def expand_into(targets, left, one, two, base, rhs_t):
    rows = left.shape[0] // 2
    dot = dot_nt if rhs_t else dot_nn
    size = one.shape[0] if rhs_t else one.shape[1]
    top, low = dot(left, one), dot(left, two)
    mixed = jnp.where(first_half((rows, size)), top[rows:], low[rows:])
    for ref, to, at, many in targets:
        wide = ref.shape[1] // 3
        for place, value in enumerate((top, low, mixed)):
            ref[to : to + many, pl.ds(place * wide + base, size)] = value[at : at + many].astype(BF16)


def head_kernel(far, scale, slice_width, tok_hbm, ctrl_hbm, slot_hbm, *refs):
    out_refs, (gid_ref, low_ref, w_ref, tok_ref, ctrl_ref, slot_ref, acc_ref, sems, more) = refs[:-9], refs[-9:]
    targets_of = [plan(out_refs[:NEAR], False, far)]
    if out_refs[NEAR:]:
        targets_of.append(plan(out_refs[NEAR:], True, far))
    _, width = tok_ref.shape
    chunks = sems.shape[0]
    size = width // chunks
    spans = [slice(c * size, (c + 1) * size) for c in range(chunks)]
    extra = start_all(
        [
            pltpu.make_async_copy(ctrl_hbm, ctrl_ref, more.at[0]),
            pltpu.make_async_copy(slot_hbm, slot_ref, more.at[1]),
        ]
    )
    copies = start_all(
        [pltpu.make_async_copy(tok_hbm.at[:, span], tok_ref.at[:, span], sems.at[c]) for c, span in enumerate(spans)]
    )
    me, member = placed_here()
    experts = ctrl_ref.shape[0]
    cols = SUB * experts
    c8 = lax.shift_right_logical(iota((cols, experts), 0), 3)
    onehot = jnp.where(iota((cols, experts), 1) == (rel_of(c8, far) ^ me), 1.0, 0.0)
    for copy in extra:
        copy.wait()
    gid_ref[...] = lax.shift_right_logical(slot_ref[...], GSIZE.bit_length() - 1)
    for c, span in enumerate(spans):
        copies[c].wait()
        part = dot_nt(tok_ref[:, span], ctrl_ref[:, span])
        if c:
            acc_ref[...] += part
        else:
            acc_ref[...] = part
    logits = lax.dot_general(
        onehot,
        acc_ref[...].T * scale,
        (((1,), (0,)), ((), ())),
        precision=lax.Precision.HIGHEST,
        preferred_element_type=F32,
    )
    soften(logits, gid_ref[...], low_ref, w_ref)
    left = jnp.concatenate([low_ref[0], low_ref[1]], axis=0)
    half = slice_width // 2
    part = half // len(targets_of)
    size = pick(part, 768)
    for which, targets in enumerate(targets_of):
        for step in range(part // size):
            start = member * slice_width + which * part + step * size
            one = pl.multiple_of(start, 128)
            two = pl.multiple_of(start + half, 128)
            expand_into(
                targets, left, tok_ref[:, pl.ds(one, size)], tok_ref[:, pl.ds(two, size)], step * size, False
            )


def cot_kernel(src_hbm, low_ref, *refs):
    out_refs, (src_ref, sems) = refs[:NEAR], refs[NEAR:]
    half = src_ref.shape[1] // 2
    steps = sems.shape[0] // 2
    size = half // steps
    spans = [slice(at, at + size) for step in range(steps) for at in (step * size, half + step * size)]
    copies = start_all(
        [pltpu.make_async_copy(src_hbm.at[:, span], src_ref.at[:, span], sems.at[c]) for c, span in enumerate(spans)]
    )
    left = jnp.concatenate([low_ref[0], low_ref[1]], axis=0)
    for step in range(steps):
        copies[2 * step].wait()
        copies[2 * step + 1].wait()
        expand_into(
            plan(out_refs, False, 0),
            left,
            src_ref[:, spans[2 * step]],
            src_ref[:, spans[2 * step + 1]],
            step * size,
            False,
        )


def expand_kernel(per, idx_ref, left_ref, one_ref, two_ref, *out_refs):
    one, two = one_ref[0, 0], two_ref[0, 0]
    size = one.shape[0]
    step = pl.program_id(0)
    for chunk, out_ref in enumerate(out_refs):

        @pl.when(step // per == chunk)
        def _():
            base = pl.multiple_of(lax.rem(step, per) * size, size)
            expand_into(plan([out_ref], False, 0), left_ref[...], one, two, base, True)


def expand_weights(left, weights, at, chunks, stay=False):
    _, _, half, hidden = weights.shape
    part = half // chunks
    size = pick(part, 768)
    rows = left.shape[0] // 2
    outs = [shape_of((rows, part * 3), BF16)] * chunks
    return call(
        functools.partial(expand_kernel, part // size),
        (half // size,),
        [
            whole(left),
            pl.BlockSpec((1, 1, size, hidden), lambda i, idx: (idx[0], 0, i, 0)),
            pl.BlockSpec((1, 1, size, hidden), lambda i, idx: (idx[0], 1, i, 0)),
        ],
        [whole(out) for out in outs],
        outs,
        flops=8 * rows * half * hidden,
        nbytes=4 * half * hidden + 6 * rows * half,
    )(at, left, *[keep(weights) if stay else weights] * 2)


def rows_of(by_far, far, piece):
    if by_far:
        return [(0, SUB * NEAR * piece, SUB * NEAR)]
    return [(SUB * k, SUB * (NEAR * k + piece), SUB) for k in range(far)]


def gather(parts, orders, far, shifts, dst_ref, sems):
    copies, at = [], 0
    for shift in range(shifts):
        for chunk, by_far in enumerate(orders):
            for piece in range(far if by_far else NEAR):
                for src, dst, many in rows_of(by_far, far, piece):
                    copies.append(
                        pltpu.make_async_copy(
                            parts[at].at[src : src + many],
                            dst_ref.at[shift, chunk, dst : dst + many],
                            sems.at[len(copies)],
                        )
                    )
                at += 1
    return copies


def moves_of(orders, far):
    return sum(len(rows_of(by_far, far, piece)) for by_far in orders for piece in range(far if by_far else NEAR))


def load_slice(w_hbm, turn, buf_ref, at, sems, size):
    return [
        pltpu.make_async_copy(
            w_hbm.at[turn, :, step * size : (step + 1) * size],
            buf_ref.at[at, :, step * size : (step + 1) * size],
            sems.at[at, step],
        )
        for step in range(sems.shape[1])
    ]


def contract_slice(rows_ref, shift, w_ref, at, loads, acc, fresh):
    _, chunks, rows, width = rows_ref.shape
    part = width // 3
    size = part * chunks // len(loads)
    for step, load in enumerate(loads):
        load.wait()
        base = step * size
        chunk, within = base // part, base % part
        packed = rows_ref[shift, chunk, :, 2 * part + within : 2 * part + within + size]
        one = rows_ref[shift, chunk, :, within : within + size]
        two = rows_ref[shift, chunk, :, part + within : part + within + size]
        top = dot_nn(jnp.concatenate([one, packed], axis=0), w_ref[at, 0, base : base + size])
        low = dot_nn(jnp.concatenate([two, packed], axis=0), w_ref[at, 1, base : base + size])
        straight = top[:rows] + low[:rows]
        halves = jnp.where(first_half(straight.shape), top[rows:], low[rows:])
        if fresh and not step:
            acc[0] = straight
            acc[1] = halves
        else:
            acc[0] += straight
            acc[1] += halves


def own_kernel(far, orders, w_hbm, *refs):
    parts, (out_ref, rows_ref, w_ref, sem_part, sem_w) = refs[:-5], refs[-5:]
    member = lax.axis_index("narrow").astype(jnp.int32)
    copies = start_all(gather(parts, orders, far, 1, rows_ref, sem_part))
    loads = start_all(load_slice(w_hbm, member, w_ref, 0, sem_w, w_ref.shape[2] // sem_w.shape[1]))
    for copy in copies:
        copy.wait()
    contract_slice(rows_ref, 0, w_ref, 0, loads, out_ref, True)


def contract_own(far, chunks, orders, weights):
    _, _, half, hidden = weights.shape
    flat = [piece for chunk in chunks for piece in chunk]
    cols = sum(piece.shape[0] for piece in chunks[0])
    size = pick(half // len(orders), 768)
    out = shape_of((2, cols, hidden), F32)
    return call(
        functools.partial(own_kernel, far, orders),
        (1,),
        [HBM] + [ANY] * len(flat),
        whole(out),
        out,
        scratch=[
            pltpu.VMEM((1, len(orders), cols, half // len(orders) * 3), BF16),
            pltpu.VMEM((1, 2, half, hidden), BF16),
            pltpu.SemaphoreType.DMA((moves_of(orders, far),)),
            pltpu.SemaphoreType.DMA((1, half // size)),
        ],
        scalars=0,
        flops=8 * cols * half * hidden,
        nbytes=4 * half * hidden + 6 * cols * half,
    )(keep(weights), *flat)


def turn_kernel(far, n_narrow, orders, sends, forward, w_in, w_out, *refs):
    others = n_narrow - 1
    n_in = 1 if forward else 2
    count = n_narrow * sum(far if by_far else NEAR for by_far in orders)
    ins, parts, refs = refs[:n_in], refs[n_in : n_in + count], refs[n_in + count :]
    out_refs, refs = refs[: others * sends], refs[others * sends :]
    act_ref, all_ref, refs = refs[0], refs[1], refs[2:]
    if forward:
        pre_out, refs = refs[0], refs[1:]
    in_bufs, refs = refs[:n_in], refs[n_in:]
    wa, wb, sem_in, sem_part, sem_a, sem_b = refs
    acc = in_bufs[0]
    member = lax.axis_index("narrow").astype(jnp.int32)
    steps = sem_a.shape[1]
    half = wa.shape[2]
    size = half // steps
    small = [pltpu.make_async_copy(src, dst, sem_in.at[i]) for i, (src, dst) in enumerate(zip(ins, in_bufs))]
    gathered = gather(parts, orders, far, n_narrow, all_ref, sem_part)
    per = len(gathered) // n_narrow
    load_a, load_b = [], []
    for at in range(others):
        load_a.append(load_slice(w_in, lax.rem(member + others - at, n_narrow), wa, at, sem_a, size))
        load_b.append(load_slice(w_out, lax.rem(member + at + 1, n_narrow), wb, at, sem_b, size))
    start_all(gathered[per:])
    start_all(small)
    for loads in load_a + load_b:
        start_all(loads)
    start_all(gathered[:per])
    for copy in gathered[per:] + small:
        copy.wait()
    rows = acc.shape[1]
    for at in range(others):
        contract_slice(all_ref, at + 1, wa, at, load_a[at], acc, False)
    halves = acc[1]
    other = jnp.where(
        first_half(halves.shape), pltpu.roll(halves, rows - HALF, 0), pltpu.roll(halves, HALF, 0)
    )
    total = jnp.concatenate([acc[0], halves + other], axis=0)
    if forward:
        pre_out[...] = total
        act_ref[...] = (total * jax.nn.sigmoid(total)).astype(BF16)
    else:
        pre = in_bufs[1][...]
        sig = jax.nn.sigmoid(pre)
        act_ref[...] = (total * (sig * (1.0 + pre * (1.0 - sig)))).astype(BF16)
    part = half // sends
    for at in range(others):
        for step in range(steps):
            load_b[at][step].wait()
            base = step * size
            expand_into(
                plan([out_refs[at * sends + base // part]], False, 0),
                act_ref[...],
                wb[at, 0, base : base + size],
                wb[at, 1, base : base + size],
                base % part,
                True,
            )
    for copy in gathered[:per]:
        copy.wait()


def run_turn(far, own, pre, slices, orders, sends, w_in, w_out):
    n_narrow, _, half, hidden = w_in.shape
    flat = [piece for one in slices for chunk in one for piece in chunk]
    cols = own.shape[1]
    chunks = len(orders)
    size = pick(half // max(chunks, sends), 768)
    steps = half // size
    forward = pre is None
    ins = [own] if forward else [own, pre]
    outs = [shape_of((cols, half // sends * 3), BF16)] * ((n_narrow - 1) * sends)
    outs += [shape_of((2 * cols, hidden), BF16), shape_of((n_narrow, chunks, cols, half // chunks * 3), BF16)]
    if forward:
        outs.append(shape_of((2 * cols, hidden), F32))
    got = call(
        functools.partial(turn_kernel, far, n_narrow, orders, sends, forward),
        (1,),
        [HBM] * 2 + [ANY] * (len(ins) + len(flat)),
        [whole(out) for out in outs],
        [pltpu.HBM(out.shape, out.dtype) for out in outs],
        scratch=[pltpu.VMEM(array.shape, F32) for array in ins]
        + [
            pltpu.VMEM((n_narrow - 1, 2, half, hidden), BF16),
            pltpu.VMEM((n_narrow - 1, 2, half, hidden), BF16),
            pltpu.SemaphoreType.DMA((len(ins),)),
            pltpu.SemaphoreType.DMA((n_narrow * moves_of(orders, far),)),
            pltpu.SemaphoreType.DMA((n_narrow - 1, steps)),
            pltpu.SemaphoreType.DMA((n_narrow - 1, steps)),
        ],
        scalars=0,
        flops=16 * cols * half * hidden * (n_narrow - 1),
        nbytes=(n_narrow - 1) * (8 * half * hidden + 12 * cols * half),
    )(keep(w_in), keep(w_out), *ins, *flat)
    count = (n_narrow - 1) * sends
    out = [list(got[at * sends : (at + 1) * sends]) for at in range(n_narrow - 1)]
    return out, got[count], got[count + 1], got[-1] if forward else None


def grad_kernel(idx_ref, act_ref, one_ref, two_ref, packed_ref, out_ref, held):
    rows = act_ref.shape[0] // 2

    @pl.when(pl.program_id(0) == 0)
    def _():
        act = act_ref[...]
        mask = first_half((rows, act.shape[1]))
        low = act[rows:].astype(F32)
        zero = jnp.zeros_like(low)
        for side in range(2):
            held[side, :rows] = act[:rows]
            held[side, rows:] = (jnp.where(mask, low, zero) if side == 0 else jnp.where(mask, zero, low)).astype(BF16)

    packed = packed_ref[0, 0]
    out_ref[0, 0] = dot_tn(jnp.concatenate([one_ref[0, 0], packed], axis=0), held[0]).astype(BF16)
    out_ref[0, 1] = dot_tn(jnp.concatenate([two_ref[0, 0], packed], axis=0), held[1]).astype(BF16)


def weight_grad(act, gathered, like, at, after=()):
    parts_n, _, half, hidden = like
    _, chunks, rows, _ = gathered.shape
    part = half // chunks
    size = pick(part, 768)
    per, steps = part // size, half // size
    out = shape_of(like, BF16)

    def rows_at(place):
        return pl.BlockSpec(
            (1, 1, rows, size),
            lambda i, idx: (i // steps, lax.rem(i, steps) // per, 0, place * per + lax.rem(i, per)),
        )

    return call(
        grad_kernel,
        (parts_n * steps,),
        [whole(act), rows_at(0), rows_at(1), rows_at(2)],
        pl.BlockSpec(
            (1, 2, size, hidden),
            lambda i, idx: (lax.rem(idx[0] + parts_n - i // steps, parts_n), 0, lax.rem(i, steps), 0),
        ),
        out,
        scratch=[pltpu.VMEM((2, 2 * rows, hidden), BF16)],
        flops=8 * rows * half * parts_n * hidden,
        nbytes=parts_n * (4 * half * hidden + 6 * rows * half),
        after=after,
    )(at, act, gathered, gathered, gathered)


def regroup_kernel(count, *refs):
    ins, outs, sems = refs[:count], refs[count:-1], refs[-1]
    copies = start_all(
        [
            pltpu.make_async_copy(
                src.at[SUB * j : SUB * (j + 1)], dst.at[SUB * i : SUB * (i + 1)], sems.at[i * len(outs) + j]
            )
            for i, src in enumerate(ins)
            for j, dst in enumerate(outs)
        ]
    )
    for copy in copies:
        copy.wait()


def regroup(parts):
    many = parts[0].shape[0] // SUB
    out = shape_of((SUB * len(parts), parts[0].shape[1]), BF16)
    return call(
        functools.partial(regroup_kernel, len(parts)),
        (1,),
        [ANY] * len(parts),
        [whole(out)] * many,
        [out] * many,
        scratch=[pltpu.SemaphoreType.DMA((many * len(parts),))],
        scalars=0,
        nbytes=4 * many * out.shape[0] * out.shape[1],
    )(*parts)


def sum_kernel(count, *refs):
    ins, outs, (buf, sems) = refs[:count], refs[count:-2], refs[-2:]
    each = outs[0].shape[0]
    copies = [
        [
            pltpu.make_async_copy(
                src.at[k * each : (k + 1) * each], buf.at[i, k * each : (k + 1) * each], sems.at[k * count + i]
            )
            for i, src in enumerate(ins)
        ]
        for k in range(len(outs))
    ]
    for some in copies:
        start_all(some)
    for k, out_ref in enumerate(outs):
        for copy in copies[k]:
            copy.wait()
        total = buf[0, k * each : (k + 1) * each].astype(F32)
        for i in range(1, count):
            total = total + buf[i, k * each : (k + 1) * each].astype(F32)
        out_ref[...] = total.astype(BF16)


def sum_parts(arrays, pieces):
    rows, width = arrays[0].shape
    out = shape_of((rows // pieces, width), BF16)
    return call(
        functools.partial(sum_kernel, len(arrays)),
        (1,),
        [ANY] * len(arrays),
        [whole(out)] * pieces,
        [out] * pieces,
        scratch=[
            pltpu.VMEM((len(arrays), rows, width), BF16),
            pltpu.SemaphoreType.DMA((len(arrays) * pieces,)),
        ],
        scalars=0,
        nbytes=2 * (len(arrays) + 1) * rows * width,
    )(*arrays)


def mix_kernel(chunks, total, start, sliced, more, last, src_hbm, *refs):
    count = chunks * NEAR
    if last:
        gid_ref, refs = refs[0], refs[1:]
    if more:
        prev_hbm, refs = refs[0], refs[1:]
    parts, (out_ref, acc_ref, src_ref, part_ref, sems, sem_prev, sem_part) = refs[:count], refs[count:]
    part = src_ref.shape[2] // chunks
    half = part * total
    steps = sems.shape[1]
    size = src_ref.shape[2] // steps
    each = parts[0].shape[0]
    small = [
        pltpu.make_async_copy(
            src, part_ref.at[i // NEAR, (i % NEAR) * each : (i % NEAR + 1) * each], sem_part.at[i]
        )
        for i, src in enumerate(parts)
    ]
    if more:
        small.append(pltpu.make_async_copy(prev_hbm, acc_ref, sem_prev.at[0]))
    offset = lax.axis_index("narrow").astype(jnp.int32) * (2 * half) if sliced else 0
    copies = [
        [
            pltpu.make_async_copy(
                src_hbm.at[:, pl.ds(pl.multiple_of(offset + side * half + start * part + step * size, 128), size)],
                src_ref.at[side, :, step * size : (step + 1) * size],
                sems.at[side, step],
            )
            for side in range(2)
        ]
        for step in range(steps)
    ]
    start_all(small)
    for pair in copies:
        start_all(pair)
    for copy in small:
        copy.wait()
    rows = acc_ref.shape[1]
    for step in range(steps):
        copies[step][0].wait()
        copies[step][1].wait()
        chunk, base = step * size // part, step * size % part
        packed = part_ref[chunk, :, 2 * part + base : 2 * part + base + size]
        one = part_ref[chunk, :, base : base + size]
        two = part_ref[chunk, :, part + base : part + base + size]
        span = slice(step * size, (step + 1) * size)
        top = dot_nt(jnp.concatenate([one, packed], axis=0), src_ref[0, :, span])
        low = dot_nt(jnp.concatenate([two, packed], axis=0), src_ref[1, :, span])
        straight = top[:rows] + low[:rows]
        halves = jnp.where(first_half(straight.shape), top[rows:], low[rows:])
        if more or step:
            acc_ref[0] += straight
            acc_ref[1] += halves
        else:
            acc_ref[0] = straight
            acc_ref[1] = halves
    if last:
        in_a, in_b = group_masks(gid_ref[...], rows)
        picked = jnp.where(in_a, acc_ref[0], 0.0) + jnp.where(in_b, acc_ref[1], 0.0)
        out_ref[...] = jnp.sum(picked.reshape(rows // SUB, SUB, -1), axis=1)
    else:
        out_ref[...] = acc_ref[...]


def run_mix(source, slice_width, parts, total, start, sliced, gid=None, prev=None):
    flat = [part for chunk in parts for part in chunk]
    chunks, count = len(parts), source.shape[0]
    cols = sum(part.shape[0] for part in parts[0])
    more, last = prev is not None, gid is not None
    part = slice_width // 2 // total
    size = pick(part, 768)
    out = shape_of((cols // SUB, count) if last else (2, cols, count), F32)
    return call(
        functools.partial(mix_kernel, chunks, total, start, sliced, more, last),
        (1,),
        [HBM] + ([whole(gid)] if last else []) + [ANY] * (more + len(flat)),
        whole(out),
        out,
        scratch=[
            pltpu.VMEM((2, cols, count), F32),
            pltpu.VMEM((2, count, part * chunks), BF16),
            pltpu.VMEM((chunks, cols, flat[0].shape[1]), BF16),
            pltpu.SemaphoreType.DMA((2, part * chunks // size)),
            pltpu.SemaphoreType.DMA((1,)),
            pltpu.SemaphoreType.DMA((len(flat),)),
        ],
        scalars=0,
        flops=8 * cols * count * part * chunks,
        nbytes=4 * count * part * chunks + 6 * cols * part * chunks,
    )(keep(source), *([gid] if last else []), *([prev] if more else []), *flat)


def ctrl_kernel(far, scale, turns, slice_width, tok_hbm, gid_ref, w_ref, *refs):
    mix_refs, (low_ref, keep_ref, send_ref, tok_ref, sems) = refs[:turns], refs[turns:]
    me, member = placed_here()
    experts, count = w_ref.shape
    cols = SUB * experts
    steps = sems.shape[0]
    size = slice_width // steps
    spans = [slice(step * size, (step + 1) * size) for step in range(steps)]
    copies = start_all(
        [
            pltpu.make_async_copy(
                tok_hbm.at[:, pl.ds(pl.multiple_of(member * slice_width + span.start, size), size)],
                tok_ref.at[:, span],
                sems.at[c],
            )
            for c, span in enumerate(spans)
        ]
    )
    mix = mix_refs[0][...]
    for ref in mix_refs[1:]:
        mix = mix + ref[...]
    weights = w_ref[...]
    in_a, in_b = group_masks(gid_ref[...], cols)
    spread = jnp.broadcast_to((weights * mix)[:, None, :], (experts, SUB, count)).reshape(cols, count)
    sum_a = jnp.sum(jnp.where(in_a, spread, 0.0), axis=1, keepdims=True)
    sum_b = jnp.sum(jnp.where(in_b, spread, 0.0), axis=1, keepdims=True)
    in_b = jnp.logical_and(in_b, first_half((cols, count)))
    back = jnp.where(in_a, sum_a, 0.0) + jnp.where(in_b, sum_b, 0.0)
    total = jnp.sum(back.reshape(experts, SUB, count), axis=1)
    low = (weights * (mix - total)).astype(BF16)
    place = rel_of(iota((experts, experts), 1), far) ^ me
    row = iota((experts, experts), 0)
    onehot = jnp.where(row == place, 1.0, 0.0).astype(BF16)
    low_ref[...] = dot_nn(onehot, low).astype(BF16)
    few = experts // 2
    turned = jnp.where(row == (place ^ ((me & 1) * few)), 1.0, 0.0).astype(BF16)
    ordered = dot_nn(turned, low).astype(BF16)
    for step in range(steps):
        copies[step].wait()
        part = scale * dot_nn(ordered, tok_ref[:, spans[step]])
        keep_ref[:, spans[step]] = part[:few].astype(BF16)
        send_ref[:, spans[step]] = part[few:].astype(BF16)


def token_kernel(scale, steps, chunks, idx_ref, left_ref, low_ref, ctrl_ref, *refs):
    in_refs, out_ref = refs[: chunks * NEAR], refs[chunks * NEAR]
    step = pl.program_id(0)
    size = out_ref.shape[1]
    part = in_refs[0].shape[1] // 3
    per = part // size
    side, within = step // steps, lax.rem(step, steps)
    for chunk in range(chunks):

        @pl.when(within // per == chunk)
        def _():
            own = in_refs[chunk * NEAR : (chunk + 1) * NEAR]
            lower = lax.rem(within, per) * size
            base = pl.multiple_of(side * part + lower, 128)
            third = pl.multiple_of(2 * part + lower, 128)
            straight = [ref[:, pl.ds(base, size)] for ref in own]
            packed = [ref[:, pl.ds(third, size)] for ref in own]
            back = dot_tn(left_ref[0], jnp.concatenate(straight + packed, axis=0))
            out_ref[...] = (back + scale * dot_tn(low_ref[...], ctrl_ref[...])).astype(BF16)


def on_device(sizes, tokens, group_slot, controller, expert_in, expert_out, cotangent):
    n_dp, n_narrow = sizes
    count, model_width = tokens.shape
    slice_width = cotangent.shape[1]
    half = slice_width // 2
    experts = controller.shape[1]
    hidden = expert_in.shape[2]
    far = n_dp // NEAR
    splits = 2 if half % 256 == 0 else 1
    cols = SUB * experts
    assert experts == n_dp and count // GSIZE == SUB + HALF and far & (far - 1) == 0
    scale = 1.0 / math.sqrt(model_width)
    me = lax.axis_index("dp").astype(jnp.int32)
    member = lax.axis_index("narrow").astype(jnp.int32)
    at = jnp.stack([member])
    ctrl_t = controller.T
    first = expert_in.reshape(n_narrow, 2, half, hidden)
    second = expert_out.reshape(n_narrow, 2, half, hidden)

    def swap(array, bits):
        return lax.ppermute(array, "dp", [(i, i ^ bits) for i in range(n_dp)]) if bits else array

    def shifted(array, shift):
        return lax.ppermute(array, "narrow", [(i, (i + shift) % n_narrow) for i in range(n_narrow)])

    def near_swap(parts):
        return [swap(part, bits) for bits, part in enumerate(parts)]

    def far_swap(parts):
        return [swap(part, NEAR * bits) for bits, part in enumerate(parts)]

    def spread(parts):
        slices = [parts]
        for shift in range(1, n_narrow):
            moved = []
            for part in parts:
                moved.append(shifted(part, shift))
            slices.append(moved)
        return slices

    def homeward(own, others):
        arrived = [shifted(other, shift) for shift, other in enumerate(others, 1)]
        parts = far_swap(sum_parts([own] + arrived, far))
        return near_swap(regroup(parts))

    def pairwise(values):
        values = [value.astype(F32) for value in values]
        while len(values) > 1:
            values = [values[i] + values[i + 1] for i in range(0, len(values), 2)]
        return values[0]

    near_piece = shape_of((SUB * far, 3 * half // splits), BF16)
    far_piece = shape_of((SUB * NEAR, 3 * half // splits), BF16)
    low_shape, w_shape = shape_of((2, cols, count), BF16), shape_of((experts, count), F32)
    gid_shape = shape_of((1, count), jnp.int32)
    outs = [near_piece] * NEAR + [far_piece] * (far * (splits - 1)) + [gid_shape, low_shape, w_shape]
    loads = 8
    *rows_out, gid, low, weights = call(
        functools.partial(head_kernel, far, scale, slice_width),
        (1,),
        [HBM] * 3,
        [whole(out) for out in outs],
        outs,
        scratch=[
            pltpu.VMEM((count, model_width), BF16),
            pltpu.VMEM((experts, model_width), BF16),
            pltpu.VMEM((1, count), jnp.int32),
            pltpu.VMEM((count, experts), F32),
            pltpu.SemaphoreType.DMA((loads,)),
            pltpu.SemaphoreType.DMA((2,)),
        ],
        scalars=0,
        flops=2 * cols * count * model_width,
        nbytes=2 * count * model_width,
    )(keep(tokens), keep(ctrl_t), keep(group_slot))
    lanes = [spread(far_swap(regroup(near_swap(rows_out[:NEAR]))))]
    if splits > 1:
        lanes.append(spread(near_swap(regroup(far_swap(rows_out[NEAR:])))))
    mixed = [list(pair) for pair in zip(*lanes)]
    size = pick(half, 768)
    packed = shape_of((SUB * far, 3 * half), BF16)
    cot_out = call(
        cot_kernel,
        (1,),
        [HBM, whole(low_shape)],
        [whole(packed)] * NEAR,
        [packed] * NEAR,
        scratch=[pltpu.VMEM((count, slice_width), BF16), pltpu.SemaphoreType.DMA((2 * (half // size),))],
        scalars=0,
        flops=4 * cols * count * slice_width,
        nbytes=2 * count * slice_width,
    )(keep(cotangent), low)
    mixed_cot = [[parts] for parts in spread(far_swap(regroup(near_swap(cot_out))))]

    orders = (True, False)[:splits]
    pre_own = contract_own(far, mixed[0], orders, first)
    sends, hidden_act, mixed_all, pre = run_turn(far, pre_own, None, mixed, orders, splits, first, second)
    result_own = expand_weights(hidden_act, second, at, splits, True)
    result = [homeward(result_own[c], [one[c] for one in sends]) for c in range(splits)]
    slope_own = contract_own(far, mixed_cot[0], (True,), second)
    sends, act_grad, cot_all, _ = run_turn(far, slope_own, pre, mixed_cot, (True,), splits, second, first)
    back_own = expand_weights(act_grad, first, at, splits)
    back = [homeward(back_own[c], [one[c] for one in sends]) for c in range(splits)]
    out_grad = weight_grad(hidden_act, cot_all, second.shape, at)
    in_grad = weight_grad(act_grad, mixed_all, first.shape, at)

    mix_part = run_mix(cotangent, slice_width, result, splits, 0, False)
    for c in range(splits - 1):
        mix_part = run_mix(tokens, slice_width, back[c : c + 1], splits, c, True, None, mix_part)
    out_grad, in_grad = out_grad.reshape(expert_out.shape), in_grad.reshape(expert_in.shape)
    mix = run_mix(tokens, slice_width, back[-1:], splits, splits - 1, True, gid, mix_part)
    mixes = [mix] + [shifted(mix, shift) for shift in range(1, n_narrow)]
    steps = slice_width // pick(slice_width, 1024)
    few = shape_of((experts // 2, slice_width), BF16)
    low_grad, ctrl_keep, ctrl_send = call(
        functools.partial(ctrl_kernel, far, scale, n_narrow, slice_width),
        (1,),
        [HBM, whole(gid), whole(weights)] + [whole(mix)] * n_narrow,
        [whole(shape_of((experts, count), BF16)), whole(few), whole(few)],
        [shape_of((experts, count), BF16), few, few],
        scratch=[pltpu.VMEM((count, slice_width), BF16), pltpu.SemaphoreType.DMA((steps,))],
        scalars=0,
        flops=2 * experts * count * slice_width,
        nbytes=2 * count * slice_width,
    )(keep(tokens), gid, weights, *mixes)
    total = pairwise([ctrl_keep, swap(ctrl_send, 1)]).astype(BF16)
    total = pairwise([total, swap(total, 2)]).astype(BF16)
    total = pairwise(far_swap([total] * far))
    other = swap(total, 1)
    lower = (me & 1) == 0
    total = jnp.concatenate([jnp.where(lower, total, other), jnp.where(lower, other, total)], axis=0)
    ctrl_grad = total.T

    size = pick(half // len(back), 768)
    steps = half // size
    side = jnp.where((jnp.arange(cols) & HALF)[:, None] == 0, low[1], jnp.zeros_like(low[1]))
    sides = jnp.stack([jnp.concatenate([low[0], side]), jnp.concatenate([low[0], low[1] - side])])
    token_grad = call(
        functools.partial(token_kernel, scale, steps, len(back)),
        (2 * steps,),
        [
            pl.BlockSpec((1, 2 * cols, count), lambda i, idx: (i // steps, 0, 0)),
            whole(low_grad),
            pl.BlockSpec((experts, size), lambda i, idx: (0, idx[0] * 2 * steps + i)),
        ]
        + [whole(part) for chunk in back for part in chunk],
        pl.BlockSpec((count, size), lambda i, idx: (0, i)),
        shape_of((count, slice_width), BF16),
        flops=4 * cols * count * slice_width,
        nbytes=2 * count * slice_width,
    )(at, sides, low_grad, ctrl_t, *[part for chunk in back for part in chunk])
    return (token_grad, ctrl_grad, in_grad, out_grad)


def solution(mesh):
    sizes = (mesh.shape["dp"], mesh.shape["narrow"])
    placed = (
        P("dp", None),
        P("dp", None),
        P(),
        P("dp", None, "narrow"),
        P("dp", None, "narrow"),
        P("dp", "narrow"),
    )

    def body(*args):
        return on_device(sizes, *args)

    return jax.shard_map(
        body,
        mesh=mesh,
        in_specs=placed,
        out_specs=(
            P("dp", "narrow"),
            P("narrow", None),
            P("dp", None, "narrow"),
            P("dp", None, "narrow"),
        ),
        check_vma=False,
    )
```

```python
import functools
import math

import jax
import jax.numpy as jnp
from jax import lax
from jax.experimental import pallas as pl
from jax.experimental.pallas import tpu as pltpu
from jax.sharding import PartitionSpec as P


GSIZE = 32
SUB = 8
HALF = 4
NEAR = 4
F32 = jnp.float32
BF16 = jnp.bfloat16
VMEM_LIMIT = 20 * 1024 * 1024


def dot_nn(a, b):
    return lax.dot_general(a, b, (((1,), (0,)), ((), ())), preferred_element_type=F32)


def dot_nt(a, b):
    return lax.dot_general(a, b, (((1,), (1,)), ((), ())), preferred_element_type=F32)


def dot_tn(a, b):
    return lax.dot_general(a, b, (((0,), (0,)), ((), ())), preferred_element_type=F32)


def iota(shape, dim):
    return lax.broadcasted_iota(jnp.int32, shape, dim)


def first_half(shape):
    return (iota(shape, 0) & HALF) == 0


def pick(width, most):
    size = most
    while width % size:
        size //= 2
    return size


ANY = pl.BlockSpec(memory_space=pl.ANY)
HBM = pl.BlockSpec(memory_space=pltpu.HBM)


def call(kernel, grid, in_specs, out_specs, out_shape, scratch=(), scalars=1, flops=0, nbytes=0, after=()):
    skip = len(after)

    def body(*refs):
        kernel(*refs[:scalars], *refs[scalars + skip :])

    run = pl.pallas_call(
        body,
        grid_spec=pltpu.PrefetchScalarGridSpec(
            num_scalar_prefetch=scalars,
            grid=grid,
            in_specs=[ANY] * skip + list(in_specs),
            out_specs=out_specs,
            scratch_shapes=list(scratch),
        ),
        out_shape=out_shape,
        compiler_params=pltpu.CompilerParams(
            dimension_semantics=("arbitrary",) * len(grid),
            vmem_limit_bytes=VMEM_LIMIT,
        ),
        cost_estimate=pl.CostEstimate(flops=int(flops), bytes_accessed=int(nbytes), transcendentals=0),
    )
    return lambda *args: run(*args[:scalars], *after, *args[scalars:])


def placed_here():
    return lax.axis_index("dp").astype(jnp.int32), lax.axis_index("narrow").astype(jnp.int32)


def keep(array):
    return pltpu.with_memory_space_constraint(array, pltpu.HBM)


def start_all(copies):
    for copy in copies:
        copy.start()
    return copies


def whole(array):
    rank = len(array.shape)
    return pl.BlockSpec(array.shape, lambda *_: (0,) * rank)


def shape_of(dims, dtype):
    return jax.ShapeDtypeStruct(dims, dtype)


def rel_of(c8, far):
    return (c8 % far) * NEAR + c8 // far if isinstance(c8, int) else (
        (c8 & (far - 1)) * NEAR + lax.shift_right_logical(c8, far.bit_length() - 1)
    )


def group_masks(gid, cols):
    row = iota((cols, gid.shape[1]), 0)
    in_a = gid == (row & (SUB - 1))
    in_b = gid == (SUB + (row & (HALF - 1)))
    return in_a, in_b


def soften(logits, gid, low_ref, w_ref):
    experts = w_ref.shape[0]
    masks = group_masks(gid, logits.shape[0])
    shared = jnp.zeros_like(logits)
    for part, mask in enumerate(masks):
        top = jnp.max(jnp.where(mask, logits, -jnp.inf), axis=1, keepdims=True)
        raised = jnp.where(mask, jnp.exp(jnp.where(mask, logits - top, 0.0)), 0.0)
        weights = raised / jnp.sum(raised, axis=1, keepdims=True)
        low_ref[part] = weights.astype(BF16)
        if part:
            weights = jnp.where(first_half(weights.shape), weights, 0.0)
        shared += weights
    w_ref[...] = jnp.sum(shared.reshape(experts, SUB, -1), axis=1)


def plan(refs, by_far, far):
    if not by_far:
        each = refs[0].shape[0]
        return [(ref, 0, at * each, each) for at, ref in enumerate(refs)]
    return [(ref, SUB * y, SUB * (y * far + k), SUB) for k, ref in enumerate(refs) for y in range(NEAR)]


def expand_into(targets, left, one, two, base, rhs_t):
    rows = left.shape[0] // 2
    dot = dot_nt if rhs_t else dot_nn
    size = one.shape[0] if rhs_t else one.shape[1]
    top, low = dot(left, one), dot(left, two)
    mixed = jnp.where(first_half((rows, size)), top[rows:], low[rows:])
    for ref, to, at, many in targets:
        wide = ref.shape[1] // 3
        for place, value in enumerate((top, low, mixed)):
            ref[to : to + many, pl.ds(place * wide + base, size)] = value[at : at + many].astype(BF16)


def head_kernel(far, scale, slice_width, tok_hbm, ctrl_hbm, slot_hbm, *refs):
    out_refs, (gid_ref, low_ref, w_ref, tok_ref, ctrl_ref, slot_ref, acc_ref, sems, more) = refs[:-9], refs[-9:]
    targets_of = [plan(out_refs[:NEAR], False, far)]
    if out_refs[NEAR:]:
        targets_of.append(plan(out_refs[NEAR:], True, far))
    _, width = tok_ref.shape
    chunks = sems.shape[0]
    size = width // chunks
    spans = [slice(c * size, (c + 1) * size) for c in range(chunks)]
    extra = start_all(
        [
            pltpu.make_async_copy(ctrl_hbm, ctrl_ref, more.at[0]),
            pltpu.make_async_copy(slot_hbm, slot_ref, more.at[1]),
        ]
    )
    copies = start_all(
        [pltpu.make_async_copy(tok_hbm.at[:, span], tok_ref.at[:, span], sems.at[c]) for c, span in enumerate(spans)]
    )
    me, member = placed_here()
    experts = ctrl_ref.shape[0]
    cols = SUB * experts
    c8 = lax.shift_right_logical(iota((cols, experts), 0), 3)
    onehot = jnp.where(iota((cols, experts), 1) == (rel_of(c8, far) ^ me), 1.0, 0.0)
    for copy in extra:
        copy.wait()
    gid_ref[...] = lax.shift_right_logical(slot_ref[...], GSIZE.bit_length() - 1)
    for c, span in enumerate(spans):
        copies[c].wait()
        part = dot_nt(tok_ref[:, span], ctrl_ref[:, span])
        if c:
            acc_ref[...] += part
        else:
            acc_ref[...] = part
    logits = lax.dot_general(
        onehot,
        acc_ref[...].T * scale,
        (((1,), (0,)), ((), ())),
        precision=lax.Precision.HIGHEST,
        preferred_element_type=F32,
    )
    soften(logits, gid_ref[...], low_ref, w_ref)
    left = jnp.concatenate([low_ref[0], low_ref[1]], axis=0)
    half = slice_width // 2
    part = half // len(targets_of)
    size = pick(part, 768)
    for which, targets in enumerate(targets_of):
        for step in range(part // size):
            start = member * slice_width + which * part + step * size
            one = pl.multiple_of(start, 128)
            two = pl.multiple_of(start + half, 128)
            expand_into(
                targets, left, tok_ref[:, pl.ds(one, size)], tok_ref[:, pl.ds(two, size)], step * size, False
            )


def cot_kernel(src_hbm, low_ref, *refs):
    out_refs, (src_ref, sems) = refs[:NEAR], refs[NEAR:]
    half = src_ref.shape[1] // 2
    steps = sems.shape[0] // 2
    size = half // steps
    spans = [slice(at, at + size) for step in range(steps) for at in (step * size, half + step * size)]
    copies = start_all(
        [pltpu.make_async_copy(src_hbm.at[:, span], src_ref.at[:, span], sems.at[c]) for c, span in enumerate(spans)]
    )
    left = jnp.concatenate([low_ref[0], low_ref[1]], axis=0)
    for step in range(steps):
        copies[2 * step].wait()
        copies[2 * step + 1].wait()
        expand_into(
            plan(out_refs, False, 0),
            left,
            src_ref[:, spans[2 * step]],
            src_ref[:, spans[2 * step + 1]],
            step * size,
            False,
        )


def expand_kernel(per, idx_ref, left_ref, one_ref, two_ref, *out_refs):
    one, two = one_ref[0, 0], two_ref[0, 0]
    size = one.shape[0]
    step = pl.program_id(0)
    for chunk, out_ref in enumerate(out_refs):

        @pl.when(step // per == chunk)
        def _():
            base = pl.multiple_of(lax.rem(step, per) * size, size)
            expand_into(plan([out_ref], False, 0), left_ref[...], one, two, base, True)


def expand_weights(left, weights, at, chunks, stay=False):
    _, _, half, hidden = weights.shape
    part = half // chunks
    size = pick(part, 768)
    rows = left.shape[0] // 2
    outs = [shape_of((rows, part * 3), BF16)] * chunks
    return call(
        functools.partial(expand_kernel, part // size),
        (half // size,),
        [
            whole(left),
            pl.BlockSpec((1, 1, size, hidden), lambda i, idx: (idx[0], 0, i, 0)),
            pl.BlockSpec((1, 1, size, hidden), lambda i, idx: (idx[0], 1, i, 0)),
        ],
        [whole(out) for out in outs],
        outs,
        flops=8 * rows * half * hidden,
        nbytes=4 * half * hidden + 6 * rows * half,
    )(at, keep(left), *[keep(weights) if stay else weights] * 2)


def rows_of(by_far, far, piece):
    if by_far:
        return [(0, SUB * NEAR * piece, SUB * NEAR)]
    return [(SUB * k, SUB * (NEAR * k + piece), SUB) for k in range(far)]


def gather(parts, orders, far, shifts, dst_ref, sems):
    copies, at = [], 0
    for shift in range(shifts):
        for chunk, by_far in enumerate(orders):
            for piece in range(far if by_far else NEAR):
                for src, dst, many in rows_of(by_far, far, piece):
                    copies.append(
                        pltpu.make_async_copy(
                            parts[at].at[src : src + many],
                            dst_ref.at[shift, chunk, dst : dst + many],
                            sems.at[len(copies)],
                        )
                    )
                at += 1
    return copies


def moves_of(orders, far):
    return sum(len(rows_of(by_far, far, piece)) for by_far in orders for piece in range(far if by_far else NEAR))


def load_slice(w_hbm, turn, buf_ref, at, sems, size):
    return [
        pltpu.make_async_copy(
            w_hbm.at[turn, :, step * size : (step + 1) * size],
            buf_ref.at[at, :, step * size : (step + 1) * size],
            sems.at[at, step],
        )
        for step in range(sems.shape[1])
    ]


def contract_slice(rows_ref, shift, w_ref, at, loads, acc, fresh):
    _, chunks, rows, width = rows_ref.shape
    part = width // 3
    size = part * chunks // len(loads)
    for step, load in enumerate(loads):
        load.wait()
        base = step * size
        chunk, within = base // part, base % part
        packed = rows_ref[shift, chunk, :, 2 * part + within : 2 * part + within + size]
        one = rows_ref[shift, chunk, :, within : within + size]
        two = rows_ref[shift, chunk, :, part + within : part + within + size]
        top = dot_nn(jnp.concatenate([one, packed], axis=0), w_ref[at, 0, base : base + size])
        low = dot_nn(jnp.concatenate([two, packed], axis=0), w_ref[at, 1, base : base + size])
        straight = top[:rows] + low[:rows]
        halves = jnp.where(first_half(straight.shape), top[rows:], low[rows:])
        if fresh and not step:
            acc[0] = straight
            acc[1] = halves
        else:
            acc[0] += straight
            acc[1] += halves


def own_kernel(far, orders, w_hbm, *refs):
    parts, (out_ref, rows_ref, w_ref, sem_part, sem_w) = refs[:-5], refs[-5:]
    member = lax.axis_index("narrow").astype(jnp.int32)
    copies = start_all(gather(parts, orders, far, 1, rows_ref, sem_part))
    loads = start_all(load_slice(w_hbm, member, w_ref, 0, sem_w, w_ref.shape[2] // sem_w.shape[1]))
    for copy in copies:
        copy.wait()
    contract_slice(rows_ref, 0, w_ref, 0, loads, out_ref, True)


def contract_own(far, chunks, orders, weights):
    _, _, half, hidden = weights.shape
    flat = [piece for chunk in chunks for piece in chunk]
    cols = sum(piece.shape[0] for piece in chunks[0])
    size = pick(half // len(orders), 768)
    out = shape_of((2, cols, hidden), F32)
    return call(
        functools.partial(own_kernel, far, orders),
        (1,),
        [HBM] + [ANY] * len(flat),
        whole(out),
        out,
        scratch=[
            pltpu.VMEM((1, len(orders), cols, half // len(orders) * 3), BF16),
            pltpu.VMEM((1, 2, half, hidden), BF16),
            pltpu.SemaphoreType.DMA((moves_of(orders, far),)),
            pltpu.SemaphoreType.DMA((1, half // size)),
        ],
        scalars=0,
        flops=8 * cols * half * hidden,
        nbytes=4 * half * hidden + 6 * cols * half,
    )(keep(weights), *flat)


def turn_kernel(far, n_narrow, orders, sends, forward, w_in, w_out, *refs):
    others = n_narrow - 1
    n_in = 1 if forward else 2
    count = n_narrow * sum(far if by_far else NEAR for by_far in orders)
    ins, parts, refs = refs[:n_in], refs[n_in : n_in + count], refs[n_in + count :]
    out_refs, refs = refs[: others * sends], refs[others * sends :]
    act_ref, all_ref, refs = refs[0], refs[1], refs[2:]
    if forward:
        pre_out, refs = refs[0], refs[1:]
    in_bufs, refs = refs[:n_in], refs[n_in:]
    wa, wb, sem_in, sem_part, sem_a, sem_b = refs
    acc = in_bufs[0]
    member = lax.axis_index("narrow").astype(jnp.int32)
    steps = sem_a.shape[1]
    half = wa.shape[2]
    size = half // steps
    small = [pltpu.make_async_copy(src, dst, sem_in.at[i]) for i, (src, dst) in enumerate(zip(ins, in_bufs))]
    gathered = gather(parts, orders, far, n_narrow, all_ref, sem_part)
    per = len(gathered) // n_narrow
    load_a, load_b = [], []
    for at in range(others):
        load_a.append(load_slice(w_in, lax.rem(member + others - at, n_narrow), wa, at, sem_a, size))
        load_b.append(load_slice(w_out, lax.rem(member + at + 1, n_narrow), wb, at, sem_b, size))
    start_all(gathered[per:])
    start_all(small)
    for loads in load_a + load_b:
        start_all(loads)
    start_all(gathered[:per])
    for copy in gathered[per:] + small:
        copy.wait()
    rows = acc.shape[1]
    for at in range(others):
        contract_slice(all_ref, at + 1, wa, at, load_a[at], acc, False)
    halves = acc[1]
    other = jnp.where(
        first_half(halves.shape), pltpu.roll(halves, rows - HALF, 0), pltpu.roll(halves, HALF, 0)
    )
    total = jnp.concatenate([acc[0], halves + other], axis=0)
    if forward:
        pre_out[...] = total
        act_ref[...] = (total * jax.nn.sigmoid(total)).astype(BF16)
    else:
        pre = in_bufs[1][...]
        sig = jax.nn.sigmoid(pre)
        act_ref[...] = (total * (sig * (1.0 + pre * (1.0 - sig)))).astype(BF16)
    part = half // sends
    for at in range(others):
        for step in range(steps):
            load_b[at][step].wait()
            base = step * size
            expand_into(
                plan([out_refs[at * sends + base // part]], False, 0),
                act_ref[...],
                wb[at, 0, base : base + size],
                wb[at, 1, base : base + size],
                base % part,
                True,
            )
    for copy in gathered[:per]:
        copy.wait()


def run_turn(far, own, pre, slices, orders, sends, w_in, w_out):
    n_narrow, _, half, hidden = w_in.shape
    flat = [piece for one in slices for chunk in one for piece in chunk]
    cols = own.shape[1]
    chunks = len(orders)
    size = pick(half // max(chunks, sends), 768)
    steps = half // size
    forward = pre is None
    ins = [own] if forward else [own, pre]
    outs = [shape_of((cols, half // sends * 3), BF16)] * ((n_narrow - 1) * sends)
    outs += [shape_of((2 * cols, hidden), BF16), shape_of((n_narrow, chunks, cols, half // chunks * 3), BF16)]
    if forward:
        outs.append(shape_of((2 * cols, hidden), F32))
    got = call(
        functools.partial(turn_kernel, far, n_narrow, orders, sends, forward),
        (1,),
        [HBM] * 2 + [ANY] * (len(ins) + len(flat)),
        [whole(out) for out in outs],
        [pltpu.HBM(out.shape, out.dtype) for out in outs],
        scratch=[pltpu.VMEM(array.shape, F32) for array in ins]
        + [
            pltpu.VMEM((n_narrow - 1, 2, half, hidden), BF16),
            pltpu.VMEM((n_narrow - 1, 2, half, hidden), BF16),
            pltpu.SemaphoreType.DMA((len(ins),)),
            pltpu.SemaphoreType.DMA((n_narrow * moves_of(orders, far),)),
            pltpu.SemaphoreType.DMA((n_narrow - 1, steps)),
            pltpu.SemaphoreType.DMA((n_narrow - 1, steps)),
        ],
        scalars=0,
        flops=16 * cols * half * hidden * (n_narrow - 1),
        nbytes=(n_narrow - 1) * (8 * half * hidden + 12 * cols * half),
    )(keep(w_in), keep(w_out), *ins, *flat)
    count = (n_narrow - 1) * sends
    out = [list(got[at * sends : (at + 1) * sends]) for at in range(n_narrow - 1)]
    return out, got[count], got[count + 1], got[-1] if forward else None


def grad_kernel(idx_ref, act_ref, one_ref, two_ref, packed_ref, out_ref, held):
    rows = act_ref.shape[0] // 2

    @pl.when(pl.program_id(0) == 0)
    def _():
        act = act_ref[...]
        mask = first_half((rows, act.shape[1]))
        low = act[rows:].astype(F32)
        zero = jnp.zeros_like(low)
        for side in range(2):
            held[side, :rows] = act[:rows]
            held[side, rows:] = (jnp.where(mask, low, zero) if side == 0 else jnp.where(mask, zero, low)).astype(BF16)

    packed = packed_ref[0, 0]
    out_ref[0, 0] = dot_tn(jnp.concatenate([one_ref[0, 0], packed], axis=0), held[0]).astype(BF16)
    out_ref[0, 1] = dot_tn(jnp.concatenate([two_ref[0, 0], packed], axis=0), held[1]).astype(BF16)


def weight_grad(act, gathered, like, at, after=()):
    parts_n, _, half, hidden = like
    _, chunks, rows, _ = gathered.shape
    part = half // chunks
    size = pick(part, 768)
    per, steps = part // size, half // size
    out = shape_of(like, BF16)

    def rows_at(place):
        return pl.BlockSpec(
            (1, 1, rows, size),
            lambda i, idx: (i // steps, lax.rem(i, steps) // per, 0, place * per + lax.rem(i, per)),
        )

    return call(
        grad_kernel,
        (parts_n * steps,),
        [whole(act), rows_at(0), rows_at(1), rows_at(2)],
        pl.BlockSpec(
            (1, 2, size, hidden),
            lambda i, idx: (lax.rem(idx[0] + parts_n - i // steps, parts_n), 0, lax.rem(i, steps), 0),
        ),
        out,
        scratch=[pltpu.VMEM((2, 2 * rows, hidden), BF16)],
        flops=8 * rows * half * parts_n * hidden,
        nbytes=parts_n * (4 * half * hidden + 6 * rows * half),
        after=after,
    )(at, act, gathered, gathered, gathered)


def regroup_kernel(chunks, count, *refs):
    ins, outs, sems = refs[: chunks * count], refs[chunks * count : -1], refs[-1]
    width = ins[0].shape[1]
    copies = []
    for at, src in enumerate(ins):
        chunk, i = at // count, at % count
        for j, dst in enumerate(outs):
            copies.append(
                pltpu.make_async_copy(
                    src.at[SUB * j : SUB * (j + 1)],
                    dst.at[SUB * i : SUB * (i + 1), chunk * width : (chunk + 1) * width],
                    sems.at[len(copies)],
                )
            )
    start_all(copies)
    for copy in copies:
        copy.wait()


def regroup(*chunks):
    flat = [part for parts in chunks for part in parts]
    count, (rows, width) = len(chunks[0]), flat[0].shape
    many = rows // SUB
    out = shape_of((SUB * count, width * len(chunks)), BF16)
    return call(
        functools.partial(regroup_kernel, len(chunks), count),
        (1,),
        [ANY] * len(flat),
        [whole(out)] * many,
        [out] * many,
        scratch=[pltpu.SemaphoreType.DMA((many * len(flat),))],
        scalars=0,
        nbytes=4 * rows * width * len(flat),
    )(*flat)


def sum_kernel(count, *refs):
    ins, outs, (buf, sems) = refs[:count], refs[count:-2], refs[-2:]
    each = outs[0].shape[0]
    copies = [
        [
            pltpu.make_async_copy(
                src.at[k * each : (k + 1) * each], buf.at[i, k * each : (k + 1) * each], sems.at[k * count + i]
            )
            for i, src in enumerate(ins)
        ]
        for k in range(len(outs))
    ]
    for some in copies:
        start_all(some)
    for k, out_ref in enumerate(outs):
        for copy in copies[k]:
            copy.wait()
        total = buf[0, k * each : (k + 1) * each].astype(F32)
        for i in range(1, count):
            total = total + buf[i, k * each : (k + 1) * each].astype(F32)
        out_ref[...] = total.astype(BF16)


def sum_parts(arrays, pieces):
    rows, width = arrays[0].shape
    out = shape_of((rows // pieces, width), BF16)
    return call(
        functools.partial(sum_kernel, len(arrays)),
        (1,),
        [ANY] * len(arrays),
        [whole(out)] * pieces,
        [out] * pieces,
        scratch=[
            pltpu.VMEM((len(arrays), rows, width), BF16),
            pltpu.SemaphoreType.DMA((len(arrays) * pieces,)),
        ],
        scalars=0,
        nbytes=2 * (len(arrays) + 1) * rows * width,
    )(*arrays)


def mix_kernel(chunks, total, start, sliced, more, last, src_hbm, *refs):
    count = NEAR
    if last:
        gid_ref, refs = refs[0], refs[1:]
    if more:
        prev_hbm, refs = refs[0], refs[1:]
    parts, (out_ref, acc_ref, src_ref, part_ref, sems, sem_prev, sem_part) = refs[:count], refs[count:]
    part = src_ref.shape[2] // chunks
    half = part * total
    steps = sems.shape[1]
    size = src_ref.shape[2] // steps
    each = parts[0].shape[0]
    small = [
        pltpu.make_async_copy(
            src.at[:, 3 * part * chunk : 3 * part * (chunk + 1)],
            part_ref.at[chunk, i * each : (i + 1) * each],
            sem_part.at[chunk * NEAR + i],
        )
        for chunk in range(chunks)
        for i, src in enumerate(parts)
    ]
    if more:
        small.append(pltpu.make_async_copy(prev_hbm, acc_ref, sem_prev.at[0]))
    offset = lax.axis_index("narrow").astype(jnp.int32) * (2 * half) if sliced else 0
    copies = [
        [
            pltpu.make_async_copy(
                src_hbm.at[:, pl.ds(pl.multiple_of(offset + side * half + start * part + step * size, 128), size)],
                src_ref.at[side, :, step * size : (step + 1) * size],
                sems.at[side, step],
            )
            for side in range(2)
        ]
        for step in range(steps)
    ]
    start_all(small)
    for pair in copies:
        start_all(pair)
    for copy in small:
        copy.wait()
    rows = acc_ref.shape[1]
    for step in range(steps):
        copies[step][0].wait()
        copies[step][1].wait()
        chunk, base = step * size // part, step * size % part
        packed = part_ref[chunk, :, 2 * part + base : 2 * part + base + size]
        one = part_ref[chunk, :, base : base + size]
        two = part_ref[chunk, :, part + base : part + base + size]
        span = slice(step * size, (step + 1) * size)
        top = dot_nt(jnp.concatenate([one, packed], axis=0), src_ref[0, :, span])
        low = dot_nt(jnp.concatenate([two, packed], axis=0), src_ref[1, :, span])
        straight = top[:rows] + low[:rows]
        halves = jnp.where(first_half(straight.shape), top[rows:], low[rows:])
        if more or step:
            acc_ref[0] += straight
            acc_ref[1] += halves
        else:
            acc_ref[0] = straight
            acc_ref[1] = halves
    if last:
        in_a, in_b = group_masks(gid_ref[...], rows)
        picked = jnp.where(in_a, acc_ref[0], 0.0) + jnp.where(in_b, acc_ref[1], 0.0)
        out_ref[...] = jnp.sum(picked.reshape(rows // SUB, SUB, -1), axis=1)
    else:
        out_ref[...] = acc_ref[...]


def run_mix(source, slice_width, flat, chunks, total, start, sliced, gid=None, prev=None):
    count = source.shape[0]
    cols = sum(part.shape[0] for part in flat)
    more, last = prev is not None, gid is not None
    part = slice_width // 2 // total
    size = pick(part, 768)
    out = shape_of((cols // SUB, count) if last else (2, cols, count), F32)
    return call(
        functools.partial(mix_kernel, chunks, total, start, sliced, more, last),
        (1,),
        [HBM] + ([whole(gid)] if last else []) + [ANY] * (more + len(flat)),
        whole(out),
        out,
        scratch=[
            pltpu.VMEM((2, cols, count), F32),
            pltpu.VMEM((2, count, part * chunks), BF16),
            pltpu.VMEM((chunks, cols, 3 * part), BF16),
            pltpu.SemaphoreType.DMA((2, part * chunks // size)),
            pltpu.SemaphoreType.DMA((1,)),
            pltpu.SemaphoreType.DMA((chunks * len(flat),)),
        ],
        scalars=0,
        flops=8 * cols * count * part * chunks,
        nbytes=4 * count * part * chunks + 6 * cols * part * chunks,
    )(keep(source), *([gid] if last else []), *([prev] if more else []), *flat)


def ctrl_kernel(far, scale, turns, slice_width, tok_hbm, gid_ref, w_ref, *refs):
    mix_refs, (low_ref, keep_ref, send_ref, tok_ref, sems) = refs[:turns], refs[turns:]
    me, member = placed_here()
    experts, count = w_ref.shape
    cols = SUB * experts
    steps = sems.shape[0]
    size = slice_width // steps
    spans = [slice(step * size, (step + 1) * size) for step in range(steps)]
    copies = start_all(
        [
            pltpu.make_async_copy(
                tok_hbm.at[:, pl.ds(pl.multiple_of(member * slice_width + span.start, size), size)],
                tok_ref.at[:, span],
                sems.at[c],
            )
            for c, span in enumerate(spans)
        ]
    )
    mix = mix_refs[0][...]
    for ref in mix_refs[1:]:
        mix = mix + ref[...]
    weights = w_ref[...]
    in_a, in_b = group_masks(gid_ref[...], cols)
    spread = jnp.broadcast_to((weights * mix)[:, None, :], (experts, SUB, count)).reshape(cols, count)
    sum_a = jnp.sum(jnp.where(in_a, spread, 0.0), axis=1, keepdims=True)
    sum_b = jnp.sum(jnp.where(in_b, spread, 0.0), axis=1, keepdims=True)
    in_b = jnp.logical_and(in_b, first_half((cols, count)))
    back = jnp.where(in_a, sum_a, 0.0) + jnp.where(in_b, sum_b, 0.0)
    total = jnp.sum(back.reshape(experts, SUB, count), axis=1)
    low = (weights * (mix - total)).astype(BF16)
    place = rel_of(iota((experts, experts), 1), far) ^ me
    row = iota((experts, experts), 0)
    onehot = jnp.where(row == place, 1.0, 0.0).astype(BF16)
    low_ref[...] = dot_nn(onehot, low).astype(BF16)
    few = experts // 2
    turned = jnp.where(row == (place ^ ((me & 1) * few)), 1.0, 0.0).astype(BF16)
    ordered = dot_nn(turned, low).astype(BF16)
    for step in range(steps):
        copies[step].wait()
        part = scale * dot_nn(ordered, tok_ref[:, spans[step]])
        keep_ref[:, spans[step]] = part[:few].astype(BF16)
        send_ref[:, spans[step]] = part[few:].astype(BF16)


def token_kernel(scale, steps, chunks, idx_ref, left_ref, low_ref, ctrl_ref, *refs):
    in_refs, out_ref = refs[: chunks * NEAR], refs[chunks * NEAR]
    step = pl.program_id(0)
    size = out_ref.shape[1]
    part = in_refs[0].shape[1] // 3
    per = part // size
    side, within = step // steps, lax.rem(step, steps)
    for chunk in range(chunks):

        @pl.when(within // per == chunk)
        def _():
            own = in_refs[chunk * NEAR : (chunk + 1) * NEAR]
            lower = lax.rem(within, per) * size
            base = pl.multiple_of(side * part + lower, 128)
            third = pl.multiple_of(2 * part + lower, 128)
            straight = [ref[:, pl.ds(base, size)] for ref in own]
            packed = [ref[:, pl.ds(third, size)] for ref in own]
            back = dot_tn(left_ref[0], jnp.concatenate(straight + packed, axis=0))
            out_ref[...] = (back + scale * dot_tn(low_ref[...], ctrl_ref[...])).astype(BF16)


def on_device(sizes, tokens, group_slot, controller, expert_in, expert_out, cotangent):
    n_dp, n_narrow = sizes
    count, model_width = tokens.shape
    slice_width = cotangent.shape[1]
    half = slice_width // 2
    experts = controller.shape[1]
    hidden = expert_in.shape[2]
    far = n_dp // NEAR
    splits = 2 if half % 256 == 0 else 1
    cols = SUB * experts
    assert experts == n_dp and count // GSIZE == SUB + HALF and far & (far - 1) == 0
    scale = 1.0 / math.sqrt(model_width)
    me = lax.axis_index("dp").astype(jnp.int32)
    member = lax.axis_index("narrow").astype(jnp.int32)
    at = jnp.stack([member])
    ctrl_t = controller.T
    first = expert_in.reshape(n_narrow, 2, half, hidden)
    second = expert_out.reshape(n_narrow, 2, half, hidden)

    def swap(array, bits):
        return lax.ppermute(array, "dp", [(i, i ^ bits) for i in range(n_dp)]) if bits else array

    def shifted(array, shift):
        return lax.ppermute(array, "narrow", [(i, (i + shift) % n_narrow) for i in range(n_narrow)])

    def near_swap(parts):
        return [swap(part, bits) for bits, part in enumerate(parts)]

    def far_swap(parts):
        return [swap(part, NEAR * bits) for bits, part in enumerate(parts)]

    def spread(parts):
        slices = [parts]
        for shift in range(1, n_narrow):
            moved = []
            for part in parts:
                moved.append(shifted(part, shift))
            slices.append(moved)
        return slices

    def summed(own, others):
        arrived = [shifted(other, shift) for shift, other in enumerate(others, 1)]
        return far_swap(sum_parts([own] + arrived, far))

    def pairwise(values):
        values = [value.astype(F32) for value in values]
        while len(values) > 1:
            values = [values[i] + values[i + 1] for i in range(0, len(values), 2)]
        return values[0]

    near_piece = shape_of((SUB * far, 3 * half // splits), BF16)
    far_piece = shape_of((SUB * NEAR, 3 * half // splits), BF16)
    low_shape, w_shape = shape_of((2, cols, count), BF16), shape_of((experts, count), F32)
    gid_shape = shape_of((1, count), jnp.int32)
    outs = [near_piece] * NEAR + [far_piece] * (far * (splits - 1)) + [gid_shape, low_shape, w_shape]
    loads = 8
    *rows_out, gid, low, weights = call(
        functools.partial(head_kernel, far, scale, slice_width),
        (1,),
        [HBM] * 3,
        [whole(out) for out in outs],
        outs,
        scratch=[
            pltpu.VMEM((count, model_width), BF16),
            pltpu.VMEM((experts, model_width), BF16),
            pltpu.VMEM((1, count), jnp.int32),
            pltpu.VMEM((count, experts), F32),
            pltpu.SemaphoreType.DMA((loads,)),
            pltpu.SemaphoreType.DMA((2,)),
        ],
        scalars=0,
        flops=2 * cols * count * model_width,
        nbytes=2 * count * model_width,
    )(keep(tokens), keep(ctrl_t), keep(group_slot))
    lanes = [spread(far_swap(regroup(near_swap(rows_out[:NEAR]))))]
    if splits > 1:
        lanes.append(spread(near_swap(regroup(far_swap(rows_out[NEAR:])))))
    mixed = [list(pair) for pair in zip(*lanes)]
    size = pick(half, 768)
    packed = shape_of((SUB * far, 3 * half), BF16)
    cot_out = call(
        cot_kernel,
        (1,),
        [HBM, whole(low_shape)],
        [whole(packed)] * NEAR,
        [packed] * NEAR,
        scratch=[pltpu.VMEM((count, slice_width), BF16), pltpu.SemaphoreType.DMA((2 * (half // size),))],
        scalars=0,
        flops=4 * cols * count * slice_width,
        nbytes=2 * count * slice_width,
    )(keep(cotangent), low)
    mixed_cot = [[parts] for parts in spread(far_swap(regroup(near_swap(cot_out))))]

    orders = (True, False)[:splits]
    pre_own = contract_own(far, mixed[0], orders, first)
    sends, hidden_act, mixed_all, pre = run_turn(far, pre_own, None, mixed, orders, splits, first, second)
    result_own = expand_weights(hidden_act, second, at, splits, True)
    result = [summed(result_own[c], [one[c] for one in sends]) for c in range(splits)]
    result = near_swap(regroup(*result))
    slope_own = contract_own(far, mixed_cot[0], (True,), second)
    sends, act_grad, cot_all, _ = run_turn(far, slope_own, pre, mixed_cot, (True,), splits, second, first)
    back_own = expand_weights(act_grad, first, at, splits)
    back = []
    for c in range(splits):
        parts = summed(back_own[c], [one[c] for one in sends])
        back.append(near_swap(regroup(parts)))
    out_grad = weight_grad(hidden_act, cot_all, second.shape, at)
    in_grad = weight_grad(act_grad, mixed_all, first.shape, at)

    mix_part = run_mix(cotangent, slice_width, result, splits, splits, 0, False)
    for c in range(splits - 1):
        mix_part = run_mix(tokens, slice_width, back[c], 1, splits, c, True, None, mix_part)
    out_grad, in_grad = out_grad.reshape(expert_out.shape), in_grad.reshape(expert_in.shape)
    mix = run_mix(tokens, slice_width, back[-1], 1, splits, splits - 1, True, gid, mix_part)
    mixes = [mix] + [shifted(mix, shift) for shift in range(1, n_narrow)]
    steps = slice_width // pick(slice_width, 1024)
    few = shape_of((experts // 2, slice_width), BF16)
    low_grad, ctrl_keep, ctrl_send = call(
        functools.partial(ctrl_kernel, far, scale, n_narrow, slice_width),
        (1,),
        [HBM, whole(gid), whole(weights)] + [whole(mix)] * n_narrow,
        [whole(shape_of((experts, count), BF16)), whole(few), whole(few)],
        [shape_of((experts, count), BF16), few, few],
        scratch=[pltpu.VMEM((count, slice_width), BF16), pltpu.SemaphoreType.DMA((steps,))],
        scalars=0,
        flops=2 * experts * count * slice_width,
        nbytes=2 * count * slice_width,
    )(keep(tokens), gid, weights, *mixes)
    total = pairwise([ctrl_keep, swap(ctrl_send, 1)]).astype(BF16)
    total = pairwise([total, swap(total, 2)]).astype(BF16)
    total = pairwise(far_swap([total] * far))
    other = swap(total, 1)
    lower = (me & 1) == 0
    total = jnp.concatenate([jnp.where(lower, total, other), jnp.where(lower, other, total)], axis=0)
    ctrl_grad = total.T

    size = pick(half // len(back), 768)
    steps = half // size
    side = jnp.where((jnp.arange(cols) & HALF)[:, None] == 0, low[1], jnp.zeros_like(low[1]))
    sides = jnp.stack([jnp.concatenate([low[0], side]), jnp.concatenate([low[0], low[1] - side])])
    token_grad = call(
        functools.partial(token_kernel, scale, steps, len(back)),
        (2 * steps,),
        [
            pl.BlockSpec((1, 2 * cols, count), lambda i, idx: (i // steps, 0, 0)),
            whole(low_grad),
            pl.BlockSpec((experts, size), lambda i, idx: (0, idx[0] * 2 * steps + i)),
        ]
        + [whole(part) for chunk in back for part in chunk],
        pl.BlockSpec((count, size), lambda i, idx: (0, i)),
        shape_of((count, slice_width), BF16),
        flops=4 * cols * count * slice_width,
        nbytes=2 * count * slice_width,
    )(at, sides, low_grad, ctrl_t, *[part for chunk in back for part in chunk])
    return (token_grad, ctrl_grad, in_grad, out_grad)


def solution(mesh):
    sizes = (mesh.shape["dp"], mesh.shape["narrow"])
    placed = (
        P("dp", None),
        P("dp", None),
        P(),
        P("dp", None, "narrow"),
        P("dp", None, "narrow"),
        P("dp", "narrow"),
    )

    def body(*args):
        return on_device(sizes, *args)

    return jax.shard_map(
        body,
        mesh=mesh,
        in_specs=placed,
        out_specs=(
            P("dp", "narrow"),
            P("narrow", None),
            P("dp", None, "narrow"),
            P("dp", None, "narrow"),
        ),
        check_vma=False,
    )
```

```python
import functools
import math

import jax
import jax.numpy as jnp
from jax import lax
from jax.experimental import pallas as pl
from jax.experimental.pallas import tpu as pltpu
from jax.sharding import PartitionSpec as P


GSIZE = 32
SUB = 8
HALF = 4
NEAR = 4
F32 = jnp.float32
BF16 = jnp.bfloat16
VMEM_LIMIT = 20 * 1024 * 1024


def dot_nn(a, b):
    return lax.dot_general(a, b, (((1,), (0,)), ((), ())), preferred_element_type=F32)


def dot_nt(a, b):
    return lax.dot_general(a, b, (((1,), (1,)), ((), ())), preferred_element_type=F32)


def dot_tn(a, b):
    return lax.dot_general(a, b, (((0,), (0,)), ((), ())), preferred_element_type=F32)


def iota(shape, dim):
    return lax.broadcasted_iota(jnp.int32, shape, dim)


def first_half(shape):
    return (iota(shape, 0) & HALF) == 0


def pick(width, most):
    size = most
    while width % size:
        size //= 2
    return size


ANY = pl.BlockSpec(memory_space=pl.ANY)
HBM = pl.BlockSpec(memory_space=pltpu.HBM)


def call(kernel, grid, in_specs, out_specs, out_shape, scratch=(), scalars=1, flops=0, nbytes=0, after=()):
    skip = len(after)

    def body(*refs):
        kernel(*refs[:scalars], *refs[scalars + skip :])

    run = pl.pallas_call(
        body,
        grid_spec=pltpu.PrefetchScalarGridSpec(
            num_scalar_prefetch=scalars,
            grid=grid,
            in_specs=[ANY] * skip + list(in_specs),
            out_specs=out_specs,
            scratch_shapes=list(scratch),
        ),
        out_shape=out_shape,
        compiler_params=pltpu.CompilerParams(
            dimension_semantics=("arbitrary",) * len(grid),
            vmem_limit_bytes=VMEM_LIMIT,
        ),
        cost_estimate=pl.CostEstimate(flops=int(flops), bytes_accessed=int(nbytes), transcendentals=0),
    )
    return lambda *args: run(*args[:scalars], *after, *args[scalars:])


def placed_here():
    return lax.axis_index("dp").astype(jnp.int32), lax.axis_index("narrow").astype(jnp.int32)


def keep(array):
    return pltpu.with_memory_space_constraint(array, pltpu.HBM)


def start_all(copies):
    for copy in copies:
        copy.start()
    return copies


def whole(array):
    rank = len(array.shape)
    return pl.BlockSpec(array.shape, lambda *_: (0,) * rank)


def shape_of(dims, dtype):
    return jax.ShapeDtypeStruct(dims, dtype)


def rel_of(c8, far):
    return (c8 % far) * NEAR + c8 // far if isinstance(c8, int) else (
        (c8 & (far - 1)) * NEAR + lax.shift_right_logical(c8, far.bit_length() - 1)
    )


def group_masks(gid, cols):
    row = iota((cols, gid.shape[1]), 0)
    in_a = gid == (row & (SUB - 1))
    in_b = gid == (SUB + (row & (HALF - 1)))
    return in_a, in_b


def soften(logits, gid, low_ref, w_ref):
    experts = w_ref.shape[0]
    masks = group_masks(gid, logits.shape[0])
    shared = jnp.zeros_like(logits)
    for part, mask in enumerate(masks):
        top = jnp.max(jnp.where(mask, logits, -jnp.inf), axis=1, keepdims=True)
        raised = jnp.where(mask, jnp.exp(jnp.where(mask, logits - top, 0.0)), 0.0)
        weights = raised / jnp.sum(raised, axis=1, keepdims=True)
        low_ref[part] = weights.astype(BF16)
        if part:
            weights = jnp.where(first_half(weights.shape), weights, 0.0)
        shared += weights
    w_ref[...] = jnp.sum(shared.reshape(experts, SUB, -1), axis=1)


def plan(refs, by_far, far):
    if not by_far:
        each = refs[0].shape[0]
        return [(ref, 0, at * each, each) for at, ref in enumerate(refs)]
    return [(ref, SUB * y, SUB * (y * far + k), SUB) for k, ref in enumerate(refs) for y in range(NEAR)]


def expand_into(targets, left, one, two, base, rhs_t):
    rows = left.shape[0] // 2
    dot = dot_nt if rhs_t else dot_nn
    size = one.shape[0] if rhs_t else one.shape[1]
    top, low = dot(left, one), dot(left, two)
    mixed = jnp.where(first_half((rows, size)), top[rows:], low[rows:])
    for ref, to, at, many in targets:
        wide = ref.shape[1] // 3
        for place, value in enumerate((top, low, mixed)):
            ref[to : to + many, pl.ds(place * wide + base, size)] = value[at : at + many].astype(BF16)


def head_kernel(far, scale, slice_width, tok_hbm, ctrl_hbm, slot_hbm, *refs):
    out_refs, (gid_ref, low_ref, w_ref, tok_ref, ctrl_ref, slot_ref, acc_ref, sems, more) = refs[:-9], refs[-9:]
    targets_of = [plan(out_refs[:NEAR], False, far)]
    if out_refs[NEAR:]:
        targets_of.append(plan(out_refs[NEAR:], True, far))
    _, width = tok_ref.shape
    chunks = sems.shape[0]
    size = width // chunks
    spans = [slice(c * size, (c + 1) * size) for c in range(chunks)]
    extra = start_all(
        [
            pltpu.make_async_copy(ctrl_hbm, ctrl_ref, more.at[0]),
            pltpu.make_async_copy(slot_hbm, slot_ref, more.at[1]),
        ]
    )
    copies = start_all(
        [pltpu.make_async_copy(tok_hbm.at[:, span], tok_ref.at[:, span], sems.at[c]) for c, span in enumerate(spans)]
    )
    me, member = placed_here()
    experts = ctrl_ref.shape[0]
    cols = SUB * experts
    c8 = lax.shift_right_logical(iota((cols, experts), 0), 3)
    onehot = jnp.where(iota((cols, experts), 1) == (rel_of(c8, far) ^ me), 1.0, 0.0)
    for copy in extra:
        copy.wait()
    gid_ref[...] = lax.shift_right_logical(slot_ref[...], GSIZE.bit_length() - 1)
    for c, span in enumerate(spans):
        copies[c].wait()
        part = dot_nt(tok_ref[:, span], ctrl_ref[:, span])
        if c:
            acc_ref[...] += part
        else:
            acc_ref[...] = part
    logits = lax.dot_general(
        onehot,
        acc_ref[...].T * scale,
        (((1,), (0,)), ((), ())),
        precision=lax.Precision.HIGHEST,
        preferred_element_type=F32,
    )
    soften(logits, gid_ref[...], low_ref, w_ref)
    left = jnp.concatenate([low_ref[0], low_ref[1]], axis=0)
    half = slice_width // 2
    part = half // len(targets_of)
    size = pick(part, 768)
    for which, targets in enumerate(targets_of):
        for step in range(part // size):
            start = member * slice_width + which * part + step * size
            one = pl.multiple_of(start, 128)
            two = pl.multiple_of(start + half, 128)
            expand_into(
                targets, left, tok_ref[:, pl.ds(one, size)], tok_ref[:, pl.ds(two, size)], step * size, False
            )


def cot_kernel(src_hbm, low_ref, *refs):
    out_refs, (src_ref, sems) = refs[:NEAR], refs[NEAR:]
    half = src_ref.shape[1] // 2
    steps = sems.shape[0] // 2
    size = half // steps
    spans = [slice(at, at + size) for step in range(steps) for at in (step * size, half + step * size)]
    copies = start_all(
        [pltpu.make_async_copy(src_hbm.at[:, span], src_ref.at[:, span], sems.at[c]) for c, span in enumerate(spans)]
    )
    left = jnp.concatenate([low_ref[0], low_ref[1]], axis=0)
    for step in range(steps):
        copies[2 * step].wait()
        copies[2 * step + 1].wait()
        expand_into(
            plan(out_refs, False, 0),
            left,
            src_ref[:, spans[2 * step]],
            src_ref[:, spans[2 * step + 1]],
            step * size,
            False,
        )


def expand_kernel(per, idx_ref, left_ref, one_ref, two_ref, *out_refs):
    one, two = one_ref[0, 0], two_ref[0, 0]
    size = one.shape[0]
    step = pl.program_id(0)
    for chunk, out_ref in enumerate(out_refs):

        @pl.when(step // per == chunk)
        def _():
            base = pl.multiple_of(lax.rem(step, per) * size, size)
            expand_into(plan([out_ref], False, 0), left_ref[...], one, two, base, True)


def expand_weights(left, weights, at, chunks, stay=False):
    _, _, half, hidden = weights.shape
    part = half // chunks
    size = pick(part, 768)
    rows = left.shape[0] // 2
    outs = [shape_of((rows, part * 3), BF16)] * chunks
    return call(
        functools.partial(expand_kernel, part // size),
        (half // size,),
        [
            whole(left),
            pl.BlockSpec((1, 1, size, hidden), lambda i, idx: (idx[0], 0, i, 0)),
            pl.BlockSpec((1, 1, size, hidden), lambda i, idx: (idx[0], 1, i, 0)),
        ],
        [whole(out) for out in outs],
        outs,
        flops=8 * rows * half * hidden,
        nbytes=4 * half * hidden + 6 * rows * half,
    )(at, keep(left), *[keep(weights) if stay else weights] * 2)


def rows_of(by_far, far, piece):
    if by_far:
        return [(0, SUB * NEAR * piece, SUB * NEAR)]
    return [(SUB * k, SUB * (NEAR * k + piece), SUB) for k in range(far)]


def gather(parts, orders, far, shifts, dst_ref, sems):
    copies, at = [], 0
    for shift in range(shifts):
        for chunk, by_far in enumerate(orders):
            for piece in range(far if by_far else NEAR):
                for src, dst, many in rows_of(by_far, far, piece):
                    copies.append(
                        pltpu.make_async_copy(
                            parts[at].at[src : src + many],
                            dst_ref.at[shift, chunk, dst : dst + many],
                            sems.at[len(copies)],
                        )
                    )
                at += 1
    return copies


def moves_of(orders, far):
    return sum(len(rows_of(by_far, far, piece)) for by_far in orders for piece in range(far if by_far else NEAR))


def load_slice(w_hbm, turn, buf_ref, at, sems, size):
    return [
        pltpu.make_async_copy(
            w_hbm.at[turn, :, step * size : (step + 1) * size],
            buf_ref.at[at, :, step * size : (step + 1) * size],
            sems.at[at, step],
        )
        for step in range(sems.shape[1])
    ]


def contract_slice(rows_ref, shift, w_ref, at, loads, acc, fresh):
    _, chunks, rows, width = rows_ref.shape
    part = width // 3
    size = part * chunks // len(loads)
    for step, load in enumerate(loads):
        load.wait()
        base = step * size
        chunk, within = base // part, base % part
        packed = rows_ref[shift, chunk, :, 2 * part + within : 2 * part + within + size]
        one = rows_ref[shift, chunk, :, within : within + size]
        two = rows_ref[shift, chunk, :, part + within : part + within + size]
        top = dot_nn(jnp.concatenate([one, packed], axis=0), w_ref[at, 0, base : base + size])
        low = dot_nn(jnp.concatenate([two, packed], axis=0), w_ref[at, 1, base : base + size])
        straight = top[:rows] + low[:rows]
        halves = jnp.where(first_half(straight.shape), top[rows:], low[rows:])
        if fresh and not step:
            acc[0] = straight
            acc[1] = halves
        else:
            acc[0] += straight
            acc[1] += halves


def own_kernel(far, orders, w_hbm, *refs):
    parts, (out_ref, rows_ref, w_ref, sem_part, sem_w) = refs[:-5], refs[-5:]
    member = lax.axis_index("narrow").astype(jnp.int32)
    copies = start_all(gather(parts, orders, far, 1, rows_ref, sem_part))
    loads = start_all(load_slice(w_hbm, member, w_ref, 0, sem_w, w_ref.shape[2] // sem_w.shape[1]))
    for copy in copies:
        copy.wait()
    contract_slice(rows_ref, 0, w_ref, 0, loads, out_ref, True)


def contract_own(far, chunks, orders, weights):
    _, _, half, hidden = weights.shape
    flat = [piece for chunk in chunks for piece in chunk]
    cols = sum(piece.shape[0] for piece in chunks[0])
    size = pick(half // len(orders), 768)
    out = shape_of((2, cols, hidden), F32)
    return call(
        functools.partial(own_kernel, far, orders),
        (1,),
        [HBM] + [ANY] * len(flat),
        whole(out),
        out,
        scratch=[
            pltpu.VMEM((1, len(orders), cols, half // len(orders) * 3), BF16),
            pltpu.VMEM((1, 2, half, hidden), BF16),
            pltpu.SemaphoreType.DMA((moves_of(orders, far),)),
            pltpu.SemaphoreType.DMA((1, half // size)),
        ],
        scalars=0,
        flops=8 * cols * half * hidden,
        nbytes=4 * half * hidden + 6 * cols * half,
    )(keep(weights), *flat)


def turn_kernel(far, n_narrow, orders, sends, forward, w_in, w_out, *refs):
    others = n_narrow - 1
    n_in = 1 if forward else 2
    count = n_narrow * sum(far if by_far else NEAR for by_far in orders)
    ins, parts, refs = refs[:n_in], refs[n_in : n_in + count], refs[n_in + count :]
    out_refs, refs = refs[: others * sends], refs[others * sends :]
    act_ref, all_ref, refs = refs[0], refs[1], refs[2:]
    if forward:
        pre_out, refs = refs[0], refs[1:]
    in_bufs, refs = refs[:n_in], refs[n_in:]
    wa, wb, sem_in, sem_part, sem_a, sem_b = refs
    acc = in_bufs[0]
    member = lax.axis_index("narrow").astype(jnp.int32)
    steps = sem_a.shape[1]
    half = wa.shape[2]
    size = half // steps
    small = [pltpu.make_async_copy(src, dst, sem_in.at[i]) for i, (src, dst) in enumerate(zip(ins, in_bufs))]
    gathered = gather(parts, orders, far, n_narrow, all_ref, sem_part)
    per = len(gathered) // n_narrow
    load_a, load_b = [], []
    for at in range(others):
        load_a.append(load_slice(w_in, lax.rem(member + others - at, n_narrow), wa, at, sem_a, size))
        load_b.append(load_slice(w_out, lax.rem(member + at + 1, n_narrow), wb, at, sem_b, size))
    start_all(gathered[per:])
    start_all(small)
    for loads in load_a + load_b:
        start_all(loads)
    start_all(gathered[:per])
    for copy in gathered[per:] + small:
        copy.wait()
    rows = acc.shape[1]
    for at in range(others):
        contract_slice(all_ref, at + 1, wa, at, load_a[at], acc, False)
    halves = acc[1]
    other = jnp.where(
        first_half(halves.shape), pltpu.roll(halves, rows - HALF, 0), pltpu.roll(halves, HALF, 0)
    )
    total = jnp.concatenate([acc[0], halves + other], axis=0)
    if forward:
        pre_out[...] = total
        act_ref[...] = (total * jax.nn.sigmoid(total)).astype(BF16)
    else:
        pre = in_bufs[1][...]
        sig = jax.nn.sigmoid(pre)
        act_ref[...] = (total * (sig * (1.0 + pre * (1.0 - sig)))).astype(BF16)
    part = half // sends
    for at in range(others):
        for step in range(steps):
            load_b[at][step].wait()
            base = step * size
            expand_into(
                plan([out_refs[at * sends + base // part]], False, 0),
                act_ref[...],
                wb[at, 0, base : base + size],
                wb[at, 1, base : base + size],
                base % part,
                True,
            )
    for copy in gathered[:per]:
        copy.wait()


def run_turn(far, own, pre, slices, orders, sends, w_in, w_out):
    n_narrow, _, half, hidden = w_in.shape
    flat = [piece for one in slices for chunk in one for piece in chunk]
    cols = own.shape[1]
    chunks = len(orders)
    size = pick(half // max(chunks, sends), 768)
    steps = half // size
    forward = pre is None
    ins = [own] if forward else [own, pre]
    outs = [shape_of((cols, half // sends * 3), BF16)] * ((n_narrow - 1) * sends)
    outs += [shape_of((2 * cols, hidden), BF16), shape_of((n_narrow, chunks, cols, half // chunks * 3), BF16)]
    if forward:
        outs.append(shape_of((2 * cols, hidden), F32))
    got = call(
        functools.partial(turn_kernel, far, n_narrow, orders, sends, forward),
        (1,),
        [HBM] * 2 + [ANY] * (len(ins) + len(flat)),
        [whole(out) for out in outs],
        [pltpu.HBM(out.shape, out.dtype) for out in outs],
        scratch=[pltpu.VMEM(array.shape, F32) for array in ins]
        + [
            pltpu.VMEM((n_narrow - 1, 2, half, hidden), BF16),
            pltpu.VMEM((n_narrow - 1, 2, half, hidden), BF16),
            pltpu.SemaphoreType.DMA((len(ins),)),
            pltpu.SemaphoreType.DMA((n_narrow * moves_of(orders, far),)),
            pltpu.SemaphoreType.DMA((n_narrow - 1, steps)),
            pltpu.SemaphoreType.DMA((n_narrow - 1, steps)),
        ],
        scalars=0,
        flops=16 * cols * half * hidden * (n_narrow - 1),
        nbytes=(n_narrow - 1) * (8 * half * hidden + 12 * cols * half),
    )(keep(w_in), keep(w_out), *ins, *flat)
    count = (n_narrow - 1) * sends
    out = [list(got[at * sends : (at + 1) * sends]) for at in range(n_narrow - 1)]
    return out, got[count], got[count + 1], got[-1] if forward else None


def grad_kernel(idx_ref, act_ref, one_ref, two_ref, packed_ref, out_ref, held):
    rows = act_ref.shape[0] // 2

    @pl.when(pl.program_id(0) == 0)
    def _():
        act = act_ref[...]
        mask = first_half((rows, act.shape[1]))
        low = act[rows:].astype(F32)
        zero = jnp.zeros_like(low)
        for side in range(2):
            held[side, :rows] = act[:rows]
            held[side, rows:] = (jnp.where(mask, low, zero) if side == 0 else jnp.where(mask, zero, low)).astype(BF16)

    packed = packed_ref[0, 0]
    out_ref[0, 0] = dot_tn(jnp.concatenate([one_ref[0, 0], packed], axis=0), held[0]).astype(BF16)
    out_ref[0, 1] = dot_tn(jnp.concatenate([two_ref[0, 0], packed], axis=0), held[1]).astype(BF16)


def weight_grad(act, gathered, like, at, after=()):
    parts_n, _, half, hidden = like
    _, chunks, rows, _ = gathered.shape
    part = half // chunks
    size = pick(part, 768)
    per, steps = part // size, half // size
    out = shape_of(like, BF16)

    def rows_at(place):
        return pl.BlockSpec(
            (1, 1, rows, size),
            lambda i, idx: (i // steps, lax.rem(i, steps) // per, 0, place * per + lax.rem(i, per)),
        )

    return call(
        grad_kernel,
        (parts_n * steps,),
        [whole(act), rows_at(0), rows_at(1), rows_at(2)],
        pl.BlockSpec(
            (1, 2, size, hidden),
            lambda i, idx: (lax.rem(idx[0] + parts_n - i // steps, parts_n), 0, lax.rem(i, steps), 0),
        ),
        out,
        scratch=[pltpu.VMEM((2, 2 * rows, hidden), BF16)],
        flops=8 * rows * half * parts_n * hidden,
        nbytes=parts_n * (4 * half * hidden + 6 * rows * half),
        after=after,
    )(at, act, gathered, gathered, gathered)


def regroup_kernel(chunks, count, *refs):
    ins, outs, sems = refs[: chunks * count], refs[chunks * count : -1], refs[-1]
    width = ins[0].shape[1]
    copies = []
    for at, src in enumerate(ins):
        chunk, i = at // count, at % count
        for j, dst in enumerate(outs):
            copies.append(
                pltpu.make_async_copy(
                    src.at[SUB * j : SUB * (j + 1)],
                    dst.at[SUB * i : SUB * (i + 1), chunk * width : (chunk + 1) * width],
                    sems.at[len(copies)],
                )
            )
    start_all(copies)
    for copy in copies:
        copy.wait()


def regroup(*chunks):
    flat = [part for parts in chunks for part in parts]
    count, (rows, width) = len(chunks[0]), flat[0].shape
    many = rows // SUB
    out = shape_of((SUB * count, width * len(chunks)), BF16)
    return call(
        functools.partial(regroup_kernel, len(chunks), count),
        (1,),
        [ANY] * len(flat),
        [whole(out)] * many,
        [out] * many,
        scratch=[pltpu.SemaphoreType.DMA((many * len(flat),))],
        scalars=0,
        nbytes=4 * rows * width * len(flat),
    )(*flat)


def sum_kernel(count, *refs):
    ins, outs, (buf, sems) = refs[:count], refs[count:-2], refs[-2:]
    each = outs[0].shape[0]
    copies = [
        [
            pltpu.make_async_copy(
                src.at[k * each : (k + 1) * each], buf.at[i, k * each : (k + 1) * each], sems.at[k * count + i]
            )
            for i, src in enumerate(ins)
        ]
        for k in range(len(outs))
    ]
    for some in copies:
        start_all(some)
    for k, out_ref in enumerate(outs):
        for copy in copies[k]:
            copy.wait()
        total = buf[0, k * each : (k + 1) * each].astype(F32)
        for i in range(1, count):
            total = total + buf[i, k * each : (k + 1) * each].astype(F32)
        out_ref[...] = total.astype(BF16)


def sum_parts(arrays, pieces):
    rows, width = arrays[0].shape
    out = shape_of((rows // pieces, width), BF16)
    return call(
        functools.partial(sum_kernel, len(arrays)),
        (1,),
        [ANY] * len(arrays),
        [whole(out)] * pieces,
        [out] * pieces,
        scratch=[
            pltpu.VMEM((len(arrays), rows, width), BF16),
            pltpu.SemaphoreType.DMA((len(arrays) * pieces,)),
        ],
        scalars=0,
        nbytes=2 * (len(arrays) + 1) * rows * width,
    )(*arrays)


def mix_kernel(chunks, total, start, sliced, more, last, src_hbm, *refs):
    count = NEAR
    if last:
        gid_ref, refs = refs[0], refs[1:]
    if more:
        prev_hbm, refs = refs[0], refs[1:]
    parts, (out_ref, acc_ref, src_ref, part_ref, sems, sem_prev, sem_part) = refs[:count], refs[count:]
    part = src_ref.shape[2] // chunks
    half = part * total
    steps = sems.shape[1]
    size = src_ref.shape[2] // steps
    each = parts[0].shape[0]
    small = [
        pltpu.make_async_copy(
            src.at[:, 3 * part * chunk : 3 * part * (chunk + 1)],
            part_ref.at[chunk, i * each : (i + 1) * each],
            sem_part.at[chunk * NEAR + i],
        )
        for chunk in range(chunks)
        for i, src in enumerate(parts)
    ]
    if more:
        small.append(pltpu.make_async_copy(prev_hbm, acc_ref, sem_prev.at[0]))
    offset = lax.axis_index("narrow").astype(jnp.int32) * (2 * half) if sliced else 0
    copies = [
        [
            pltpu.make_async_copy(
                src_hbm.at[:, pl.ds(pl.multiple_of(offset + side * half + start * part + step * size, 128), size)],
                src_ref.at[side, :, step * size : (step + 1) * size],
                sems.at[side, step],
            )
            for side in range(2)
        ]
        for step in range(steps)
    ]
    start_all(small)
    for pair in copies:
        start_all(pair)
    for copy in small:
        copy.wait()
    rows = acc_ref.shape[1]
    for step in range(steps):
        copies[step][0].wait()
        copies[step][1].wait()
        chunk, base = step * size // part, step * size % part
        packed = part_ref[chunk, :, 2 * part + base : 2 * part + base + size]
        one = part_ref[chunk, :, base : base + size]
        two = part_ref[chunk, :, part + base : part + base + size]
        span = slice(step * size, (step + 1) * size)
        top = dot_nt(jnp.concatenate([one, packed], axis=0), src_ref[0, :, span])
        low = dot_nt(jnp.concatenate([two, packed], axis=0), src_ref[1, :, span])
        straight = top[:rows] + low[:rows]
        halves = jnp.where(first_half(straight.shape), top[rows:], low[rows:])
        if more or step:
            acc_ref[0] += straight
            acc_ref[1] += halves
        else:
            acc_ref[0] = straight
            acc_ref[1] = halves
    if last:
        in_a, in_b = group_masks(gid_ref[...], rows)
        picked = jnp.where(in_a, acc_ref[0], 0.0) + jnp.where(in_b, acc_ref[1], 0.0)
        out_ref[...] = jnp.sum(picked.reshape(rows // SUB, SUB, -1), axis=1)
    else:
        out_ref[...] = acc_ref[...]


def run_mix(source, slice_width, flat, chunks, total, start, sliced, gid=None, prev=None):
    count = source.shape[0]
    cols = sum(part.shape[0] for part in flat)
    more, last = prev is not None, gid is not None
    part = slice_width // 2 // total
    size = pick(part, 768)
    out = shape_of((cols // SUB, count) if last else (2, cols, count), F32)
    return call(
        functools.partial(mix_kernel, chunks, total, start, sliced, more, last),
        (1,),
        [HBM] + ([whole(gid)] if last else []) + [ANY] * (more + len(flat)),
        whole(out),
        out,
        scratch=[
            pltpu.VMEM((2, cols, count), F32),
            pltpu.VMEM((2, count, part * chunks), BF16),
            pltpu.VMEM((chunks, cols, 3 * part), BF16),
            pltpu.SemaphoreType.DMA((2, part * chunks // size)),
            pltpu.SemaphoreType.DMA((1,)),
            pltpu.SemaphoreType.DMA((chunks * len(flat),)),
        ],
        scalars=0,
        flops=8 * cols * count * part * chunks,
        nbytes=4 * count * part * chunks + 6 * cols * part * chunks,
    )(keep(source), *([gid] if last else []), *([prev] if more else []), *flat)


def ctrl_kernel(far, scale, turns, slice_width, tok_hbm, gid_ref, w_ref, *refs):
    mix_refs, (low_ref, keep_ref, send_ref, tok_ref, sems) = refs[:turns], refs[turns:]
    me, member = placed_here()
    experts, count = w_ref.shape
    cols = SUB * experts
    steps = sems.shape[0]
    size = slice_width // steps
    spans = [slice(step * size, (step + 1) * size) for step in range(steps)]
    copies = start_all(
        [
            pltpu.make_async_copy(
                tok_hbm.at[:, pl.ds(pl.multiple_of(member * slice_width + span.start, size), size)],
                tok_ref.at[:, span],
                sems.at[c],
            )
            for c, span in enumerate(spans)
        ]
    )
    mix = mix_refs[0][...]
    for ref in mix_refs[1:]:
        mix = mix + ref[...]
    weights = w_ref[...]
    in_a, in_b = group_masks(gid_ref[...], cols)
    spread = jnp.broadcast_to((weights * mix)[:, None, :], (experts, SUB, count)).reshape(cols, count)
    sum_a = jnp.sum(jnp.where(in_a, spread, 0.0), axis=1, keepdims=True)
    sum_b = jnp.sum(jnp.where(in_b, spread, 0.0), axis=1, keepdims=True)
    in_b = jnp.logical_and(in_b, first_half((cols, count)))
    back = jnp.where(in_a, sum_a, 0.0) + jnp.where(in_b, sum_b, 0.0)
    total = jnp.sum(back.reshape(experts, SUB, count), axis=1)
    low = (weights * (mix - total)).astype(BF16)
    place = rel_of(iota((experts, experts), 1), far) ^ me
    row = iota((experts, experts), 0)
    onehot = jnp.where(row == place, 1.0, 0.0).astype(BF16)
    low_ref[...] = dot_nn(onehot, low).astype(BF16)
    few = experts // 2
    turned = jnp.where(row == (place ^ ((me & 1) * few)), 1.0, 0.0).astype(BF16)
    ordered = dot_nn(turned, low).astype(BF16)
    for step in range(steps):
        copies[step].wait()
        part = scale * dot_nn(ordered, tok_ref[:, spans[step]])
        keep_ref[:, spans[step]] = part[:few].astype(BF16)
        send_ref[:, spans[step]] = part[few:].astype(BF16)


def token_kernel(scale, steps, chunks, idx_ref, left_ref, low_ref, ctrl_ref, *refs):
    in_refs, out_ref = refs[: chunks * NEAR], refs[chunks * NEAR]
    step = pl.program_id(0)
    size = out_ref.shape[1]
    part = in_refs[0].shape[1] // 3
    per = part // size
    side, within = step // steps, lax.rem(step, steps)
    for chunk in range(chunks):

        @pl.when(within // per == chunk)
        def _():
            own = in_refs[chunk * NEAR : (chunk + 1) * NEAR]
            lower = lax.rem(within, per) * size
            base = pl.multiple_of(side * part + lower, 128)
            third = pl.multiple_of(2 * part + lower, 128)
            straight = [ref[:, pl.ds(base, size)] for ref in own]
            packed = [ref[:, pl.ds(third, size)] for ref in own]
            back = dot_tn(left_ref[0], jnp.concatenate(straight + packed, axis=0))
            out_ref[...] = (back + scale * dot_tn(low_ref[...], ctrl_ref[...])).astype(BF16)


def on_device(sizes, tokens, group_slot, controller, expert_in, expert_out, cotangent):
    n_dp, n_narrow = sizes
    count, model_width = tokens.shape
    slice_width = cotangent.shape[1]
    half = slice_width // 2
    experts = controller.shape[1]
    hidden = expert_in.shape[2]
    far = n_dp // NEAR
    splits = 2 if half % 256 == 0 else 1
    cols = SUB * experts
    assert experts == n_dp and count // GSIZE == SUB + HALF and far & (far - 1) == 0
    scale = 1.0 / math.sqrt(model_width)
    me = lax.axis_index("dp").astype(jnp.int32)
    member = lax.axis_index("narrow").astype(jnp.int32)
    at = jnp.stack([member])
    ctrl_t = controller.T
    first = expert_in.reshape(n_narrow, 2, half, hidden)
    second = expert_out.reshape(n_narrow, 2, half, hidden)

    def swap(array, bits):
        return lax.ppermute(array, "dp", [(i, i ^ bits) for i in range(n_dp)]) if bits else array

    def shifted(array, shift):
        return lax.ppermute(array, "narrow", [(i, (i + shift) % n_narrow) for i in range(n_narrow)])

    def swapped(parts, unit):
        moved = []
        for bits, part in enumerate(parts):
            moved.append(swap(part, unit * bits))
        return moved

    def near_swap(parts):
        return swapped(parts, 1)

    def far_swap(parts):
        return swapped(parts, NEAR)

    def spread(parts):
        slices = [parts]
        for shift in range(1, n_narrow):
            moved = []
            for part in parts:
                moved.append(shifted(part, shift))
            slices.append(moved)
        return slices

    def summed(own, others):
        arrived = [shifted(other, shift) for shift, other in enumerate(others, 1)]
        return far_swap(sum_parts([own] + arrived, far))

    def pairwise(values):
        values = [value.astype(F32) for value in values]
        while len(values) > 1:
            values = [values[i] + values[i + 1] for i in range(0, len(values), 2)]
        return values[0]

    near_piece = shape_of((SUB * far, 3 * half // splits), BF16)
    far_piece = shape_of((SUB * NEAR, 3 * half // splits), BF16)
    low_shape, w_shape = shape_of((2, cols, count), BF16), shape_of((experts, count), F32)
    gid_shape = shape_of((1, count), jnp.int32)
    outs = [near_piece] * NEAR + [far_piece] * (far * (splits - 1)) + [gid_shape, low_shape, w_shape]
    loads = 8
    *rows_out, gid, low, weights = call(
        functools.partial(head_kernel, far, scale, slice_width),
        (1,),
        [HBM] * 3,
        [whole(out) for out in outs],
        outs,
        scratch=[
            pltpu.VMEM((count, model_width), BF16),
            pltpu.VMEM((experts, model_width), BF16),
            pltpu.VMEM((1, count), jnp.int32),
            pltpu.VMEM((count, experts), F32),
            pltpu.SemaphoreType.DMA((loads,)),
            pltpu.SemaphoreType.DMA((2,)),
        ],
        scalars=0,
        flops=2 * cols * count * model_width,
        nbytes=2 * count * model_width,
    )(keep(tokens), keep(ctrl_t), keep(group_slot))
    lanes = [spread(far_swap(regroup(near_swap(rows_out[:NEAR]))))]
    if splits > 1:
        lanes.append(spread(near_swap(regroup(far_swap(rows_out[NEAR:])))))
    mixed = [list(pair) for pair in zip(*lanes)]
    size = pick(half, 768)
    packed = shape_of((SUB * far, 3 * half), BF16)
    cot_out = call(
        cot_kernel,
        (1,),
        [HBM, whole(low_shape)],
        [whole(packed)] * NEAR,
        [packed] * NEAR,
        scratch=[pltpu.VMEM((count, slice_width), BF16), pltpu.SemaphoreType.DMA((2 * (half // size),))],
        scalars=0,
        flops=4 * cols * count * slice_width,
        nbytes=2 * count * slice_width,
    )(keep(cotangent), low)
    mixed_cot = [[parts] for parts in spread(far_swap(regroup(near_swap(cot_out))))]

    orders = (True, False)[:splits]
    pre_own = contract_own(far, mixed[0], orders, first)
    sends, hidden_act, mixed_all, pre = run_turn(far, pre_own, None, mixed, orders, splits, first, second)
    result_own = expand_weights(hidden_act, second, at, splits, True)
    result = [summed(result_own[c], [one[c] for one in sends]) for c in range(splits)]
    result = near_swap(regroup(*result))
    slope_own = contract_own(far, mixed_cot[0], (True,), second)
    sends, act_grad, cot_all, _ = run_turn(far, slope_own, pre, mixed_cot, (True,), splits, second, first)
    back_own = expand_weights(act_grad, first, at, splits)
    back = []
    for c in range(splits):
        parts = summed(back_own[c], [one[c] for one in sends])
        back.append(near_swap(regroup(parts)))
    out_grad = weight_grad(hidden_act, cot_all, second.shape, at)
    in_grad = weight_grad(act_grad, mixed_all, first.shape, at)

    mix_part = run_mix(cotangent, slice_width, result, splits, splits, 0, False)
    for c in range(splits - 1):
        mix_part = run_mix(tokens, slice_width, back[c], 1, splits, c, True, None, mix_part)
    out_grad, in_grad = out_grad.reshape(expert_out.shape), in_grad.reshape(expert_in.shape)
    mix = run_mix(tokens, slice_width, back[-1], 1, splits, splits - 1, True, gid, mix_part)
    mixes = [mix] + [shifted(mix, shift) for shift in range(1, n_narrow)]
    steps = slice_width // pick(slice_width, 1024)
    few = shape_of((experts // 2, slice_width), BF16)
    low_grad, ctrl_keep, ctrl_send = call(
        functools.partial(ctrl_kernel, far, scale, n_narrow, slice_width),
        (1,),
        [HBM, whole(gid), whole(weights)] + [whole(mix)] * n_narrow,
        [whole(shape_of((experts, count), BF16)), whole(few), whole(few)],
        [shape_of((experts, count), BF16), few, few],
        scratch=[pltpu.VMEM((count, slice_width), BF16), pltpu.SemaphoreType.DMA((steps,))],
        scalars=0,
        flops=2 * experts * count * slice_width,
        nbytes=2 * count * slice_width,
    )(keep(tokens), gid, weights, *mixes)
    total = pairwise([ctrl_keep, swap(ctrl_send, 1)]).astype(BF16)
    total = pairwise([total, swap(total, 2)]).astype(BF16)
    total = pairwise([swap(total, NEAR * bits) for bits in range(far)])
    other = swap(total, 1)
    lower = (me & 1) == 0
    total = jnp.concatenate([jnp.where(lower, total, other), jnp.where(lower, other, total)], axis=0)
    ctrl_grad = total.T

    size = pick(half // len(back), 768)
    steps = half // size
    side = jnp.where((jnp.arange(cols) & HALF)[:, None] == 0, low[1], jnp.zeros_like(low[1]))
    sides = jnp.stack([jnp.concatenate([low[0], side]), jnp.concatenate([low[0], low[1] - side])])
    token_grad = call(
        functools.partial(token_kernel, scale, steps, len(back)),
        (2 * steps,),
        [
            pl.BlockSpec((1, 2 * cols, count), lambda i, idx: (i // steps, 0, 0)),
            whole(low_grad),
            pl.BlockSpec((experts, size), lambda i, idx: (0, idx[0] * 2 * steps + i)),
        ]
        + [whole(part) for chunk in back for part in chunk],
        pl.BlockSpec((count, size), lambda i, idx: (0, i)),
        shape_of((count, slice_width), BF16),
        flops=4 * cols * count * slice_width,
        nbytes=2 * count * slice_width,
    )(at, sides, low_grad, ctrl_t, *[part for chunk in back for part in chunk])
    return (token_grad, ctrl_grad, in_grad, out_grad)


def solution(mesh):
    sizes = (mesh.shape["dp"], mesh.shape["narrow"])
    placed = (
        P("dp", None),
        P("dp", None),
        P(),
        P("dp", None, "narrow"),
        P("dp", None, "narrow"),
        P("dp", "narrow"),
    )

    def body(*args):
        return on_device(sizes, *args)

    return jax.shard_map(
        body,
        mesh=mesh,
        in_specs=placed,
        out_specs=(
            P("dp", "narrow"),
            P("narrow", None),
            P("dp", None, "narrow"),
            P("dp", None, "narrow"),
        ),
        check_vma=False,
    )
```
